32 devices in a mesh: segment: 2 (over x), slab: 16 (over z, y, core).
Axes of the slice: x: 2, y: 2, z: 4, core: 2. Of those that a mesh axis runs over, the one named last changes fastest.
Arguments:
- activations: bfloat16 [2, 2, 64, 8, 8, 128], P('segment', None, 'slab'), may hold values from -6 to 6
- weights: bfloat16 [2, 3456, 128], P('segment'), may hold values from -0.109375 to 0.109375
- out_grad: bfloat16 [2, 64, 8, 8, 128], P(None, 'slab'), may hold values from -6 to 6
Outputs:
- update: float32 [2, 3456, 128], P('segment')
- input_grads: bfloat16 [2, 2, 64, 8, 8, 128], P('segment', None, 'slab')
The draws below stay inside these ranges and needn't reach their ends.
All inputs are finite; a program needn't handle non-finite values.
Results may differ from the reference program's by a relative error of at most 0.017.
Values may be sent and summed in bfloat16 or wider, within the bound.
No kernel may reach another device: no remote copies, remote signals or barrier semaphores. Data moves between devices by JAX's collectives and lax.ppermute only.
A program may use at most 64 MiB of HBM per device.

```python
import jax
import jax.numpy as jnp
from jax import lax

C = 128
X = 8
Y = 8
M = 2
LAYERS = 2
NZ = 64
N_SEGMENT = 2


def shard_levels(stream_key, dims, shards, smallest, top_value):
    def one(dim, parts):
        steps = jax.random.uniform(jax.random.fold_in(jax.random.fold_in(stream_key, 6), dim), (parts,), jnp.float32, smallest / len(shards), top_value / len(shards))
        return jnp.repeat(jnp.exp(steps), dims[dim] // parts).reshape((-1,) + (1,) * (len(dims) - dim - 1))

    factor_of = one(*shards[0])
    for cut in shards[1:]:
        factor_of = factor_of * one(*cut)
    return factor_of


def noise(stream_key, dims, width, most, cuts=(), dtype=jnp.bfloat16):
    values = width * jax.random.normal(stream_key, dims, jnp.float32)
    if cuts:
        values = values * shard_levels(stream_key, dims, cuts, -0.22, 0.18)
    return jnp.clip(values, -most, most).astype(dtype)


def setup_inputs(seed: int = 0) -> dict:
    keys = jax.random.split(jax.random.key(seed), 4)
    activations = noise(keys[0], (LAYERS, M, NZ, X, Y, C), 1.0, 6.0, ((0, 2), (2, 16)))
    weights = noise(keys[1], (LAYERS, 27 * C, C), (27 * C) ** -0.5, 0.109375, ((0, 2),))
    out_grad = noise(keys[2], (M, NZ, X, Y, C), 1.0, 6.0, ((1, 16),))
    return {"activations": activations, "weights": weights, "out_grad": out_grad}


def shifted(volume, offset):
    depth_off = offset // 9
    width_off = offset // 3 % 3
    height_off = offset % 3
    padded = jnp.pad(volume, ((1, 1), (1, 1), (1, 1), (0, 0)))
    return padded[depth_off:depth_off + NZ, width_off:width_off + X, height_off:height_off + Y]

def reference(activations, weights, out_grad):
    cell_count = NZ * X * Y
    incoming = out_grad
    grads_all = []
    raw_all = []
    for segment_num in reversed(range(N_SEGMENT)):
        kernel = weights[segment_num].astype(jnp.float32).reshape(27, C, C)
        raw = jnp.zeros((27, C, C), jnp.float32)
        segment_grads = []
        for micro_num in range(M):
            inputs = activations[segment_num, micro_num].astype(jnp.float32)
            upstream = incoming[micro_num].astype(jnp.float32).reshape(cell_count, C)
            preact = jnp.zeros((cell_count, C), jnp.float32)
            for offset in range(27):
                preact = preact + jnp.dot(shifted(inputs, offset).reshape(cell_count, C), kernel[offset], precision=lax.Precision.HIGHEST, preferred_element_type=jnp.float32)
            sigval = jax.nn.sigmoid(preact)
            deltas = (upstream * sigval * (1.0 + preact * (1.0 - sigval))).astype(jnp.bfloat16)
            delta_vol = deltas.astype(jnp.float32).reshape(NZ, X, Y, C)
            backward = jnp.zeros((cell_count, C), jnp.float32)
            terms = []
            for offset in range(27):
                moved = shifted(inputs, offset).reshape(cell_count, C)
                terms.append(jnp.dot(moved.T, delta_vol.reshape(cell_count, C), precision=lax.Precision.HIGHEST, preferred_element_type=jnp.float32))
                backward = backward + jnp.dot(shifted(delta_vol, 26 - offset).reshape(cell_count, C), kernel[offset].T, precision=lax.Precision.HIGHEST, preferred_element_type=jnp.float32)
            raw = raw + jnp.stack(terms)
            segment_grads.append((upstream + backward).astype(jnp.bfloat16).reshape(NZ, X, Y, C))
        incoming = jnp.stack(segment_grads)
        grads_all.insert(0, incoming)
        raw_all.insert(0, raw.reshape(27 * C, C))
    raw_stack = jnp.stack(raw_all)
    norm_value = jnp.sqrt(jnp.sum(raw_stack * raw_stack))
    bound_value = jnp.sqrt(jnp.float32(27 * C * C * N_SEGMENT))
    factor = jnp.minimum(jnp.float32(1.0), bound_value / (norm_value + 1e-06))
    return (raw_stack * factor, jnp.stack(grads_all))
```

```python
import math

import jax
import jax.numpy as jnp
from jax import lax
from jax.sharding import PartitionSpec as P

BF16 = jnp.bfloat16
F32 = jnp.float32


def pair_routes(count):
    near = [(i, i ^ 1) for i in range(count)]
    far = [(i, ((i + 1) ^ 1) - 1) for i in range(1, count - 1)]
    return near, far


def rims(low_planes, high_planes):
    near, far = pair_routes(lax.axis_size("slab"))
    even = lax.axis_index("slab") % 2 == 0
    got_near = lax.ppermute(jnp.where(even, high_planes, low_planes), "slab", near)
    got_far = lax.ppermute(jnp.where(even, low_planes, high_planes), "slab", far)
    return jnp.where(even, got_far, got_near), jnp.where(even, got_near, got_far)


def patches_of(rimmed, order):
    micro, depth, width, height, channels = rimmed.shape
    depth -= 2
    padded = jnp.pad(rimmed, ((0, 0), (0, 0), (1, 1), (1, 1), (0, 0)))
    pieces = []
    for offset in order:
        dz, dx, dy = offset // 9, offset // 3 % 3, offset % 3
        pieces.append(padded[:, dz : dz + depth, dx : dx + width, dy : dy + height])
    joined = jnp.concatenate(pieces, axis=-1)
    return joined.reshape(micro * depth * width * height, 27 * channels)


FORWARD = tuple(range(27))
BACKWARD = tuple(reversed(range(27)))


def exchange(value, bit):
    count = lax.axis_size("slab")
    return lax.ppermute(value, "slab", [(i, i ^ bit) for i in range(count)])


def shards(activations, weights, out_grad):
    acts = activations[0]
    weight = weights[0]
    channels = weight.shape[1]
    micro, depth, width, height = acts.shape[:4]
    cells = micro * depth * width * height
    segments = lax.axis_size("segment")
    count = lax.axis_size("slab")
    sindex = lax.axis_index("segment")
    index = lax.axis_index("slab")
    last = sindex == segments - 1

    low = jnp.concatenate([acts[:, :2], out_grad[:, :1]], axis=1)
    high = jnp.concatenate([acts[:, -2:], out_grad[:, -1:]], axis=1)
    below, above = rims(low, high)
    wide = jnp.concatenate([below[:, :2], acts, above[:, :2]], axis=1)
    wide_up = jnp.concatenate([below[:, 2:], out_grad, above[:, 2:]], axis=1)

    patches = patches_of(wide, FORWARD)
    preact = jnp.dot(patches, weight, preferred_element_type=F32)
    sig = jax.nn.sigmoid(preact)
    slope = (sig * (1.0 + preact * (1.0 - sig))).reshape(micro, depth + 2, width, height, channels)
    inner_patches = patches.reshape(micro, depth + 2, width * height, 27 * channels)[:, 1:-1]
    inner_patches = inner_patches.reshape(cells, 27 * channels)
    inner_slope = slope[:, 1:-1]

    kernel = weight.reshape(27, channels, channels)

    def conv_back(delta_rim):
        moved = patches_of(delta_rim, BACKWARD).reshape(cells, 27, channels)
        out = lax.dot_general(
            moved, kernel, (((1, 2), (0, 2)), ((), ())), preferred_element_type=F32
        )
        return out.reshape(micro, depth, width, height, channels)

    back = [(i, (i - 1) % segments) for i in range(segments)]
    delta_rim = (wide_up.astype(F32) * slope).astype(BF16)
    result = (out_grad.astype(F32) + conv_back(delta_rim)).astype(BF16)
    upstream = out_grad
    deltas = delta_rim[:, 1:-1]
    for step in range(1, segments):
        incoming = lax.ppermute(result, "segment", back)
        upstream = jnp.where(last, out_grad, incoming)
        deltas = (upstream.astype(F32) * inner_slope).astype(BF16)
        if step < segments - 1:
            below, above = rims(deltas[:, :1], deltas[:, -1:])
            around = jnp.concatenate([below, deltas, above], axis=1)
            result = (upstream.astype(F32) + conv_back(around)).astype(BF16)

    partial = lax.dot_general(
        inner_patches,
        deltas.reshape(cells, channels),
        (((0,), (0,)), ((), ())),
        preferred_element_type=F32,
    )
    below, above = rims(deltas[:, :1], deltas[:, -1:])
    around = jnp.concatenate([below, deltas, above], axis=1)
    gradients = (upstream.astype(F32) + conv_back(around)).astype(BF16)

    bits = []
    while 1 << len(bits) < count:
        bits.append(1 << len(bits))
    for bit in bits:
        half = partial.shape[0] // 2
        mine = jnp.where(index & bit, half, 0)
        keep = lax.dynamic_slice_in_dim(partial, mine, half, 0)
        send = lax.dynamic_slice_in_dim(partial, half - mine, half, 0).astype(BF16)
        partial = keep + exchange(send, bit).astype(F32)

    squares = jnp.broadcast_to(jnp.sum(partial * partial), (8, 128))
    total = squares
    turn = squares
    for _ in range(segments - 1):
        turn = lax.ppermute(turn, "segment", back)
        total = total + turn
    for bit in reversed(bits):
        total = total + exchange(total, bit)
    bound = math.sqrt(27.0 * channels * channels * segments)
    factor = jnp.minimum(1.0, bound / (jnp.sqrt(total[0, 0]) + 1e-06))

    gathered = partial.astype(BF16)
    for bit in reversed(bits):
        got = exchange(gathered, bit)
        odd = (index & bit) != 0
        gathered = jnp.concatenate(
            [jnp.where(odd, got, gathered), jnp.where(odd, gathered, got)], axis=0
        )
    update = gathered.astype(F32) * factor
    return (update[None], gradients[None])


def solution(mesh):
    return jax.shard_map(
        shards,
        mesh=mesh,
        in_specs=(
            P("segment", None, "slab", None, None, None),
            P("segment", None, None),
            P(None, "slab", None, None, None),
        ),
        out_specs=(P("segment", None, None), P("segment", None, "slab", None, None, None)),
        check_vma=False,
    )
```

```python
import functools
import math

import jax
import jax.numpy as jnp
from jax import lax
from jax.experimental import pallas as pl
from jax.experimental.pallas import tpu as pltpu
from jax.sharding import PartitionSpec as P

BF16 = jnp.bfloat16
F32 = jnp.float32


def pair_routes(count):
    near = [(i, i ^ 1) for i in range(count)]
    far = [(i, ((i + 1) ^ 1) - 1) for i in range(1, count - 1)]
    return near, far


def rims(low_planes, high_planes):
    near, far = pair_routes(lax.axis_size("slab"))
    even = lax.axis_index("slab") % 2 == 0
    got_near = lax.ppermute(jnp.where(even, high_planes, low_planes), "slab", near)
    got_far = lax.ppermute(jnp.where(even, low_planes, high_planes), "slab", far)
    return jnp.where(even, got_far, got_near), jnp.where(even, got_near, got_far)


def patches_of(rimmed, order):
    micro, depth, width, height, channels = rimmed.shape
    depth -= 2
    padded = jnp.pad(rimmed, ((0, 0), (0, 0), (1, 1), (1, 1), (0, 0)))
    pieces = []
    for offset in order:
        dz, dx, dy = offset // 9, offset // 3 % 3, offset % 3
        pieces.append(padded[:, dz : dz + depth, dx : dx + width, dy : dy + height])
    joined = jnp.concatenate(pieces, axis=-1)
    return joined.reshape(micro * depth * width * height, 27 * channels)


FORWARD = tuple(range(27))
BACKWARD = tuple(reversed(range(27)))


def exchange(value, mask):
    count = lax.axis_size("slab")
    return lax.ppermute(value, "slab", [(i, i ^ mask) for i in range(count)])


def cross(value, back, mask):
    segments, count = lax.axis_size("segment"), lax.axis_size("slab")
    if back == 0 and mask == 0:
        return value
    route = [
        (s * count + i, (s - back) % segments * count + (i ^ mask))
        for s in range(segments)
        for i in range(count)
    ]
    return lax.ppermute(value, ("segment", "slab"), route)


def block(value, place, rows, dtype):
    return lax.dynamic_slice_in_dim(value, place * rows, rows, 0).astype(dtype)


def place_kernel(bound, spot_ref, *refs):
    pieces, out_ref = refs[:-1], refs[-1]
    rows = out_ref.shape[1]
    here = pl.program_id(0)
    sums = [piece[rows:].astype(F32) for piece in pieces]
    while len(sums) > 1:
        sums = [a + b for a, b in zip(sums[::2], sums[1::2], strict=True)]
    norm = jnp.sqrt(jnp.sum(sums[0], axis=0, keepdims=True))
    factor = jnp.minimum(1.0, bound / (norm + 1e-06))
    for number, piece in enumerate(pieces):

        @pl.when(spot_ref[0] ^ number == here)
        def _():
            out_ref[0] = piece[:rows].astype(F32) * factor


def shards(activations, weights, out_grad):
    acts = activations[0]
    weight = weights[0]
    channels = weight.shape[1]
    micro, depth, width, height = acts.shape[:4]
    cells = micro * depth * width * height
    segments = lax.axis_size("segment")
    count = lax.axis_size("slab")
    sindex = lax.axis_index("segment")
    index = lax.axis_index("slab")
    last = sindex == segments - 1

    low = jnp.concatenate([acts[:, :2], out_grad[:, :1]], axis=1)
    high = jnp.concatenate([acts[:, -2:], out_grad[:, -1:]], axis=1)
    below, above = rims(low, high)
    wide = jnp.concatenate([below[:, :2], acts, above[:, :2]], axis=1)
    wide_up = jnp.concatenate([below[:, 2:], out_grad, above[:, 2:]], axis=1)

    patches = patches_of(wide, FORWARD)
    preact = jnp.dot(patches, weight, preferred_element_type=F32)
    sig = jax.nn.sigmoid(preact)
    slope = (sig * (1.0 + preact * (1.0 - sig))).reshape(micro, depth + 2, width, height, channels)
    inner_patches = patches.reshape(micro, depth + 2, width * height, 27 * channels)[:, 1:-1]
    inner_patches = inner_patches.reshape(cells, 27 * channels)
    inner_slope = slope[:, 1:-1]

    kernel = weight.reshape(27, channels, channels)

    def conv_back(delta_rim):
        moved = patches_of(delta_rim, BACKWARD).reshape(cells, 27, channels)
        out = lax.dot_general(
            moved, kernel, (((1, 2), (0, 2)), ((), ())), preferred_element_type=F32
        )
        return out.reshape(micro, depth, width, height, channels)

    back = [(i, (i - 1) % segments) for i in range(segments)]
    delta_rim = (wide_up.astype(F32) * slope).astype(BF16)
    result = (out_grad.astype(F32) + conv_back(delta_rim)).astype(BF16)
    upstream = out_grad
    deltas = delta_rim[:, 1:-1]
    for step in range(1, segments):
        incoming = lax.ppermute(result, "segment", back)
        upstream = jnp.where(last, out_grad, incoming)
        deltas = (upstream.astype(F32) * inner_slope).astype(BF16)
        if step < segments - 1:
            below, above = rims(deltas[:, :1], deltas[:, -1:])
            around = jnp.concatenate([below, deltas, above], axis=1)
            result = (upstream.astype(F32) + conv_back(around)).astype(BF16)

    partial = lax.dot_general(
        inner_patches,
        deltas.reshape(cells, channels),
        (((0,), (0,)), ((), ())),
        preferred_element_type=F32,
    )

    bits = [1 << n for n in range(1, count.bit_length() - 1)]
    inner = [bits[n : n + 2] for n in range(2, len(bits), 2)]
    crossing = inner[-1][0] if len(inner[-1]) == 1 else 0
    side = lax.rem(index, 2) ^ jnp.where(index & crossing, 1, 0)
    quarter = jnp.where(index & 2, 2, 0) + jnp.where(index & 4, 1, 0)
    rows = partial.shape[0] // 8
    masks = {1: 4, 2: 2, 3: 6}

    pieces = {}
    far = []
    for turn in (3, 2, 1, 0):
        there = quarter ^ turn
        got = exchange(block(partial, (1 - side) * 4 + there, rows, BF16), 1)
        if turn == 0:
            got, deltas = lax.optimization_barrier((got, deltas))
        piece = block(partial, side * 4 + there, rows, F32) + got.astype(F32)
        if turn:
            far.append(exchange(piece.astype(BF16), masks[turn]))
    chunk = piece + sum(other.astype(F32) for other in far)

    below, above = rims(deltas[:, :1], deltas[:, -1:])
    around = jnp.concatenate([below, deltas, above], axis=1)
    gradients = (upstream.astype(F32) + conv_back(around)).astype(BF16)

    def places(group):
        own = sum(jnp.where(index & bit, 1 << n, 0) for n, bit in enumerate(group))
        others = []
        for turn in range(1, 1 << len(group)):
            mask = sum(bit for n, bit in enumerate(group) if turn >> n & 1)
            others.append((mask | 1 if mask == crossing else mask, own ^ turn))
        return own, others

    for group in inner:
        own, others = places(group)
        part = chunk.shape[0] >> len(group)
        got = [exchange(block(chunk, there, part, BF16), mask) for mask, there in others]
        chunk = block(chunk, own, part, F32) + sum(g.astype(F32) for g in got)

    gathered = chunk.astype(BF16)
    for group in reversed(inner):
        own, others = places(group)
        got = [(there, exchange(gathered, mask)) for mask, there in others]
        if group is inner[-1]:
            squares = jnp.broadcast_to(jnp.sum(chunk * chunk), (8, 128))
            sums = []
            for mask in [0] + [mask for mask, _ in others]:
                sums.append(sum(cross(squares, back, mask) for back in range(segments)))
            while len(sums) > 1:
                sums = [a + b for a, b in zip(sums[::2], sums[1::2], strict=True)]
            squares = sums[0][0]
        blocks = []
        for n in range(1 << len(group)):
            value = jnp.where(own == n, gathered, got[0][1])
            for there, other in got[1:]:
                value = jnp.where(there == n, other, value)
            blocks.append(value)
        gathered = jnp.concatenate(blocks, axis=0)

    first = lax.reduce_precision(squares, 8, 7)
    second = lax.reduce_precision(squares - first, 8, 7)
    third = squares - first - second
    terms = jnp.zeros((16, channels), F32).at[0].set(first).at[1].set(second).at[2].set(third)
    payload = jnp.concatenate([gathered, terms.astype(BF16)], axis=0)
    near = [payload] + [exchange(payload, masks[turn]) for turn in (1, 2, 3)]
    both = near + [exchange(piece, 1) for piece in near]
    bound = math.sqrt(27.0 * channels * channels * segments)
    whole = [pl.BlockSpec(memory_space=pltpu.VMEM)] * 8
    update = pl.pallas_call(
        functools.partial(place_kernel, bound),
        out_shape=jax.ShapeDtypeStruct((8, rows, channels), F32),
        grid=(8,),
        in_specs=[pl.BlockSpec(memory_space=pltpu.SMEM)] + whole,
        out_specs=pl.BlockSpec((1, rows, channels), lambda j: (j, 0, 0)),
    )((side * 4 + quarter).reshape(1), *both)
    return (update.reshape(1, 8 * rows, channels), gradients[None])


def solution(mesh):
    return jax.shard_map(
        shards,
        mesh=mesh,
        in_specs=(
            P("segment", None, "slab", None, None, None),
            P("segment", None, None),
            P(None, "slab", None, None, None),
        ),
        out_specs=(P("segment", None, None), P("segment", None, "slab", None, None, None)),
        check_vma=False,
    )
```

```python
import functools
import math

import jax
import jax.numpy as jnp
from jax import lax
from jax.experimental import pallas as pl
from jax.experimental.pallas import tpu as pltpu
from jax.sharding import PartitionSpec as P

BF16 = jnp.bfloat16
F32 = jnp.float32
VMEM = pl.BlockSpec(memory_space=pltpu.VMEM)
SMEM = pl.BlockSpec(memory_space=pltpu.SMEM)
ANY = pl.BlockSpec(memory_space=pl.ANY)


def swap(to_near, to_far):
    count = lax.axis_size("slab")
    near = [(i, i ^ 1) for i in range(count)]
    far = [(i, ((i + 1) ^ 1) - 1) for i in range(1, count - 1)]
    return lax.ppermute(to_near, "slab", near), lax.ppermute(to_far, "slab", far)


def exchange(value, mask):
    count = lax.axis_size("slab")
    return lax.ppermute(value, "slab", [(i, i ^ mask) for i in range(count)])


def cross(value, back, mask):
    segments, count = lax.axis_size("segment"), lax.axis_size("slab")
    if back == 0 and mask == 0:
        return value
    route = [
        (s * count + i, (s - back) % segments * count + (i ^ mask))
        for s in range(segments)
        for i in range(count)
    ]
    return lax.ppermute(value, ("segment", "slab"), route)


def block(value, place, rows, dtype):
    return lax.dynamic_slice_in_dim(value, place * rows, rows, 0).astype(dtype)


def write_shifts(plane, height, out_ref, first):
    cells, channels = plane.shape
    width = cells // height
    rows = plane.astype(F32).reshape(width, height, channels)
    at = lax.broadcasted_iota(jnp.int32, rows.shape, 1)
    zero = jnp.zeros((1, height, channels), F32)
    before = jnp.where(at == 0, 0.0, pltpu.roll(rows, 1, 1))
    after = jnp.where(at == height - 1, 0.0, pltpu.roll(rows, height - 1, 1))
    for dy, moved in enumerate((before, rows, after)):
        for dx in range(3):
            if dx == 0:
                value = jnp.concatenate([zero, moved[:-1]], axis=0)
            elif dx == 1:
                value = moved
            else:
                value = jnp.concatenate([moved[1:], zero], axis=0)
            j = dx * 3 + dy
            out_ref[first : first + cells, j * channels : (j + 1) * channels] = value.reshape(
                cells, channels
            ).astype(BF16)


def back_product(shifts, weight_ref, rows, cells):
    channels = weight_ref.shape[1]
    total = None
    for dz in range(3):
        mirrored = [26 - 9 * dz - j for j in range(9)]
        side = jnp.concatenate(
            [weight_ref[k * channels : (k + 1) * channels, :] for k in mirrored], axis=1
        )
        term = lax.dot_general(
            shifts[dz * cells : dz * cells + rows, :],
            side,
            (((1,), (1,)), ((), ())),
            preferred_element_type=F32,
        )
        total = term if total is None else total + term
    return total


def rim_kernel(flag, acts, grad, near, far, sems):
    micro, depth = acts.shape[:2]
    top = flag[0]
    copies = []
    for which, (out, high) in enumerate(((near, top), (far, 1 - top))):
        for m in range(micro):
            for part, (source, size, at) in enumerate(((acts, 2, 0), (grad, 1, 2))):
                copy = pltpu.make_async_copy(
                    source.at[m, pl.ds(high * (depth - size), size)],
                    out.at[m, at : at + size],
                    sems.at[which, m, part],
                )
                copy.start()
                copies.append(copy)
    for copy in copies:
        copy.wait()


def first_kernel(height, flag, acts, near, far, grad, weight, result, slopes, shifts, deltas):
    micro, depth, cells, channels = acts.shape
    even = flag[0] == 1
    span = 9 * channels
    rows = depth * cells
    for m in range(micro):

        def rim(a, b, n):
            return jnp.where(even, a[m, n].astype(F32), b[m, n].astype(F32))

        planes = [rim(far, near, n) for n in range(2)]
        planes += [acts[m, n] for n in range(depth)]
        planes += [rim(near, far, n) for n in range(2)]
        for n, plane in enumerate(planes):
            write_shifts(plane, height, shifts.at[m], n * cells)
        preact = None
        for dz in range(3):
            term = jnp.dot(
                shifts[m, dz * cells : dz * cells + rows + 2 * cells, :],
                weight[dz * span : (dz + 1) * span, :],
                preferred_element_type=F32,
            )
            preact = term if preact is None else preact + term
        sig = 1.0 / (1.0 + jnp.exp(-preact))
        slope = sig * (1.0 + preact * (1.0 - sig))
        slopes[m] = slope[cells : cells + rows]
        ups = [rim(far, near, 2)] + [grad[m, n].astype(F32) for n in range(depth)]
        ups.append(rim(near, far, 2))
        for n, up in enumerate(ups):
            delta = (up * slope[n * cells : (n + 1) * cells]).astype(BF16)
            write_shifts(delta, height, deltas.at[m], n * cells)
        back = back_product(deltas.at[m], weight, rows, cells)
        upstream = grad[m].reshape(rows, channels).astype(F32)
        result[m] = (upstream + back).astype(BF16)


def patch_kernel(cells, shifts, out):
    micro, total, span = shifts.shape
    rows = total - 4 * cells
    for m in range(micro):
        for dz in range(3):
            first = (1 + dz) * cells
            out[m * rows : (m + 1) * rows, dz * span : (dz + 1) * span] = shifts[
                m, first : first + rows, :
            ]


def back_kernel(height, flag, deltas, near, far, upstream, weight, out, shifts):
    micro, depth, cells, channels = deltas.shape
    even = flag[0] == 1
    rows = depth * cells
    for m in range(micro):
        low, high = near[m, 0].astype(F32), far[m, 0].astype(F32)
        planes = [jnp.where(even, high, low)] + [deltas[m, n] for n in range(depth)]
        planes.append(jnp.where(even, low, high))
        for n, plane in enumerate(planes):
            write_shifts(plane, height, shifts.at[m], n * cells)
        back = back_product(shifts.at[m], weight, rows, cells)
        total = upstream[m].reshape(rows, channels).astype(F32) + back
        out[m] = total.astype(BF16).reshape(depth, cells, channels)


def place_kernel(bound, spot, *refs):
    pieces, (out, scaled, sems) = refs[:-3], refs[-3:]
    rows = scaled.shape[1]
    sums = [piece[rows:].astype(F32) for piece in pieces]
    while len(sums) > 1:
        sums = [a + b for a, b in zip(sums[::2], sums[1::2], strict=True)]
    norm = jnp.sqrt(jnp.sum(sums[0], axis=0, keepdims=True))
    factor = jnp.minimum(1.0, bound / (norm + 1e-06))
    copies = []
    for n, piece in enumerate(pieces):
        scaled[n] = piece[:rows].astype(F32) * factor
        copies.append(pltpu.make_async_copy(scaled.at[n], out.at[spot[0] ^ n], sems.at[n]))
        copies[-1].start()
    for copy in copies:
        copy.wait()


def shards(activations, weights, out_grad):
    weight = weights[0]
    channels = weight.shape[1]
    micro, depth, width, height = activations.shape[1:5]
    cells = width * height
    acts = activations[0].reshape(micro, depth, cells, channels)
    grad = out_grad.reshape(micro, depth, cells, channels)
    rows = depth * cells
    segments = lax.axis_size("segment")
    count = lax.axis_size("slab")
    index = lax.axis_index("slab")
    last = lax.axis_index("segment") == segments - 1
    flag = (1 - lax.rem(index, 2)).astype(jnp.int32).reshape(1)
    params = pltpu.CompilerParams(vmem_limit_bytes=40 << 20)

    rim = jax.ShapeDtypeStruct((micro, 3, cells, channels), BF16)
    to_near, to_far = pl.pallas_call(
        rim_kernel,
        out_shape=(rim, rim),
        in_specs=[SMEM, ANY, ANY],
        out_specs=(VMEM, VMEM),
        scratch_shapes=[pltpu.SemaphoreType.DMA((2, micro, 2))],
    )(flag, acts, grad)
    near, far = swap(to_near, to_far)

    result, slopes, shifts = pl.pallas_call(
        functools.partial(first_kernel, height),
        out_shape=(
            jax.ShapeDtypeStruct((micro, rows, channels), BF16),
            jax.ShapeDtypeStruct((micro, rows, channels), F32),
            jax.ShapeDtypeStruct((micro, rows + 4 * cells, 9 * channels), BF16),
        ),
        in_specs=[SMEM] + [VMEM] * 5,
        out_specs=(VMEM, VMEM, VMEM),
        scratch_shapes=[pltpu.VMEM((micro, rows + 2 * cells, 9 * channels), BF16)],
        compiler_params=params,
    )(flag, acts, near, far, grad, weight)
    patches = pl.pallas_call(
        functools.partial(patch_kernel, cells),
        out_shape=jax.ShapeDtypeStruct((micro * rows, 27 * channels), BF16),
        in_specs=[VMEM],
        out_specs=VMEM,
        compiler_params=params,
    )(shifts)

    def rims(value):
        low, high = value[:, :1], value[:, -1:]
        even = flag[0] == 1
        return swap(jnp.where(even, high, low), jnp.where(even, low, high))

    def conv_back(value, near, far, upstream):
        return pl.pallas_call(
            functools.partial(back_kernel, height),
            out_shape=jax.ShapeDtypeStruct((micro, depth, cells, channels), BF16),
            in_specs=[SMEM] + [VMEM] * 5,
            out_specs=VMEM,
            scratch_shapes=[pltpu.VMEM((micro, rows + 2 * cells, 9 * channels), BF16)],
            compiler_params=params,
        )(flag, value, near, far, upstream, weight)

    result = result.reshape(micro, depth, cells, channels)
    upstream, deltas = grad, None
    for step in range(1, segments):
        incoming = cross(result, 1, 0)
        upstream = jnp.where(last, grad, incoming)
        slope = slopes.reshape(micro, depth, cells, channels)
        deltas = (upstream.astype(F32) * slope).astype(BF16)
        if step < segments - 1:
            result = conv_back(deltas, *rims(deltas), upstream)

    partial = lax.dot_general(
        patches,
        deltas.reshape(micro * rows, channels),
        (((0,), (0,)), ((), ())),
        preferred_element_type=F32,
    )

    bits = [1 << n for n in range(1, count.bit_length() - 1)]
    inner = [bits[n : n + 2] for n in range(2, len(bits), 2)]
    crossing = inner[-1][0] if len(inner[-1]) == 1 else 0
    side = lax.rem(index, 2) ^ jnp.where(index & crossing, 1, 0)
    quarter = jnp.where(index & 2, 2, 0) + jnp.where(index & 4, 1, 0)
    part = partial.shape[0] // 8
    masks = {1: 4, 2: 2, 3: 6}

    pieces = {}
    far = []
    for turn in (3, 2, 1, 0):
        there = quarter ^ turn
        got = exchange(block(partial, (1 - side) * 4 + there, part, BF16), 1)
        if turn == 0:
            got, deltas = lax.optimization_barrier((got, deltas))
        piece = block(partial, side * 4 + there, part, F32) + got.astype(F32)
        if turn:
            far.append(exchange(piece.astype(BF16), masks[turn]))
    chunk = piece + sum(other.astype(F32) for other in far)

    gradients = conv_back(deltas, *rims(deltas), upstream)

    def places(group):
        own = sum(jnp.where(index & bit, 1 << n, 0) for n, bit in enumerate(group))
        others = []
        for turn in range(1, 1 << len(group)):
            mask = sum(bit for n, bit in enumerate(group) if turn >> n & 1)
            others.append((mask | 1 if mask == crossing else mask, own ^ turn))
        return own, others

    for group in inner:
        own, others = places(group)
        size = chunk.shape[0] >> len(group)
        got = [exchange(block(chunk, there, size, BF16), mask) for mask, there in others]
        chunk = block(chunk, own, size, F32) + sum(g.astype(F32) for g in got)

    gathered = chunk.astype(BF16)
    for group in reversed(inner):
        own, others = places(group)
        got = [(there, exchange(gathered, mask)) for mask, there in others]
        if group is inner[-1]:
            squares = jnp.broadcast_to(jnp.sum(chunk * chunk), (8, 128))
            sums = []
            for mask in [0] + [mask for mask, _ in others]:
                sums.append(sum(cross(squares, back, mask) for back in range(segments)))
            while len(sums) > 1:
                sums = [a + b for a, b in zip(sums[::2], sums[1::2], strict=True)]
            squares = sums[0][0]
        blocks = []
        for n in range(1 << len(group)):
            value = jnp.where(own == n, gathered, got[0][1])
            for there, other in got[1:]:
                value = jnp.where(there == n, other, value)
            blocks.append(value)
        gathered = jnp.concatenate(blocks, axis=0)

    first = lax.reduce_precision(squares, 8, 7)
    second = lax.reduce_precision(squares - first, 8, 7)
    third = squares - first - second
    terms = jnp.zeros((16, channels), F32).at[0].set(first).at[1].set(second).at[2].set(third)
    payload = jnp.concatenate([gathered, terms.astype(BF16)], axis=0)
    near = [payload] + [exchange(payload, masks[turn]) for turn in (1, 2, 3)]
    both = near + [exchange(piece, 1) for piece in near]
    bound = math.sqrt(27.0 * channels * channels * segments)
    update = pl.pallas_call(
        functools.partial(place_kernel, bound),
        out_shape=jax.ShapeDtypeStruct((8, part, channels), F32),
        in_specs=[SMEM] + [VMEM] * 8,
        out_specs=ANY,
        scratch_shapes=[pltpu.VMEM((8, part, channels), F32), pltpu.SemaphoreType.DMA((8,))],
    )((side * 4 + quarter).astype(jnp.int32).reshape(1), *both)
    gradients = gradients.reshape(1, micro, depth, width, height, channels)
    return (update.reshape(1, 8 * part, channels), gradients)


def solution(mesh):
    return jax.shard_map(
        shards,
        mesh=mesh,
        in_specs=(
            P("segment", None, "slab", None, None, None),
            P("segment", None, None),
            P(None, "slab", None, None, None),
        ),
        out_specs=(P("segment", None, None), P("segment", None, "slab", None, None, None)),
        check_vma=False,
    )
```

```python
import functools
import math

import jax
import jax.numpy as jnp
from jax import lax
from jax.experimental import pallas as pl
from jax.experimental.pallas import tpu as pltpu
from jax.sharding import PartitionSpec as P

BF16 = jnp.bfloat16
F32 = jnp.float32
VMEM = pl.BlockSpec(memory_space=pltpu.VMEM)
SMEM = pl.BlockSpec(memory_space=pltpu.SMEM)
ANY = pl.BlockSpec(memory_space=pl.ANY)


def swap(to_near, to_far):
    count = lax.axis_size("slab")
    near = [(i, i ^ 1) for i in range(count)]
    far = [(i, ((i + 1) ^ 1) - 1) for i in range(1, count - 1)]
    return lax.ppermute(to_near, "slab", near), lax.ppermute(to_far, "slab", far)


def exchange(value, mask):
    count = lax.axis_size("slab")
    return lax.ppermute(value, "slab", [(i, i ^ mask) for i in range(count)])


def cross(value, back, mask):
    segments, count = lax.axis_size("segment"), lax.axis_size("slab")
    if back == 0 and mask == 0:
        return value
    route = [
        (s * count + i, (s - back) % segments * count + (i ^ mask))
        for s in range(segments)
        for i in range(count)
    ]
    return lax.ppermute(value, ("segment", "slab"), route)


def block(value, place, rows, dtype):
    return lax.dynamic_slice_in_dim(value, place * rows, rows, 0).astype(dtype)


def write_shifts(plane, height, out_ref, first):
    cells, channels = plane.shape
    width = cells // height
    rows = plane.astype(F32).reshape(width, height, channels)
    at = lax.broadcasted_iota(jnp.int32, rows.shape, 1)
    zero = jnp.zeros((1, height, channels), F32)
    before = jnp.where(at == 0, 0.0, pltpu.roll(rows, 1, 1))
    after = jnp.where(at == height - 1, 0.0, pltpu.roll(rows, height - 1, 1))
    for dy, moved in enumerate((before, rows, after)):
        for dx in range(3):
            if dx == 0:
                value = jnp.concatenate([zero, moved[:-1]], axis=0)
            elif dx == 1:
                value = moved
            else:
                value = jnp.concatenate([moved[1:], zero], axis=0)
            j = dx * 3 + dy
            out_ref[first : first + cells, j * channels : (j + 1) * channels] = value.reshape(
                cells, channels
            ).astype(BF16)


def back_product(shifts, weight_ref, rows, cells):
    channels = weight_ref.shape[1]
    total = None
    for dz in range(3):
        mirrored = [26 - 9 * dz - j for j in range(9)]
        side = jnp.concatenate(
            [weight_ref[k * channels : (k + 1) * channels, :] for k in mirrored], axis=1
        )
        term = lax.dot_general(
            shifts[dz * cells : dz * cells + rows, :],
            side,
            (((1,), (1,)), ((), ())),
            preferred_element_type=F32,
        )
        total = term if total is None else total + term
    return total


def rim_kernel(acts, grad, weight, near, far, acts_here, grad_here, weight_here, sems, loads):
    micro, depth = acts.shape[:2]
    top = 1 - lax.rem(lax.axis_index("slab"), 2)
    copies = []
    for which, (out, high) in enumerate(((near, top), (far, 1 - top))):
        for m in range(micro):
            for part, (source, size, at) in enumerate(((acts, 2, 0), (grad, 1, 2))):
                copies.append(
                    pltpu.make_async_copy(
                        source.at[m, pl.ds(high * (depth - size), size)],
                        out.at[m, at : at + size],
                        sems.at[which, m, part],
                    )
                )
    for n, (source, out) in enumerate(
        ((acts, acts_here), (grad, grad_here), (weight, weight_here))
    ):
        copies.append(pltpu.make_async_copy(source, out, loads.at[n]))
    for copy in copies:
        copy.start()
    for copy in copies:
        copy.wait()


def first_kernel(height, acts, near, far, grad, weight, result, slopes, shifts, deltas):
    micro, depth, cells, channels = acts.shape
    even = lax.rem(lax.axis_index("slab"), 2) == 0
    span = 9 * channels
    rows = depth * cells
    for m in range(micro):

        def rim(a, b, n):
            return jnp.where(even, a[m, n].astype(F32), b[m, n].astype(F32))

        planes = [rim(far, near, n) for n in range(2)]
        planes += [acts[m, n] for n in range(depth)]
        planes += [rim(near, far, n) for n in range(2)]
        for n, plane in enumerate(planes):
            write_shifts(plane, height, shifts.at[m], n * cells)
        preact = None
        for dz in range(3):
            term = jnp.dot(
                shifts[m, dz * cells : dz * cells + rows + 2 * cells, :],
                weight[dz * span : (dz + 1) * span, :],
                preferred_element_type=F32,
            )
            preact = term if preact is None else preact + term
        sig = 1.0 / (1.0 + jnp.exp(-preact))
        slope = sig * (1.0 + preact * (1.0 - sig))
        slopes[m] = slope[cells : cells + rows]
        ups = [rim(far, near, 2)] + [grad[m, n].astype(F32) for n in range(depth)]
        ups.append(rim(near, far, 2))
        for n, up in enumerate(ups):
            delta = (up * slope[n * cells : (n + 1) * cells]).astype(BF16)
            write_shifts(delta, height, deltas.at[m], n * cells)
        back = back_product(deltas.at[m], weight, rows, cells)
        upstream = grad[m].reshape(rows, channels).astype(F32)
        result[m] = (upstream + back).astype(BF16)


def raw_kernel(spot, incoming, grad, slopes, shifts, upstream, deltas, near, far, *refs):
    sends, (keep, raw) = refs[:4], refs[4:]
    micro, depth, cells, channels = deltas.shape
    rows = depth * cells
    span = 9 * channels
    last = lax.axis_index("segment") == lax.axis_size("segment") - 1
    even = lax.rem(lax.axis_index("slab"), 2) == 0
    deltas_of = []
    for m in range(micro):
        up = jnp.where(last, grad[m].astype(F32), incoming[m].astype(F32))
        upstream[m] = up.astype(BF16)
        delta = (up.reshape(rows, channels) * slopes[m]).astype(BF16)
        deltas[m] = delta.reshape(depth, cells, channels)
        low, high = delta[:cells].astype(F32), delta[-cells:].astype(F32)
        near[m, 0] = jnp.where(even, high, low).astype(BF16)
        far[m, 0] = jnp.where(even, low, high).astype(BF16)
        deltas_of.append(delta)
    for dz in range(3):
        total = None
        for m in range(micro):
            first = (1 + dz) * cells
            term = lax.dot_general(
                shifts[m, first : first + rows, :],
                deltas_of[m],
                (((0,), (0,)), ((), ())),
                preferred_element_type=F32,
            )
            total = term if total is None else total + term
        raw[dz * span : (dz + 1) * span, :] = total
    part = keep.shape[1]
    for turn in range(4):
        keep[turn] = raw[pl.ds((spot[0] ^ turn) * part, part), :]
        sends[turn][...] = raw[pl.ds((spot[0] ^ turn ^ 4) * part, part), :].astype(BF16)


def add_kernel(turn, keep, got, out):
    out[...] = (keep[turn] + got[...].astype(F32)).astype(BF16)


def sum_kernel(keep, *refs):
    total = keep[0]
    for got in refs[:-1]:
        total = total + got[...].astype(F32)
    refs[-1][...] = total


def column_squares(value):
    value = value.astype(F32)
    return jnp.sum(value * value, axis=0, keepdims=True)


def chunk_kernel(keep, *refs):
    total = keep[...]
    for got in refs[:-2]:
        total = total + got[...].astype(F32)
    chunk, squares = refs[-2:]
    chunk[...] = total.astype(BF16)
    squares[...] = jnp.broadcast_to(column_squares(chunk[...]), squares.shape)


def payload_kernel(count, gathered, *refs):
    own, values, out = refs[:count], refs[count:-1], refs[-1]
    sums = [column_squares(piece[...]) for piece in own]
    for n, value in enumerate(values):
        sums[n % count] = sums[n % count] + value[:1, :]
    while len(sums) > 1:
        sums = [a + b for a, b in zip(sums[::2], sums[1::2], strict=True)]
    rows = gathered.shape[0]
    out[:rows] = gathered[...]
    high = sums[0].astype(BF16).astype(F32)
    middle = (sums[0] - high).astype(BF16).astype(F32)
    low = sums[0] - high - middle
    at = lax.broadcasted_iota(jnp.int32, (16, gathered.shape[1]), 0)
    terms = jnp.where(at == 0, high, jnp.where(at == 1, middle, jnp.where(at == 2, low, 0.0)))
    out[rows:] = terms.astype(BF16)


def back_kernel(height, deltas, near, far, upstream, weight, out, shifts):
    micro, depth, cells, channels = deltas.shape
    even = lax.rem(lax.axis_index("slab"), 2) == 0
    rows = depth * cells
    for m in range(micro):
        low, high = near[m, 0].astype(F32), far[m, 0].astype(F32)
        planes = [jnp.where(even, high, low)] + [deltas[m, n] for n in range(depth)]
        planes.append(jnp.where(even, low, high))
        for n, plane in enumerate(planes):
            write_shifts(plane, height, shifts.at[m], n * cells)
        back = back_product(shifts.at[m], weight, rows, cells)
        total = upstream[m].reshape(rows, channels).astype(F32) + back
        out[m] = total.astype(BF16).reshape(depth, cells, channels)


def place_kernel(bound, spot, *refs):
    pieces, (out, scaled, sems) = refs[:-3], refs[-3:]
    rows = scaled.shape[1]
    sums = [piece[rows:].astype(F32) for piece in pieces]
    while len(sums) > 1:
        sums = [a + b for a, b in zip(sums[::2], sums[1::2], strict=True)]
    norm = jnp.sqrt(jnp.sum(jnp.sum(sums[0], axis=0, keepdims=True), axis=1, keepdims=True))
    factor = jnp.minimum(1.0, bound / (norm + 1e-06))
    copies = []
    for n, piece in enumerate(pieces):
        scaled[n] = piece[:rows].astype(F32) * factor
        copies.append(pltpu.make_async_copy(scaled.at[n], out.at[spot[0] ^ n], sems.at[n]))
        copies[-1].start()
    for copy in copies:
        copy.wait()


def shards(activations, weights, out_grad):
    weight = weights[0]
    channels = weight.shape[1]
    micro, depth, width, height = activations.shape[1:5]
    cells = width * height
    acts = activations[0].reshape(micro, depth, cells, channels)
    grad = out_grad.reshape(micro, depth, cells, channels)
    rows = depth * cells
    segments = lax.axis_size("segment")
    count = lax.axis_size("slab")
    index = lax.axis_index("slab")
    last = lax.axis_index("segment") == segments - 1
    large = pltpu.CompilerParams(vmem_limit_bytes=16 << 20)
    small = pltpu.CompilerParams(vmem_limit_bytes=4 << 20)

    shape = jax.ShapeDtypeStruct
    rim = shape((micro, 3, cells, channels), BF16)
    volume = shape((micro, depth, cells, channels), BF16)
    to_near, to_far, acts, grad, weight = pl.pallas_call(
        rim_kernel,
        out_shape=(rim, rim, volume, volume, shape(weight.shape, BF16)),
        in_specs=[ANY, ANY, ANY],
        out_specs=(VMEM,) * 5,
        scratch_shapes=[pltpu.SemaphoreType.DMA((2, micro, 2)), pltpu.SemaphoreType.DMA((3,))],
        compiler_params=small,
    )(acts, grad, weight)
    near, far = swap(to_near, to_far)

    result, slopes, shifts = pl.pallas_call(
        functools.partial(first_kernel, height),
        out_shape=(
            shape((micro, rows, channels), BF16),
            shape((micro, rows, channels), F32),
            shape((micro, rows + 4 * cells, 9 * channels), BF16),
        ),
        in_specs=[VMEM] * 5,
        out_specs=(VMEM, VMEM, VMEM),
        scratch_shapes=[pltpu.VMEM((micro, rows + 2 * cells, 9 * channels), BF16)],
        compiler_params=large,
    )(acts, near, far, grad, weight)

    def rims(value):
        low, high = value[:, :1], value[:, -1:]
        even = lax.rem(index, 2) == 0
        return jnp.where(even, high, low), jnp.where(even, low, high)

    def conv_back(value, near, far, upstream):
        return pl.pallas_call(
            functools.partial(back_kernel, height),
            out_shape=jax.ShapeDtypeStruct((micro, depth, cells, channels), BF16),
            in_specs=[VMEM] * 5,
            out_specs=VMEM,
            scratch_shapes=[pltpu.VMEM((micro, rows + 2 * cells, 9 * channels), BF16)],
            compiler_params=large,
        )(value, near, far, upstream, weight)

    result = result.reshape(micro, depth, cells, channels)
    for step in range(1, segments - 1):
        incoming = cross(result, 1, 0)
        upstream = jnp.where(last, grad, incoming)
        slope = slopes.reshape(micro, depth, cells, channels)
        deltas = (upstream.astype(F32) * slope).astype(BF16)
        result = conv_back(deltas, *swap(*rims(deltas)), upstream)
    incoming = cross(result, 1, 0)

    bits = [1 << n for n in range(1, count.bit_length() - 1)]
    inner = [bits[n : n + 2] for n in range(2, len(bits), 2)]
    crossing = inner[-1][0] if len(inner[-1]) == 1 else 0
    side = lax.rem(index, 2) ^ jnp.where(index & crossing, 1, 0)
    quarter = jnp.where(index & 2, 2, 0) + jnp.where(index & 4, 1, 0)
    masks = {1: 4, 2: 2, 3: 6}
    spot = (side * 4 + quarter).astype(jnp.int32).reshape(1)
    part = weight.shape[0] // 8
    piece = shape((part, channels), BF16)
    edge = shape((micro, 1, cells, channels), BF16)

    upstream, deltas, to_near, to_far, *rest = pl.pallas_call(
        raw_kernel,
        out_shape=(volume, volume, edge, edge) + (piece,) * 4 + (shape((4, part, channels), F32),),
        in_specs=[SMEM] + [VMEM] * 4,
        out_specs=(VMEM,) * 9,
        scratch_shapes=[pltpu.VMEM((8 * part, channels), F32)],
        compiler_params=large,
    )(spot, incoming, grad, slopes, shifts)
    sends, keep = rest[:4], rest[4]
    got = {turn: exchange(sends[turn], 1) for turn in (3, 2, 1, 0)}
    far = []
    for turn in (3, 2, 1):
        added = pl.pallas_call(
            functools.partial(add_kernel, turn),
            out_shape=piece,
            in_specs=[VMEM] * 2,
            out_specs=VMEM,
            compiler_params=small,
        )(keep, got[turn])
        far.append(exchange(added, masks[turn]))
    chunk = pl.pallas_call(
        sum_kernel,
        out_shape=shape((part, channels), F32),
        in_specs=[VMEM] * 5,
        out_specs=VMEM,
        compiler_params=small,
    )(keep, got[0], *far)

    def places(group):
        own = sum(jnp.where(index & bit, 1 << n, 0) for n, bit in enumerate(group))
        others = []
        for turn in range(1, 1 << len(group)):
            mask = sum(bit for n, bit in enumerate(group) if turn >> n & 1)
            others.append((mask | 1 if mask == crossing else mask, own ^ turn))
        return own, others

    for group in inner:
        own, others = places(group)
        size = chunk.shape[0] >> len(group)
        got = [exchange(block(chunk, there, size, BF16), mask) for mask, there in others]
        chunk = block(chunk, own, size, F32)
        if group is not inner[-1]:
            chunk = chunk + sum(g.astype(F32) for g in got)
    gathered, squares = pl.pallas_call(
        chunk_kernel,
        out_shape=(shape(chunk.shape, BF16), shape((8, channels), F32)),
        in_specs=[VMEM] * (1 + len(got)),
        out_specs=(VMEM, VMEM),
        compiler_params=small,
    )(chunk, *got)

    for group in reversed(inner):
        own, others = places(group)
        got = [(there, exchange(gathered, mask)) for mask, there in others]
        if group is inner[-1]:
            members = [gathered] + [other for _, other in got]
            met = [
                cross(squares, back, mask)
                for back in range(1, segments)
                for mask in [0] + [mask for mask, _ in others]
            ]
        blocks = []
        for n in range(1 << len(group)):
            value = jnp.where(own == n, gathered, got[0][1])
            for there, other in got[1:]:
                value = jnp.where(there == n, other, value)
            blocks.append(value)
        gathered = jnp.concatenate(blocks, axis=0)
    payload = pl.pallas_call(
        functools.partial(payload_kernel, len(members)),
        out_shape=shape((part + 16, channels), BF16),
        in_specs=[VMEM] * (1 + len(members) + len(met)),
        out_specs=VMEM,
        compiler_params=small,
    )(gathered, *members, *met)
    pieces = {turn: exchange(payload, masks[turn]) for turn in (3, 2, 1)}
    pieces[3], to_near, to_far = lax.optimization_barrier((pieces[3], to_near, to_far))
    gradients = conv_back(deltas, *swap(to_near, to_far), upstream)
    near = [payload] + [pieces[turn] for turn in (1, 2, 3)]
    both = near + [exchange(piece, 1) for piece in near]
    bound = math.sqrt(27.0 * channels * channels * segments)
    update = pl.pallas_call(
        functools.partial(place_kernel, bound),
        out_shape=jax.ShapeDtypeStruct((8, part, channels), F32),
        in_specs=[SMEM] + [VMEM] * 8,
        out_specs=ANY,
        scratch_shapes=[pltpu.VMEM((8, part, channels), F32), pltpu.SemaphoreType.DMA((8,))],
        compiler_params=large,
    )((side * 4 + quarter).astype(jnp.int32).reshape(1), *both)
    gradients = gradients.reshape(1, micro, depth, width, height, channels)
    return (update.reshape(1, 8 * part, channels), gradients)


def solution(mesh):
    return jax.shard_map(
        shards,
        mesh=mesh,
        in_specs=(
            P("segment", None, "slab", None, None, None),
            P("segment", None, None),
            P(None, "slab", None, None, None),
        ),
        out_specs=(P("segment", None, None), P("segment", None, "slab", None, None, None)),
        check_vma=False,
    )
```

```python
import functools
import math

import jax
import jax.numpy as jnp
from jax import lax
from jax.experimental import pallas as pl
from jax.experimental.pallas import tpu as pltpu
from jax.sharding import PartitionSpec as P

BF16 = jnp.bfloat16
F32 = jnp.float32
VMEM = pl.BlockSpec(memory_space=pltpu.VMEM)
SMEM = pl.BlockSpec(memory_space=pltpu.SMEM)
ANY = pl.BlockSpec(memory_space=pl.ANY)
HBM = pl.BlockSpec(memory_space=pltpu.HBM)


def far_route(count):
    return [(i, ((i + 1) ^ 1) - 1) for i in range(1, count - 1)]


def swap(to_near, to_far):
    count = lax.axis_size("slab")
    near = [(i, i ^ 1) for i in range(count)]
    return lax.ppermute(to_near, "slab", near), lax.ppermute(to_far, "slab", far_route(count))


def cross_far(value):
    segments, count = lax.axis_size("segment"), lax.axis_size("slab")
    route = [
        (s * count + i, (s - 1) % segments * count + j)
        for s in range(segments)
        for i, j in far_route(count)
    ]
    return lax.ppermute(value, ("segment", "slab"), route)


def exchange(value, mask):
    count = lax.axis_size("slab")
    return lax.ppermute(value, "slab", [(i, i ^ mask) for i in range(count)])


def cross(value, back, mask):
    segments, count = lax.axis_size("segment"), lax.axis_size("slab")
    if back == 0 and mask == 0:
        return value
    route = [
        (s * count + i, (s - back) % segments * count + (i ^ mask))
        for s in range(segments)
        for i in range(count)
    ]
    return lax.ppermute(value, ("segment", "slab"), route)


def block(value, place, rows, dtype):
    return lax.dynamic_slice_in_dim(value, place * rows, rows, 0).astype(dtype)


def write_shifts(plane, height, out_ref, first):
    cells, channels = plane.shape
    width = cells // height
    rows = plane.astype(F32).reshape(width, height, channels)
    at = lax.broadcasted_iota(jnp.int32, rows.shape, 1)
    zero = jnp.zeros((1, height, channels), F32)
    before = jnp.where(at == 0, 0.0, pltpu.roll(rows, 1, 1))
    after = jnp.where(at == height - 1, 0.0, pltpu.roll(rows, height - 1, 1))
    for dy, moved in enumerate((before, rows, after)):
        for dx in range(3):
            if dx == 0:
                value = jnp.concatenate([zero, moved[:-1]], axis=0)
            elif dx == 1:
                value = moved
            else:
                value = jnp.concatenate([moved[1:], zero], axis=0)
            j = dx * 3 + dy
            out_ref[first : first + cells, j * channels : (j + 1) * channels] = value.reshape(
                cells, channels
            ).astype(BF16)


def back_product(shifts, weight_ref, rows, cells):
    channels = weight_ref.shape[1]
    total = None
    for dz in range(3):
        mirrored = [26 - 9 * dz - j for j in range(9)]
        side = jnp.concatenate(
            [weight_ref[k * channels : (k + 1) * channels, :] for k in mirrored], axis=1
        )
        term = lax.dot_general(
            shifts[dz * cells : dz * cells + rows, :],
            side,
            (((1,), (1,)), ((), ())),
            preferred_element_type=F32,
        )
        total = term if total is None else total + term
    return total


def rim_kernel(acts, grad, weight, near, far, acts_here, grad_here, weight_here, sems, loads):
    micro, depth = acts.shape[:2]
    top = 1 - lax.rem(lax.axis_index("slab"), 2)
    copies = []
    for which, (out, high) in enumerate(((near, top), (far, 1 - top))):
        for m in range(micro):
            for part, (source, size, at) in enumerate(((acts, 2, 0), (grad, 1, 2))):
                copies.append(
                    pltpu.make_async_copy(
                        source.at[m, pl.ds(high * (depth - size), size)],
                        out.at[m, at : at + size],
                        sems.at[which, m, part],
                    )
                )
    for n, (source, out) in enumerate(
        ((acts, acts_here), (grad, grad_here), (weight, weight_here))
    ):
        copies.append(pltpu.make_async_copy(source, out, loads.at[n]))
    for copy in copies:
        copy.start()
    for copy in copies:
        copy.wait()


def first_kernel(
    height, acts, near, far, grad, weight, result, to_near, to_far, slopes, shifts, deltas
):
    micro, depth, cells, channels = acts.shape
    even = lax.rem(lax.axis_index("slab"), 2) == 0
    span = 9 * channels
    rows = depth * cells
    for m in range(micro):

        def rim(a, b, n):
            return jnp.where(even, a[m, n].astype(F32), b[m, n].astype(F32))

        planes = [rim(far, near, n) for n in range(2)]
        planes += [acts[m, n] for n in range(depth)]
        planes += [rim(near, far, n) for n in range(2)]
        for n, plane in enumerate(planes):
            write_shifts(plane, height, shifts.at[m], n * cells)
        preact = None
        for dz in range(3):
            term = jnp.dot(
                shifts[m, dz * cells : dz * cells + rows + 2 * cells, :],
                weight[dz * span : (dz + 1) * span, :],
                preferred_element_type=F32,
            )
            preact = term if preact is None else preact + term
        sig = 1.0 / (1.0 + jnp.exp(-preact))
        slope = sig * (1.0 + preact * (1.0 - sig))
        slopes[m] = slope
        ups = [rim(far, near, 2)] + [grad[m, n].astype(F32) for n in range(depth)]
        ups.append(rim(near, far, 2))
        for n, up in enumerate(ups):
            delta = (up * slope[n * cells : (n + 1) * cells]).astype(BF16)
            write_shifts(delta, height, deltas.at[m], n * cells)
        back = back_product(deltas.at[m], weight, rows, cells)
        total = grad[m].reshape(rows, channels).astype(F32) + back
        result[m] = total.astype(BF16).reshape(depth, cells, channels)
        low, high = total[:cells], total[-cells:]
        to_near[m, 0] = jnp.where(even, high, low).astype(BF16)
        to_far[m, 0] = jnp.where(even, low, high).astype(BF16)


def shift_kernel(height, acts, near, far, after, shifts):
    micro, depth, cells, _ = acts.shape
    even = lax.rem(lax.axis_index("slab"), 2) == 0
    for m in range(micro):
        below = jnp.where(even, far[m, 1].astype(F32), near[m, 1].astype(F32))
        above = jnp.where(even, near[m, 0].astype(F32), far[m, 0].astype(F32))
        planes = [below] + [acts[m, n] for n in range(depth)] + [above]
        for n, plane in enumerate(planes):
            write_shifts(plane, height, shifts.at[m], n * cells)


def raw_kernel(
    spot, incoming, in_near, in_far, grad, near, far, slopes, shifts, upstream, deltas, *refs
):
    sends, (keep, raw) = refs[:4], refs[4:]
    micro, depth, cells, channels = upstream.shape
    rows = depth * cells
    span = 9 * channels
    last = lax.axis_index("segment") == lax.axis_size("segment") - 1
    even = lax.rem(lax.axis_index("slab"), 2) == 0
    deltas_of = []
    for m in range(micro):
        up = jnp.where(last, grad[m].astype(F32), incoming[m].astype(F32))
        upstream[m] = up.astype(BF16)
        by_near = jnp.where(last, near[m, 2].astype(F32), in_near[m, 0].astype(F32))
        by_far = jnp.where(last, far[m, 2].astype(F32), in_far[m, 0].astype(F32))
        below, above = jnp.where(even, by_far, by_near), jnp.where(even, by_near, by_far)
        delta = (up.reshape(rows, channels) * slopes[m, cells : cells + rows]).astype(BF16)
        deltas[m, :cells] = (below * slopes[m, :cells]).astype(BF16)
        deltas[m, cells : cells + rows] = delta
        deltas[m, cells + rows :] = (above * slopes[m, cells + rows :]).astype(BF16)
        deltas_of.append(delta)
    for dz in range(3):
        total = None
        for m in range(micro):
            term = lax.dot_general(
                shifts[m, dz * cells : dz * cells + rows, :],
                deltas_of[m],
                (((0,), (0,)), ((), ())),
                preferred_element_type=F32,
            )
            total = term if total is None else total + term
        raw[dz * span : (dz + 1) * span, :] = total
    part = keep.shape[1]
    for turn in range(4):
        keep[turn] = raw[pl.ds((spot[0] ^ turn) * part, part), :]
        sends[turn][...] = raw[pl.ds((spot[0] ^ turn ^ 4) * part, part), :].astype(BF16)


def add_kernel(turn, keep, got, out):
    out[...] = (keep[turn] + got[...].astype(F32)).astype(BF16)


def sum_kernel(keep, *refs):
    total = keep[0]
    for got in refs[:-1]:
        total = total + got[...].astype(F32)
    refs[-1][...] = total


def column_squares(value):
    value = value.astype(F32)
    return jnp.sum(value * value, axis=0, keepdims=True)


def chunk_kernel(keep, *refs):
    total = keep[...]
    for got in refs[:-2]:
        total = total + got[...].astype(F32)
    chunk, squares = refs[-2:]
    chunk[...] = total.astype(BF16)
    squares[...] = jnp.broadcast_to(column_squares(chunk[...]), squares.shape)


def payload_kernel(count, gathered, *refs):
    own, values, out = refs[:count], refs[count:-1], refs[-1]
    sums = [column_squares(piece[...]) for piece in own]
    for n, value in enumerate(values):
        sums[n % count] = sums[n % count] + value[:1, :]
    while len(sums) > 1:
        sums = [a + b for a, b in zip(sums[::2], sums[1::2], strict=True)]
    rows = gathered.shape[0]
    out[:rows] = gathered[...]
    high = sums[0].astype(BF16).astype(F32)
    middle = (sums[0] - high).astype(BF16).astype(F32)
    low = sums[0] - high - middle
    at = lax.broadcasted_iota(jnp.int32, (16, gathered.shape[1]), 0)
    terms = jnp.where(at == 0, high, jnp.where(at == 1, middle, jnp.where(at == 2, low, 0.0)))
    out[rows:] = terms.astype(BF16)


def back_kernel(height, deltas, upstream, weight, out, shifts):
    micro, depth, cells, channels = upstream.shape
    rows = depth * cells
    for m in range(micro):
        for n in range(depth + 2):
            plane = deltas[m, n * cells : (n + 1) * cells, :]
            write_shifts(plane, height, shifts.at[m], n * cells)
        back = back_product(shifts.at[m], weight, rows, cells)
        total = upstream[m].reshape(rows, channels).astype(F32) + back
        out[m] = total.astype(BF16).reshape(depth, cells, channels)


def place_kernel(bound, spot, *refs):
    pieces, (out, scaled, sems) = refs[:-3], refs[-3:]
    rows = scaled.shape[1]
    sums = [piece[rows:].astype(F32) for piece in pieces]
    while len(sums) > 1:
        sums = [a + b for a, b in zip(sums[::2], sums[1::2], strict=True)]
    norm = jnp.sqrt(jnp.sum(jnp.sum(sums[0], axis=0, keepdims=True), axis=1, keepdims=True))
    factor = jnp.minimum(1.0, bound / (norm + 1e-06))
    copies = []
    for n, piece in enumerate(pieces):
        scaled[n] = piece[:rows].astype(F32) * factor
        copies.append(pltpu.make_async_copy(scaled.at[n], out.at[spot[0] ^ n], sems.at[n]))
        copies[-1].start()
    for copy in copies:
        copy.wait()


def shards(activations, weights, out_grad):
    weight = weights[0]
    channels = weight.shape[1]
    micro, depth, width, height = activations.shape[1:5]
    cells = width * height
    acts = activations[0].reshape(micro, depth, cells, channels)
    grad = out_grad.reshape(micro, depth, cells, channels)
    rows = depth * cells
    segments = lax.axis_size("segment")
    count = lax.axis_size("slab")
    index = lax.axis_index("slab")
    last = lax.axis_index("segment") == segments - 1
    large = pltpu.CompilerParams(vmem_limit_bytes=16 << 20)
    small = pltpu.CompilerParams(vmem_limit_bytes=4 << 20)

    shape = jax.ShapeDtypeStruct
    rim = shape((micro, 3, cells, channels), BF16)
    volume = shape((micro, depth, cells, channels), BF16)
    to_near, to_far, acts, grad, weight = pl.pallas_call(
        rim_kernel,
        out_shape=(rim, rim, volume, volume, shape(weight.shape, BF16)),
        in_specs=[HBM, HBM, HBM],
        out_specs=(VMEM,) * 5,
        scratch_shapes=[pltpu.SemaphoreType.DMA((2, micro, 2)), pltpu.SemaphoreType.DMA((3,))],
        compiler_params=small,
    )(*(pltpu.with_memory_space_constraint(a, pltpu.HBM) for a in (acts, grad, weight)))
    near, far = swap(to_near, to_far)

    edge = shape((micro, 1, cells, channels), BF16)
    wide = pltpu.VMEM((micro, rows + 2 * cells, 9 * channels), BF16)
    result, to_near, to_far, slopes = pl.pallas_call(
        functools.partial(first_kernel, height),
        out_shape=(volume, edge, edge, shape((micro, rows + 2 * cells, channels), F32)),
        in_specs=[VMEM] * 5,
        out_specs=(VMEM,) * 4,
        scratch_shapes=[pltpu.VMEM((micro, rows + 4 * cells, 9 * channels), BF16), wide],
        compiler_params=large,
    )(acts, near, far, grad, weight)

    def conv_back(deltas, upstream):
        return pl.pallas_call(
            functools.partial(back_kernel, height),
            out_shape=volume,
            in_specs=[VMEM] * 3,
            out_specs=VMEM,
            scratch_shapes=[wide],
            compiler_params=large,
        )(deltas, upstream, weight)

    even = lax.rem(index, 2) == 0
    for step in range(1, segments - 1):
        incoming, in_near, in_far = cross(result, 1, 0), cross(to_near, 1, 1), cross_far(to_far)
        upstream = jnp.where(last, grad, incoming)
        by_near = jnp.where(last, near[:, 2:], in_near)
        by_far = jnp.where(last, far[:, 2:], in_far)
        below, above = jnp.where(even, by_far, by_near), jnp.where(even, by_near, by_far)
        around = jnp.concatenate([below, upstream, above], axis=1)
        around = around.reshape(slopes.shape).astype(F32)
        result = conv_back((around * slopes).astype(BF16), upstream)
        low, high = result[:, :1], result[:, -1:]
        to_near, to_far = jnp.where(even, high, low), jnp.where(even, low, high)
    incoming, in_near, in_far = cross(result, 1, 0), cross(to_near, 1, 1), cross_far(to_far)
    shifts = pl.pallas_call(
        functools.partial(shift_kernel, height),
        out_shape=shape((micro, rows + 2 * cells, 9 * channels), BF16),
        in_specs=[VMEM] * 4,
        out_specs=VMEM,
        compiler_params=large,
    )(acts, near, far, result)

    bits = [1 << n for n in range(1, count.bit_length() - 1)]
    inner = [bits[n : n + 2] for n in range(2, len(bits), 2)]
    crossing = inner[-1][0] if len(inner[-1]) == 1 else 0
    side = lax.rem(index, 2) ^ jnp.where(index & crossing, 1, 0)
    quarter = jnp.where(index & 2, 2, 0) + jnp.where(index & 4, 1, 0)
    masks = {1: 4, 2: 2, 3: 6}
    spot = (side * 4 + quarter).astype(jnp.int32).reshape(1)
    part = weight.shape[0] // 8
    piece = shape((part, channels), BF16)

    upstream, deltas, *rest = pl.pallas_call(
        raw_kernel,
        out_shape=(volume, shape(slopes.shape, BF16))
        + (piece,) * 4
        + (shape((4, part, channels), F32),),
        in_specs=[SMEM] + [VMEM] * 8,
        out_specs=(VMEM,) * 7,
        scratch_shapes=[pltpu.VMEM((8 * part, channels), F32)],
        compiler_params=large,
    )(spot, incoming, in_near, in_far, grad, near, far, slopes, shifts)
    sends, keep = rest[:4], rest[4]
    got = {turn: exchange(sends[turn], 1) for turn in (3, 2, 1, 0)}
    across = []
    for turn in (3, 2, 1):
        added = pl.pallas_call(
            functools.partial(add_kernel, turn),
            out_shape=piece,
            in_specs=[VMEM] * 2,
            out_specs=VMEM,
            compiler_params=small,
        )(keep, got[turn])
        across.append(exchange(added, masks[turn]))
    gradients = conv_back(deltas, upstream)
    across[1], gradients = lax.optimization_barrier((across[1], gradients))
    chunk = pl.pallas_call(
        sum_kernel,
        out_shape=shape((part, channels), F32),
        in_specs=[VMEM] * 5,
        out_specs=VMEM,
        compiler_params=small,
    )(keep, got[0], *across)

    def places(group):
        own = sum(jnp.where(index & bit, 1 << n, 0) for n, bit in enumerate(group))
        others = []
        for turn in range(1, 1 << len(group)):
            mask = sum(bit for n, bit in enumerate(group) if turn >> n & 1)
            others.append((mask | 1 if mask == crossing else mask, own ^ turn))
        return own, others

    for group in inner:
        own, others = places(group)
        size = chunk.shape[0] >> len(group)
        got = [exchange(block(chunk, there, size, BF16), mask) for mask, there in others]
        chunk = block(chunk, own, size, F32)
        if group is not inner[-1]:
            chunk = chunk + sum(g.astype(F32) for g in got)
    gathered, squares = pl.pallas_call(
        chunk_kernel,
        out_shape=(shape(chunk.shape, BF16), shape((8, channels), F32)),
        in_specs=[VMEM] * (1 + len(got)),
        out_specs=(VMEM, VMEM),
        compiler_params=small,
    )(chunk, *got)

    for group in reversed(inner):
        own, others = places(group)
        got = [(there, exchange(gathered, mask)) for mask, there in others]
        if group is inner[-1]:
            members = [gathered] + [other for _, other in got]
            met = [
                cross(squares, back, mask)
                for back in range(1, segments)
                for mask in [0] + [mask for mask, _ in others]
            ]
        blocks = []
        for n in range(1 << len(group)):
            value = jnp.where(own == n, gathered, got[0][1])
            for there, other in got[1:]:
                value = jnp.where(there == n, other, value)
            blocks.append(value)
        gathered = jnp.concatenate(blocks, axis=0)
    payload = pl.pallas_call(
        functools.partial(payload_kernel, len(members)),
        out_shape=shape((part + 16, channels), BF16),
        in_specs=[VMEM] * (1 + len(members) + len(met)),
        out_specs=VMEM,
        compiler_params=small,
    )(gathered, *members, *met)
    pieces = {turn: exchange(payload, masks[turn]) for turn in (3, 2, 1)}
    ours = [payload] + [pieces[turn] for turn in (1, 2, 3)]
    both = ours + [exchange(piece, 1) for piece in ours]
    bound = math.sqrt(27.0 * channels * channels * segments)
    update = pl.pallas_call(
        functools.partial(place_kernel, bound),
        out_shape=jax.ShapeDtypeStruct((8, part, channels), F32),
        in_specs=[SMEM] + [VMEM] * 8,
        out_specs=ANY,
        scratch_shapes=[pltpu.VMEM((8, part, channels), F32), pltpu.SemaphoreType.DMA((8,))],
        compiler_params=large,
    )((side * 4 + quarter).astype(jnp.int32).reshape(1), *both)
    gradients = gradients.reshape(1, micro, depth, width, height, channels)
    return (update.reshape(1, 8 * part, channels), gradients)


def solution(mesh):
    return jax.shard_map(
        shards,
        mesh=mesh,
        in_specs=(
            P("segment", None, "slab", None, None, None),
            P("segment", None, None),
            P(None, "slab", None, None, None),
        ),
        out_specs=(P("segment", None, None), P("segment", None, "slab", None, None, None)),
        check_vma=False,
    )
```

```python
import functools
import math

import jax
import jax.numpy as jnp
from jax import lax
from jax.experimental import pallas as pl
from jax.experimental.pallas import tpu as pltpu
from jax.sharding import PartitionSpec as P

BF16 = jnp.bfloat16
F32 = jnp.float32
VMEM = pl.BlockSpec(memory_space=pltpu.VMEM)
SMEM = pl.BlockSpec(memory_space=pltpu.SMEM)
ANY = pl.BlockSpec(memory_space=pl.ANY)
HBM = pl.BlockSpec(memory_space=pltpu.HBM)


def far_route(count):
    return [(i, ((i + 1) ^ 1) - 1) for i in range(1, count - 1)]


def swap(to_near, to_far):
    count = lax.axis_size("slab")
    near = [(i, i ^ 1) for i in range(count)]
    return lax.ppermute(to_near, "slab", near), lax.ppermute(to_far, "slab", far_route(count))


def cross_far(value):
    segments, count = lax.axis_size("segment"), lax.axis_size("slab")
    route = [
        (s * count + i, (s - 1) % segments * count + j)
        for s in range(segments)
        for i, j in far_route(count)
    ]
    return lax.ppermute(value, ("segment", "slab"), route)


def exchange(value, mask):
    count = lax.axis_size("slab")
    return lax.ppermute(value, "slab", [(i, i ^ mask) for i in range(count)])


def cross(value, back, mask):
    segments, count = lax.axis_size("segment"), lax.axis_size("slab")
    if back == 0 and mask == 0:
        return value
    route = [
        (s * count + i, (s - back) % segments * count + (i ^ mask))
        for s in range(segments)
        for i in range(count)
    ]
    return lax.ppermute(value, ("segment", "slab"), route)


def block(value, place, rows, dtype):
    return lax.dynamic_slice_in_dim(value, place * rows, rows, 0).astype(dtype)


def write_shifts(plane, height, out_ref, first):
    cells, channels = plane.shape
    width = cells // height
    rows = plane.astype(F32).reshape(width, height, channels)
    at = lax.broadcasted_iota(jnp.int32, rows.shape, 1)
    zero = jnp.zeros((1, height, channels), F32)
    before = jnp.where(at == 0, 0.0, pltpu.roll(rows, 1, 1))
    after = jnp.where(at == height - 1, 0.0, pltpu.roll(rows, height - 1, 1))
    for dy, moved in enumerate((before, rows, after)):
        for dx in range(3):
            if dx == 0:
                value = jnp.concatenate([zero, moved[:-1]], axis=0)
            elif dx == 1:
                value = moved
            else:
                value = jnp.concatenate([moved[1:], zero], axis=0)
            j = dx * 3 + dy
            out_ref[first : first + cells, j * channels : (j + 1) * channels] = value.reshape(
                cells, channels
            ).astype(BF16)


def back_product(shifts, weight_ref, rows, cells):
    channels = weight_ref.shape[1]
    total = None
    for dz in range(3):
        mirrored = [26 - 9 * dz - j for j in range(9)]
        side = jnp.concatenate(
            [weight_ref[k * channels : (k + 1) * channels, :] for k in mirrored], axis=1
        )
        term = lax.dot_general(
            shifts[dz * cells : dz * cells + rows, :],
            side,
            (((1,), (1,)), ((), ())),
            preferred_element_type=F32,
        )
        total = term if total is None else total + term
    return total


def rim_kernel(acts, grad, weight, near, far, acts_here, grad_here, weight_here, sems, loads):
    micro, depth = acts.shape[:2]
    top = 1 - lax.rem(lax.axis_index("slab"), 2)
    copies = []
    for which, (out, high) in enumerate(((near, top), (far, 1 - top))):
        for m in range(micro):
            for part, (source, size, at) in enumerate(((acts, 2, 0), (grad, 1, 2))):
                copies.append(
                    pltpu.make_async_copy(
                        source.at[m, pl.ds(high * (depth - size), size)],
                        out.at[m, at : at + size],
                        sems.at[which, m, part],
                    )
                )
    for n, (source, out) in enumerate(
        ((acts, acts_here), (grad, grad_here), (weight, weight_here))
    ):
        copies.append(pltpu.make_async_copy(source, out, loads.at[n]))
    for copy in copies:
        copy.start()
    for copy in copies:
        copy.wait()


def first_kernel(
    height, acts, near, far, grad, weight, result, to_near, to_far, slopes, shifts, deltas
):
    micro, depth, cells, channels = acts.shape
    even = lax.rem(lax.axis_index("slab"), 2) == 0
    span = 9 * channels
    rows = depth * cells
    for m in range(micro):

        def rim(a, b, n):
            return jnp.where(even, a[m, n].astype(F32), b[m, n].astype(F32))

        planes = [rim(far, near, n) for n in range(2)]
        planes += [acts[m, n] for n in range(depth)]
        planes += [rim(near, far, n) for n in range(2)]
        for n, plane in enumerate(planes):
            write_shifts(plane, height, shifts.at[m], n * cells)
        preact = None
        for dz in range(3):
            term = jnp.dot(
                shifts[m, dz * cells : dz * cells + rows + 2 * cells, :],
                weight[dz * span : (dz + 1) * span, :],
                preferred_element_type=F32,
            )
            preact = term if preact is None else preact + term
        sig = 1.0 / (1.0 + jnp.exp(-preact))
        slope = sig * (1.0 + preact * (1.0 - sig))
        slopes[m] = slope
        ups = [rim(far, near, 2)] + [grad[m, n].astype(F32) for n in range(depth)]
        ups.append(rim(near, far, 2))
        for n, up in enumerate(ups):
            delta = (up * slope[n * cells : (n + 1) * cells]).astype(BF16)
            write_shifts(delta, height, deltas.at[m], n * cells)
        back = back_product(deltas.at[m], weight, rows, cells)
        total = grad[m].reshape(rows, channels).astype(F32) + back
        result[m] = total.astype(BF16).reshape(depth, cells, channels)
        low, high = total[:cells], total[-cells:]
        to_near[m, 0] = jnp.where(even, high, low).astype(BF16)
        to_far[m, 0] = jnp.where(even, low, high).astype(BF16)


def shift_kernel(height, acts, near, far, after, shifts):
    micro, depth, cells, _ = acts.shape
    even = lax.rem(lax.axis_index("slab"), 2) == 0
    for m in range(micro):
        below = jnp.where(even, far[m, 1].astype(F32), near[m, 1].astype(F32))
        above = jnp.where(even, near[m, 0].astype(F32), far[m, 0].astype(F32))
        planes = [below] + [acts[m, n] for n in range(depth)] + [above]
        for n, plane in enumerate(planes):
            write_shifts(plane, height, shifts.at[m], n * cells)


def raw_kernel(
    spot, incoming, in_near, in_far, grad, near, far, slopes, shifts, upstream, deltas, *refs
):
    sends, (keep, raw) = refs[:4], refs[4:]
    micro, depth, cells, channels = upstream.shape
    rows = depth * cells
    span = 9 * channels
    last = lax.axis_index("segment") == lax.axis_size("segment") - 1
    even = lax.rem(lax.axis_index("slab"), 2) == 0
    deltas_of = []
    for m in range(micro):
        up = jnp.where(last, grad[m].astype(F32), incoming[m].astype(F32))
        upstream[m] = up.astype(BF16)
        by_near = jnp.where(last, near[m, 2].astype(F32), in_near[m, 0].astype(F32))
        by_far = jnp.where(last, far[m, 2].astype(F32), in_far[m, 0].astype(F32))
        below, above = jnp.where(even, by_far, by_near), jnp.where(even, by_near, by_far)
        delta = (up.reshape(rows, channels) * slopes[m, cells : cells + rows]).astype(BF16)
        deltas[m, :cells] = (below * slopes[m, :cells]).astype(BF16)
        deltas[m, cells : cells + rows] = delta
        deltas[m, cells + rows :] = (above * slopes[m, cells + rows :]).astype(BF16)
        deltas_of.append(delta)
    for dz in range(3):
        total = None
        for m in range(micro):
            term = lax.dot_general(
                shifts[m, dz * cells : dz * cells + rows, :],
                deltas_of[m],
                (((0,), (0,)), ((), ())),
                preferred_element_type=F32,
            )
            total = term if total is None else total + term
        raw[dz * span : (dz + 1) * span, :] = total
    part = keep.shape[1]
    for turn in range(4):
        keep[turn] = raw[pl.ds((spot[0] ^ turn) * part, part), :]
        sends[turn][...] = raw[pl.ds((spot[0] ^ turn ^ 4) * part, part), :].astype(BF16)


def add_kernel(turn, keep, got, out):
    out[...] = (keep[turn] + got[...].astype(F32)).astype(BF16)


def sum_kernel(keep, *refs):
    total = keep[0]
    for got in refs[:-1]:
        total = total + got[...].astype(F32)
    refs[-1][...] = total.astype(refs[-1].dtype)


def both_kernel(mine, other, out):
    out[...] = (mine[...].astype(F32) + other[...].astype(F32)).astype(BF16)


def column_squares(value):
    value = value.astype(F32)
    return jnp.sum(value * value, axis=0, keepdims=True)


def norm_kernel(*refs):
    sums = [column_squares(piece[...]) for piece in refs[:-1]]
    while len(sums) > 1:
        sums = [a + b for a, b in zip(sums[::2], sums[1::2], strict=True)]
    refs[-1][...] = jnp.broadcast_to(sums[0], refs[-1].shape)


def back_kernel(height, deltas, upstream, weight, out, shifts):
    micro, depth, cells, channels = upstream.shape
    rows = depth * cells
    for m in range(micro):
        for n in range(depth + 2):
            plane = deltas[m, n * cells : (n + 1) * cells, :]
            write_shifts(plane, height, shifts.at[m], n * cells)
        back = back_product(shifts.at[m], weight, rows, cells)
        total = upstream[m].reshape(rows, channels).astype(F32) + back
        out[m] = total.astype(BF16).reshape(depth, cells, channels)


def place_kernel(bound, count, spot, *refs):
    sums, pieces, (out, scaled, sems) = refs[: 2 * count], refs[2 * count : -3], refs[-3:]
    mine, other = (sum(value[:1, :] for value in sums[side::2]) for side in range(2))
    squares = mine + other
    norm = jnp.sqrt(jnp.sum(squares, axis=1, keepdims=True))
    factor = jnp.minimum(1.0, bound / (norm + 1e-06))
    copies = []
    for n, piece in enumerate(pieces):
        scaled[n] = piece[...].astype(F32) * factor
        copies.append(pltpu.make_async_copy(scaled.at[n], out.at[spot[0] ^ n], sems.at[n]))
        copies[-1].start()
    for copy in copies:
        copy.wait()


def shards(activations, weights, out_grad):
    weight = weights[0]
    channels = weight.shape[1]
    micro, depth, width, height = activations.shape[1:5]
    cells = width * height
    acts = activations[0].reshape(micro, depth, cells, channels)
    grad = out_grad.reshape(micro, depth, cells, channels)
    rows = depth * cells
    segments = lax.axis_size("segment")
    count = lax.axis_size("slab")
    index = lax.axis_index("slab")
    last = lax.axis_index("segment") == segments - 1
    large = pltpu.CompilerParams(vmem_limit_bytes=16 << 20)
    small = pltpu.CompilerParams(vmem_limit_bytes=4 << 20)

    shape = jax.ShapeDtypeStruct
    rim = shape((micro, 3, cells, channels), BF16)
    volume = shape((micro, depth, cells, channels), BF16)
    to_near, to_far, acts, grad, weight = pl.pallas_call(
        rim_kernel,
        out_shape=(rim, rim, volume, volume, shape(weight.shape, BF16)),
        in_specs=[HBM, HBM, HBM],
        out_specs=(VMEM,) * 5,
        scratch_shapes=[pltpu.SemaphoreType.DMA((2, micro, 2)), pltpu.SemaphoreType.DMA((3,))],
        compiler_params=small,
    )(*(pltpu.with_memory_space_constraint(a, pltpu.HBM) for a in (acts, grad, weight)))
    near, far = swap(to_near, to_far)

    edge = shape((micro, 1, cells, channels), BF16)
    wide = pltpu.VMEM((micro, rows + 2 * cells, 9 * channels), BF16)
    result, to_near, to_far, slopes = pl.pallas_call(
        functools.partial(first_kernel, height),
        out_shape=(volume, edge, edge, shape((micro, rows + 2 * cells, channels), F32)),
        in_specs=[VMEM] * 5,
        out_specs=(VMEM,) * 4,
        scratch_shapes=[pltpu.VMEM((micro, rows + 4 * cells, 9 * channels), BF16), wide],
        compiler_params=large,
    )(acts, near, far, grad, weight)

    def conv_back(deltas, upstream):
        return pl.pallas_call(
            functools.partial(back_kernel, height),
            out_shape=volume,
            in_specs=[VMEM] * 3,
            out_specs=VMEM,
            scratch_shapes=[wide],
            compiler_params=large,
        )(deltas, upstream, weight)

    even = lax.rem(index, 2) == 0
    for step in range(1, segments - 1):
        incoming, in_near, in_far = cross(result, 1, 0), cross(to_near, 1, 1), cross_far(to_far)
        upstream = jnp.where(last, grad, incoming)
        by_near = jnp.where(last, near[:, 2:], in_near)
        by_far = jnp.where(last, far[:, 2:], in_far)
        below, above = jnp.where(even, by_far, by_near), jnp.where(even, by_near, by_far)
        around = jnp.concatenate([below, upstream, above], axis=1)
        around = around.reshape(slopes.shape).astype(F32)
        result = conv_back((around * slopes).astype(BF16), upstream)
        low, high = result[:, :1], result[:, -1:]
        to_near, to_far = jnp.where(even, high, low), jnp.where(even, low, high)
    incoming, in_near, in_far = cross(result, 1, 0), cross(to_near, 1, 1), cross_far(to_far)
    shifts = pl.pallas_call(
        functools.partial(shift_kernel, height),
        out_shape=shape((micro, rows + 2 * cells, 9 * channels), BF16),
        in_specs=[VMEM] * 4,
        out_specs=VMEM,
        compiler_params=large,
    )(acts, near, far, result)

    bits = [1 << n for n in range(1, count.bit_length() - 1)]
    inner = [bits[n : n + 2] for n in range(2, len(bits), 2)]
    crossing = inner[-1][0] if len(inner[-1]) == 1 else 0
    side = lax.rem(index, 2) ^ jnp.where(index & crossing, 1, 0)
    quarter = jnp.where(index & 2, 2, 0) + jnp.where(index & 4, 1, 0)
    masks = {1: 4, 2: 2, 3: 6}
    spot = (side * 4 + quarter).astype(jnp.int32).reshape(1)
    part = weight.shape[0] // 8
    piece = shape((part, channels), BF16)

    upstream, deltas, *rest = pl.pallas_call(
        raw_kernel,
        out_shape=(volume, shape(slopes.shape, BF16))
        + (piece,) * 4
        + (shape((4, part, channels), F32),),
        in_specs=[SMEM] + [VMEM] * 8,
        out_specs=(VMEM,) * 7,
        scratch_shapes=[pltpu.VMEM((8 * part, channels), F32)],
        compiler_params=large,
    )(spot, incoming, in_near, in_far, grad, near, far, slopes, shifts)
    sends, keep = rest[:4], rest[4]
    got = {turn: exchange(sends[turn], 1) for turn in (3, 2, 1, 0)}
    across = []
    for turn in (3, 2, 1):
        added = pl.pallas_call(
            functools.partial(add_kernel, turn),
            out_shape=piece,
            in_specs=[VMEM] * 2,
            out_specs=VMEM,
            compiler_params=small,
        )(keep, got[turn])
        across.append(exchange(added, masks[turn]))
    gradients = conv_back(deltas, upstream)
    across[1], gradients = lax.optimization_barrier((across[1], gradients))
    single = len(inner[-1]) == 1
    direct = single and len(inner) == 1
    chunk = pl.pallas_call(
        sum_kernel,
        out_shape=shape((part, channels), BF16 if direct else F32),
        in_specs=[VMEM] * 5,
        out_specs=VMEM,
        compiler_params=small,
    )(keep, got[0], *across)

    def places(group):
        own = sum(jnp.where(index & bit, 1 << n, 0) for n, bit in enumerate(group))
        others = []
        for turn in range(1, 1 << len(group)):
            others.append((sum(bit for n, bit in enumerate(group) if turn >> n & 1), own ^ turn))
        return own, others

    paired = inner[:-1] if single else inner
    for group in paired:
        own, others = places(group)
        size = chunk.shape[0] >> len(group)
        took = [exchange(block(chunk, there, size, BF16), mask) for mask, there in others]
        chunk = block(chunk, own, size, F32) + sum(g.astype(F32) for g in took)
    gathered = chunk.astype(BF16)
    if single:
        gathered = pl.pallas_call(
            both_kernel,
            out_shape=shape(gathered.shape, BF16),
            in_specs=[VMEM] * 2,
            out_specs=VMEM,
            compiler_params=small,
        )(gathered, exchange(gathered, crossing | 1))

    for group in reversed(paired):
        own, others = places(group)
        took = [(there, exchange(gathered, mask)) for mask, there in others]
        blocks = []
        for n in range(1 << len(group)):
            value = jnp.where(own == n, gathered, took[0][1])
            for there, other in took[1:]:
                value = jnp.where(there == n, other, value)
            blocks.append(value)
        gathered = jnp.concatenate(blocks, axis=0)
    pieces = {turn: exchange(gathered, masks[turn]) for turn in (3, 2, 1)}
    ours = [gathered] + [pieces[turn] for turn in (1, 2, 3)]
    theirs = [exchange(piece, 1) for piece in ours]
    sums = [
        pl.pallas_call(
            norm_kernel,
            out_shape=shape((8, channels), F32),
            in_specs=[VMEM] * 4,
            out_specs=VMEM,
            compiler_params=small,
        )(*four)
        for four in (ours, theirs)
    ]
    sums += [cross(sums[0], back, mask) for back in range(1, segments) for mask in (0, 1)]
    bound = math.sqrt(27.0 * channels * channels * segments)
    update = pl.pallas_call(
        functools.partial(place_kernel, bound, segments),
        out_shape=jax.ShapeDtypeStruct((8, part, channels), F32),
        in_specs=[SMEM] + [VMEM] * (2 * segments + 8),
        out_specs=ANY,
        scratch_shapes=[pltpu.VMEM((8, part, channels), F32), pltpu.SemaphoreType.DMA((8,))],
        compiler_params=large,
    )((side * 4 + quarter).astype(jnp.int32).reshape(1), *sums, *ours, *theirs)
    gradients = gradients.reshape(1, micro, depth, width, height, channels)
    return (update.reshape(1, 8 * part, channels), gradients)


def solution(mesh):
    return jax.shard_map(
        shards,
        mesh=mesh,
        in_specs=(
            P("segment", None, "slab", None, None, None),
            P("segment", None, None),
            P(None, "slab", None, None, None),
        ),
        out_specs=(P("segment", None, None), P("segment", None, "slab", None, None, None)),
        check_vma=False,
    )
```

```python
import functools
import math

import jax
import jax.numpy as jnp
from jax import lax
from jax.experimental import pallas as pl
from jax.experimental.pallas import tpu as pltpu
from jax.sharding import PartitionSpec as P

BF16 = jnp.bfloat16
F32 = jnp.float32
VMEM = pl.BlockSpec(memory_space=pltpu.VMEM)
SMEM = pl.BlockSpec(memory_space=pltpu.SMEM)
ANY = pl.BlockSpec(memory_space=pl.ANY)
HBM = pl.BlockSpec(memory_space=pltpu.HBM)


def far_route(count):
    return [(i, ((i + 1) ^ 1) - 1) for i in range(1, count - 1)]


def swap(to_near, to_far):
    count = lax.axis_size("slab")
    near = [(i, i ^ 1) for i in range(count)]
    return lax.ppermute(to_near, "slab", near), lax.ppermute(to_far, "slab", far_route(count))


def cross_far(value):
    segments, count = lax.axis_size("segment"), lax.axis_size("slab")
    route = [
        (s * count + i, (s - 1) % segments * count + j)
        for s in range(segments)
        for i, j in far_route(count)
    ]
    return lax.ppermute(value, ("segment", "slab"), route)


def exchange(value, mask):
    count = lax.axis_size("slab")
    return lax.ppermute(value, "slab", [(i, i ^ mask) for i in range(count)])


def cross(value, back, mask):
    segments, count = lax.axis_size("segment"), lax.axis_size("slab")
    if back == 0 and mask == 0:
        return value
    route = [
        (s * count + i, (s - back) % segments * count + (i ^ mask))
        for s in range(segments)
        for i in range(count)
    ]
    return lax.ppermute(value, ("segment", "slab"), route)


def block(value, place, rows, dtype):
    return lax.dynamic_slice_in_dim(value, place * rows, rows, 0).astype(dtype)


def write_shifts(plane, height, out_ref, first):
    cells, channels = plane.shape
    width = cells // height
    rows = plane.astype(F32).reshape(width, height, channels)
    at = lax.broadcasted_iota(jnp.int32, rows.shape, 1)
    zero = jnp.zeros((1, height, channels), F32)
    before = jnp.where(at == 0, 0.0, pltpu.roll(rows, 1, 1))
    after = jnp.where(at == height - 1, 0.0, pltpu.roll(rows, height - 1, 1))
    for dy, moved in enumerate((before, rows, after)):
        for dx in range(3):
            if dx == 0:
                value = jnp.concatenate([zero, moved[:-1]], axis=0)
            elif dx == 1:
                value = moved
            else:
                value = jnp.concatenate([moved[1:], zero], axis=0)
            j = dx * 3 + dy
            out_ref[first : first + cells, j * channels : (j + 1) * channels] = value.reshape(
                cells, channels
            ).astype(BF16)


def back_product(shifts, mirror, block, depth):
    span = shifts.shape[1]
    total = None
    for dz in range(3):
        term = jnp.dot(
            shifts[dz * block : (dz + depth) * block, :],
            mirror[dz * span : (dz + 1) * span, :],
            preferred_element_type=F32,
        )
        total = term if total is None else total + term
    return total


def rim_kernel(acts, grad, near, far, acts_here, grad_here, sems, loads):
    micro, depth = acts.shape[:2]
    top = 1 - lax.rem(lax.axis_index("slab"), 2)
    copies = []
    for which, (out, high) in enumerate(((near, top), (far, 1 - top))):
        for m in range(micro):
            for part, (source, size, at) in enumerate(((acts, 2, 0), (grad, 1, 2))):
                copies.append(
                    pltpu.make_async_copy(
                        source.at[m, pl.ds(high * (depth - size), size)],
                        out.at[m, at : at + size],
                        sems.at[which, m, part],
                    )
                )
    for n, (source, out) in enumerate(((acts, acts_here), (grad, grad_here))):
        copies.append(pltpu.make_async_copy(source, out, loads.at[n]))
    for copy in copies:
        copy.start()
    for copy in copies:
        copy.wait()


def own_kernel(height, acts, stored, weight, mirror, part, own, sem):
    micro, depth, cells, channels = acts.shape
    block, span = micro * cells, 9 * channels
    copy = pltpu.make_async_copy(stored, weight, sem)
    copy.start()
    for n in range(depth):
        for m in range(micro):
            write_shifts(acts[m, n], height, own, n * block + m * cells)
    copy.wait()
    part[...] = jnp.zeros(part.shape, F32)
    for dz in range(3):
        rows = slice((2 - dz) * block, (2 - dz + depth) * block)
        part[rows, :] += jnp.dot(
            own[...], weight[dz * span : (dz + 1) * span, :], preferred_element_type=F32
        )
    for k in range(27):
        mirror[(26 - k) * channels : (27 - k) * channels, :] = weight[
            k * channels : (k + 1) * channels, :
        ].T


def first_kernel(
    height, near, far, grad, weight, mirror, part, result, to_near, to_far, slopes, rim, shifts
):
    micro, depth, cells, channels = grad.shape
    even = lax.rem(lax.axis_index("slab"), 2) == 0
    block, span = micro * cells, 9 * channels

    def pick(m, n, below):
        a, b = near[m, n].astype(F32), far[m, n].astype(F32)
        return jnp.where(even, b, a) if below else jnp.where(even, a, b)

    for n in range(4):
        for m in range(micro):
            write_shifts(pick(m, n % 2, n < 2), height, rim, n * block + m * cells)
    terms = [
        jnp.dot(
            rim[dz * block : (dz + 2) * block, :],
            weight[dz * span : (dz + 1) * span, :],
            preferred_element_type=F32,
        )
        for dz in range(3)
    ]
    head, tail = [term[:block] for term in terms], [term[block:] for term in terms]
    extra = {0: [head[0], head[1]], 1: [tail[0]]}
    extra.setdefault(depth, []).append(head[2])
    extra.setdefault(depth + 1, []).extend([tail[1], tail[2]])
    for n in range(depth + 2):
        rows = slice(n * block, (n + 1) * block)
        preact = part[rows, :]
        for term in extra.get(n, []):
            preact = preact + term
        sig = 1.0 / (1.0 + jnp.exp(-preact))
        slope = sig * (1.0 + preact * (1.0 - sig))
        slopes[rows, :] = slope
        for m in range(micro):
            if n == 0 or n == depth + 1:
                up = pick(m, 2, n == 0)
            else:
                up = grad[m, n - 1].astype(F32)
            delta = (up * slope[m * cells : (m + 1) * cells]).astype(BF16)
            write_shifts(delta, height, shifts, n * block + m * cells)
    back = back_product(shifts, mirror, block, depth)
    for m in range(micro):
        ends = []
        for n in range(depth):
            first = n * block + m * cells
            total = grad[m, n].astype(F32) + back[first : first + cells]
            result[m, n] = total.astype(BF16)
            if n in (0, depth - 1):
                ends.append(total)
        low, high = ends[0], ends[-1]
        to_near[m, 0] = jnp.where(even, high, low).astype(BF16)
        to_far[m, 0] = jnp.where(even, low, high).astype(BF16)


def shift_kernel(height, acts, near, far, after, shifts):
    micro, depth, cells, _ = acts.shape
    even = lax.rem(lax.axis_index("slab"), 2) == 0
    for m in range(micro):
        below = jnp.where(even, far[m, 1].astype(F32), near[m, 1].astype(F32))
        above = jnp.where(even, near[m, 0].astype(F32), far[m, 0].astype(F32))
        planes = [below] + [acts[m, n] for n in range(depth)] + [above]
        for n, plane in enumerate(planes):
            write_shifts(plane, height, shifts, (n * micro + m) * cells)


def raw_kernel(
    spot, incoming, in_near, in_far, grad, near, far, slopes, shifts, upstream, deltas, *refs
):
    sends, (keep, raw) = refs[:4], refs[4:]
    micro, depth, cells, channels = upstream.shape
    block, span = micro * cells, 9 * channels
    last = lax.axis_index("segment") == lax.axis_size("segment") - 1
    even = lax.rem(lax.axis_index("slab"), 2) == 0
    for m in range(micro):
        by_near = jnp.where(last, near[m, 2].astype(F32), in_near[m, 0].astype(F32))
        by_far = jnp.where(last, far[m, 2].astype(F32), in_far[m, 0].astype(F32))
        planes = [jnp.where(even, by_far, by_near)]
        for n in range(depth):
            up = jnp.where(last, grad[m, n].astype(F32), incoming[m, n].astype(F32))
            upstream[m, n] = up.astype(BF16)
            planes.append(up)
        planes.append(jnp.where(even, by_near, by_far))
        for n, up in enumerate(planes):
            rows = slice(n * block + m * cells, n * block + (m + 1) * cells)
            deltas[rows, :] = (up * slopes[rows, :]).astype(BF16)
    for dz in range(3):
        total = None
        for n in range(depth):
            term = lax.dot_general(
                shifts[(dz + n) * block : (dz + n + 1) * block, :],
                deltas[(n + 1) * block : (n + 2) * block, :],
                (((0,), (0,)), ((), ())),
                preferred_element_type=F32,
            )
            total = term if total is None else total + term
        raw[dz * span : (dz + 1) * span, :] = total
    part = keep.shape[1]
    for turn in range(4):
        keep[turn] = raw[pl.ds((spot[0] ^ turn) * part, part), :]
        sends[turn][...] = raw[pl.ds((spot[0] ^ turn ^ 4) * part, part), :].astype(BF16)


def add_kernel(turn, keep, got, out):
    out[...] = (keep[turn] + got[...].astype(F32)).astype(BF16)


def sum_kernel(keep, *refs):
    total = keep[0]
    for got in refs[:-1]:
        total = total + got[...].astype(F32)
    refs[-1][...] = total.astype(refs[-1].dtype)


def both_kernel(mine, other, out):
    out[...] = (mine[...].astype(F32) + other[...].astype(F32)).astype(BF16)


def column_squares(value):
    value = value.astype(F32)
    return jnp.sum(value * value, axis=0, keepdims=True)


def norm_kernel(*refs):
    sums = [column_squares(piece[...]) for piece in refs[:-1]]
    while len(sums) > 1:
        sums = [a + b for a, b in zip(sums[::2], sums[1::2], strict=True)]
    refs[-1][...] = jnp.broadcast_to(sums[0], refs[-1].shape)


def back_kernel(height, deltas, upstream, mirror, out, shifts):
    micro, depth, cells, channels = upstream.shape
    block = micro * cells
    for n in range(depth + 2):
        for m in range(micro):
            rows = slice(n * block + m * cells, n * block + (m + 1) * cells)
            write_shifts(deltas[rows, :], height, shifts, rows.start)
    back = back_product(shifts, mirror, block, depth)
    for m in range(micro):
        for n in range(depth):
            first = n * block + m * cells
            total = upstream[m, n].astype(F32) + back[first : first + cells]
            out[m, n] = total.astype(BF16)


def place_kernel(bound, count, spot, *refs):
    sums, pieces, (out, scaled, sems) = refs[: 2 * count], refs[2 * count : -3], refs[-3:]
    mine, other = (sum(value[:1, :] for value in sums[side::2]) for side in range(2))
    squares = mine + other
    norm = jnp.sqrt(jnp.sum(squares, axis=1, keepdims=True))
    factor = jnp.minimum(1.0, bound / (norm + 1e-06))
    copies = []
    for n, piece in enumerate(pieces):
        scaled[n] = piece[...].astype(F32) * factor
        copies.append(pltpu.make_async_copy(scaled.at[n], out.at[spot[0] ^ n], sems.at[n]))
        copies[-1].start()
    for copy in copies:
        copy.wait()


def shards(activations, weights, out_grad):
    weight = weights[0]
    channels = weight.shape[1]
    micro, depth, width, height = activations.shape[1:5]
    cells = width * height
    acts = activations[0].reshape(micro, depth, cells, channels)
    grad = out_grad.reshape(micro, depth, cells, channels)
    rows = depth * cells
    segments = lax.axis_size("segment")
    count = lax.axis_size("slab")
    index = lax.axis_index("slab")
    last = lax.axis_index("segment") == segments - 1
    large = pltpu.CompilerParams(vmem_limit_bytes=16 << 20)
    small = pltpu.CompilerParams(vmem_limit_bytes=4 << 20)

    shape = jax.ShapeDtypeStruct
    rim = shape((micro, 3, cells, channels), BF16)
    volume = shape((micro, depth, cells, channels), BF16)
    to_near, to_far, acts, grad = pl.pallas_call(
        rim_kernel,
        out_shape=(rim, rim, volume, volume),
        in_specs=[HBM, HBM],
        out_specs=(VMEM,) * 4,
        scratch_shapes=[pltpu.SemaphoreType.DMA((2, micro, 2)), pltpu.SemaphoreType.DMA((2,))],
        compiler_params=small,
    )(*(pltpu.with_memory_space_constraint(a, pltpu.HBM) for a in (acts, grad)))
    near, far = swap(to_near, to_far)

    plane, span = micro * cells, 9 * channels
    whole = shape(weight.shape, BF16)
    outer = shape(((depth + 2) * plane, channels), F32)
    weight, mirror, part = pl.pallas_call(
        functools.partial(own_kernel, height),
        out_shape=(whole, whole, outer),
        in_specs=[VMEM, HBM],
        out_specs=(VMEM,) * 3,
        scratch_shapes=[pltpu.VMEM((depth * plane, span), BF16), pltpu.SemaphoreType.DMA],
        compiler_params=large,
    )(acts, pltpu.with_memory_space_constraint(weight, pltpu.HBM))

    edge = shape((micro, 1, cells, channels), BF16)
    wide = pltpu.VMEM(((depth + 2) * plane, span), BF16)
    result, to_near, to_far, slopes = pl.pallas_call(
        functools.partial(first_kernel, height),
        out_shape=(
            volume,
            edge,
            edge,
            outer,
        ),
        in_specs=[VMEM] * 6,
        out_specs=(VMEM,) * 4,
        scratch_shapes=[pltpu.VMEM((4 * plane, span), BF16), wide],
        compiler_params=large,
    )(near, far, grad, weight, mirror, part)

    def conv_back(deltas, upstream):
        return pl.pallas_call(
            functools.partial(back_kernel, height),
            out_shape=volume,
            in_specs=[VMEM] * 3,
            out_specs=VMEM,
            scratch_shapes=[wide],
            compiler_params=large,
        )(deltas, upstream, mirror)

    even = lax.rem(index, 2) == 0
    for step in range(1, segments - 1):
        incoming, in_near, in_far = cross(result, 1, 0), cross(to_near, 1, 1), cross_far(to_far)
        upstream = jnp.where(last, grad, incoming)
        by_near = jnp.where(last, near[:, 2:], in_near)
        by_far = jnp.where(last, far[:, 2:], in_far)
        below, above = jnp.where(even, by_far, by_near), jnp.where(even, by_near, by_far)
        around = jnp.concatenate([below, upstream, above], axis=1)
        around = jnp.swapaxes(around, 0, 1).reshape(outer.shape).astype(F32)
        result = conv_back((around * slopes).astype(BF16), upstream)
        low, high = result[:, :1], result[:, -1:]
        to_near, to_far = jnp.where(even, high, low), jnp.where(even, low, high)
    incoming, in_near, in_far = cross(result, 1, 0), cross(to_near, 1, 1), cross_far(to_far)
    shifts = pl.pallas_call(
        functools.partial(shift_kernel, height),
        out_shape=shape(((depth + 2) * plane, span), BF16),
        in_specs=[VMEM] * 4,
        out_specs=VMEM,
        compiler_params=large,
    )(acts, near, far, result)
    bits = [1 << n for n in range(1, count.bit_length() - 1)]
    inner = [bits[n : n + 2] for n in range(2, len(bits), 2)]
    crossing = inner[-1][0] if len(inner[-1]) == 1 else 0
    side = lax.rem(index, 2) ^ jnp.where(index & crossing, 1, 0)
    quarter = jnp.where(index & 2, 2, 0) + jnp.where(index & 4, 1, 0)
    masks = {1: 4, 2: 2, 3: 6}
    spot = (side * 4 + quarter).astype(jnp.int32).reshape(1)
    part = weight.shape[0] // 8
    piece = shape((part, channels), BF16)

    upstream, deltas, *rest = pl.pallas_call(
        raw_kernel,
        out_shape=(volume, shape(outer.shape, BF16))
        + (piece,) * 4
        + (shape((4, part, channels), F32),),
        in_specs=[SMEM] + [VMEM] * 8,
        out_specs=(VMEM,) * 7,
        scratch_shapes=[pltpu.VMEM((8 * part, channels), F32)],
        compiler_params=large,
    )(spot, incoming, in_near, in_far, grad, near, far, slopes, shifts)
    sends, keep = rest[:4], rest[4]
    got = {turn: exchange(sends[turn], 1) for turn in (3, 2, 1, 0)}
    across = []
    for turn in (3, 2, 1):
        added = pl.pallas_call(
            functools.partial(add_kernel, turn),
            out_shape=piece,
            in_specs=[VMEM] * 2,
            out_specs=VMEM,
            compiler_params=small,
        )(keep, got[turn])
        across.append(exchange(added, masks[turn]))
    gradients = conv_back(deltas, upstream)
    across[1], gradients = lax.optimization_barrier((across[1], gradients))
    single = len(inner[-1]) == 1
    direct = single and len(inner) == 1
    chunk = pl.pallas_call(
        sum_kernel,
        out_shape=shape((part, channels), BF16 if direct else F32),
        in_specs=[VMEM] * 5,
        out_specs=VMEM,
        compiler_params=small,
    )(keep, got[0], *across)

    def places(group):
        own = sum(jnp.where(index & bit, 1 << n, 0) for n, bit in enumerate(group))
        others = []
        for turn in range(1, 1 << len(group)):
            others.append((sum(bit for n, bit in enumerate(group) if turn >> n & 1), own ^ turn))
        return own, others

    paired = inner[:-1] if single else inner
    for group in paired:
        own, others = places(group)
        size = chunk.shape[0] >> len(group)
        took = [exchange(block(chunk, there, size, BF16), mask) for mask, there in others]
        chunk = block(chunk, own, size, F32) + sum(g.astype(F32) for g in took)
    gathered = chunk.astype(BF16)
    if single:
        gathered = pl.pallas_call(
            both_kernel,
            out_shape=shape(gathered.shape, BF16),
            in_specs=[VMEM] * 2,
            out_specs=VMEM,
            compiler_params=small,
        )(gathered, exchange(gathered, crossing | 1))

    for group in reversed(paired):
        own, others = places(group)
        took = [(there, exchange(gathered, mask)) for mask, there in others]
        blocks = []
        for n in range(1 << len(group)):
            value = jnp.where(own == n, gathered, took[0][1])
            for there, other in took[1:]:
                value = jnp.where(there == n, other, value)
            blocks.append(value)
        gathered = jnp.concatenate(blocks, axis=0)
    pieces = {turn: exchange(gathered, masks[turn]) for turn in (3, 2, 1)}
    ours = [gathered] + [pieces[turn] for turn in (1, 2, 3)]
    theirs = [exchange(piece, 1) for piece in ours]
    sums = [
        pl.pallas_call(
            norm_kernel,
            out_shape=shape((8, channels), F32),
            in_specs=[VMEM] * 4,
            out_specs=VMEM,
            compiler_params=small,
        )(*four)
        for four in (ours, theirs)
    ]
    sums += [cross(sums[0], back, mask) for back in range(1, segments) for mask in (0, 1)]
    bound = math.sqrt(27.0 * channels * channels * segments)
    update = pl.pallas_call(
        functools.partial(place_kernel, bound, segments),
        out_shape=jax.ShapeDtypeStruct((8, part, channels), F32),
        in_specs=[SMEM] + [VMEM] * (2 * segments + 8),
        out_specs=ANY,
        scratch_shapes=[pltpu.VMEM((8, part, channels), F32), pltpu.SemaphoreType.DMA((8,))],
        compiler_params=large,
    )((side * 4 + quarter).astype(jnp.int32).reshape(1), *sums, *ours, *theirs)
    gradients = gradients.reshape(1, micro, depth, width, height, channels)
    return (update.reshape(1, 8 * part, channels), gradients)


def solution(mesh):
    return jax.shard_map(
        shards,
        mesh=mesh,
        in_specs=(
            P("segment", None, "slab", None, None, None),
            P("segment", None, None),
            P(None, "slab", None, None, None),
        ),
        out_specs=(P("segment", None, None), P("segment", None, "slab", None, None, None)),
        check_vma=False,
    )
```

```python
import functools
import math

import jax
import jax.numpy as jnp
from jax import lax
from jax.experimental import pallas as pl
from jax.experimental.pallas import tpu as pltpu
from jax.sharding import PartitionSpec as P

BF16 = jnp.bfloat16
F32 = jnp.float32
VMEM = pl.BlockSpec(memory_space=pltpu.VMEM)
SMEM = pl.BlockSpec(memory_space=pltpu.SMEM)
ANY = pl.BlockSpec(memory_space=pl.ANY)
HBM = pl.BlockSpec(memory_space=pltpu.HBM)


def far_route(count):
    return [(i, ((i + 1) ^ 1) - 1) for i in range(1, count - 1)]


def swap(to_near, to_far):
    count = lax.axis_size("slab")
    near = [(i, i ^ 1) for i in range(count)]
    return lax.ppermute(to_near, "slab", near), lax.ppermute(to_far, "slab", far_route(count))


def cross_far(value):
    segments, count = lax.axis_size("segment"), lax.axis_size("slab")
    route = [
        (s * count + i, (s - 1) % segments * count + j)
        for s in range(segments)
        for i, j in far_route(count)
    ]
    return lax.ppermute(value, ("segment", "slab"), route)


def exchange(value, mask):
    count = lax.axis_size("slab")
    return lax.ppermute(value, "slab", [(i, i ^ mask) for i in range(count)])


def cross(value, back, mask):
    segments, count = lax.axis_size("segment"), lax.axis_size("slab")
    if back == 0 and mask == 0:
        return value
    route = [
        (s * count + i, (s - back) % segments * count + (i ^ mask))
        for s in range(segments)
        for i in range(count)
    ]
    return lax.ppermute(value, ("segment", "slab"), route)


def block(value, place, rows, dtype):
    return lax.dynamic_slice_in_dim(value, place * rows, rows, 0).astype(dtype)


def write_shifts(plane, height, out_ref, first):
    cells, channels = plane.shape
    width = cells // height
    rows = plane.astype(F32).reshape(width, height, channels)
    at = lax.broadcasted_iota(jnp.int32, rows.shape, 1)
    zero = jnp.zeros((1, height, channels), F32)
    before = jnp.where(at == 0, 0.0, pltpu.roll(rows, 1, 1))
    after = jnp.where(at == height - 1, 0.0, pltpu.roll(rows, height - 1, 1))
    for dy, moved in enumerate((before, rows, after)):
        for dx in range(3):
            if dx == 0:
                value = jnp.concatenate([zero, moved[:-1]], axis=0)
            elif dx == 1:
                value = moved
            else:
                value = jnp.concatenate([moved[1:], zero], axis=0)
            j = dx * 3 + dy
            out_ref[first : first + cells, j * channels : (j + 1) * channels] = value.reshape(
                cells, channels
            ).astype(BF16)


def back_product(shifts, mirror, block, depth):
    span = shifts.shape[1]
    total = None
    for dz in range(3):
        term = jnp.dot(
            shifts[dz * block : (dz + depth) * block, :],
            mirror[dz * span : (dz + 1) * span, :],
            preferred_element_type=F32,
        )
        total = term if total is None else total + term
    return total


def rim_kernel(acts, grad, near, far, acts_here, grad_here, sems, loads):
    micro, depth = acts.shape[:2]
    top = 1 - lax.rem(lax.axis_index("slab"), 2)
    copies = []
    for which, (out, high) in enumerate(((near, top), (far, 1 - top))):
        for m in range(micro):
            for part, (source, size, at) in enumerate(((acts, 2, 0), (grad, 1, 2))):
                copies.append(
                    pltpu.make_async_copy(
                        source.at[m, pl.ds(high * (depth - size), size)],
                        out.at[m, at : at + size],
                        sems.at[which, m, part],
                    )
                )
    for n, (source, out) in enumerate(((acts, acts_here), (grad, grad_here))):
        copies.append(pltpu.make_async_copy(source, out, loads.at[n]))
    for copy in copies:
        copy.start()
    for copy in copies:
        copy.wait()


def own_kernel(height, acts, stored, weight, mirror, part, own, sem):
    micro, depth, cells, channels = acts.shape
    block, span = micro * cells, 9 * channels
    copy = pltpu.make_async_copy(stored, weight, sem)
    copy.start()
    for n in range(depth):
        for m in range(micro):
            write_shifts(acts[m, n], height, own, n * block + m * cells)
    copy.wait()
    part[...] = jnp.zeros(part.shape, F32)
    for dz in range(3):
        rows = slice((2 - dz) * block, (2 - dz + depth) * block)
        part[rows, :] += jnp.dot(
            own[...], weight[dz * span : (dz + 1) * span, :], preferred_element_type=F32
        )
    for k in range(27):
        mirror[(26 - k) * channels : (27 - k) * channels, :] = weight[
            k * channels : (k + 1) * channels, :
        ].T


def first_kernel(
    height, near, far, grad, weight, mirror, part, result, slopes, to_far, *refs
):
    rim, shifts = refs[-2:]
    micro, depth, cells, channels = grad.shape
    even = lax.rem(lax.axis_index("slab"), 2) == 0
    block, span = micro * cells, 9 * channels

    def pick(m, n, below):
        a, b = near[m, n].astype(F32), far[m, n].astype(F32)
        return jnp.where(even, b, a) if below else jnp.where(even, a, b)

    for n in range(4):
        for m in range(micro):
            write_shifts(pick(m, n % 2, n < 2), height, rim, n * block + m * cells)
    terms = [
        jnp.dot(
            rim[dz * block : (dz + 2) * block, :],
            weight[dz * span : (dz + 1) * span, :],
            preferred_element_type=F32,
        )
        for dz in range(3)
    ]
    head, tail = [term[:block] for term in terms], [term[block:] for term in terms]
    extra = {0: [head[0], head[1]], 1: [tail[0]]}
    extra.setdefault(depth, []).append(head[2])
    extra.setdefault(depth + 1, []).extend([tail[1], tail[2]])
    for n in range(depth + 2):
        rows = slice(n * block, (n + 1) * block)
        preact = part[rows, :]
        for term in extra.get(n, []):
            preact = preact + term
        sig = 1.0 / (1.0 + jnp.exp(-preact))
        slope = sig * (1.0 + preact * (1.0 - sig))
        slopes[rows, :] = slope
        for m in range(micro):
            if n == 0 or n == depth + 1:
                up = pick(m, 2, n == 0)
            else:
                up = grad[m, n - 1].astype(F32)
            delta = (up * slope[m * cells : (m + 1) * cells]).astype(BF16)
            write_shifts(delta, height, shifts, n * block + m * cells)
    back = back_product(shifts, mirror, block, depth)
    for m in range(micro):
        ends = []
        for n in range(depth):
            first = n * block + m * cells
            total = grad[m, n].astype(F32) + back[first : first + cells]
            result[m, n] = total.astype(BF16)
            if n in (0, depth - 1):
                ends.append(total)
        low, high = ends[0], ends[-1]
        for to_near in refs[:-2]:
            to_near[m, 0] = jnp.where(even, high, low).astype(BF16)
        to_far[m, 0] = jnp.where(even, low, high).astype(BF16)


def shift_kernel(height, acts, near, far, after, shifts):
    micro, depth, cells, _ = acts.shape
    even = lax.rem(lax.axis_index("slab"), 2) == 0
    for m in range(micro):
        below = jnp.where(even, far[m, 1].astype(F32), near[m, 1].astype(F32))
        above = jnp.where(even, near[m, 0].astype(F32), far[m, 0].astype(F32))
        planes = [below] + [acts[m, n] for n in range(depth)] + [above]
        for n, plane in enumerate(planes):
            write_shifts(plane, height, shifts, (n * micro + m) * cells)


def raw_kernel(
    spot, incoming, grad, far, slopes, shifts, upstream, deltas, far_slope, *refs
):
    sends, (keep, raw) = refs[:4], refs[4:]
    part = keep.shape[1]
    micro, depth, cells, channels = upstream.shape
    block, span = micro * cells, 9 * channels
    last = lax.axis_index("segment") == lax.axis_size("segment") - 1
    even = lax.rem(lax.axis_index("slab"), 2) == 0
    low, high = slice(0, block), slice((depth + 1) * block, (depth + 2) * block)
    slope = jnp.where(even, slopes[low, :], slopes[high, :])
    far_slope[...] = slope
    for m in range(micro):
        inside = slice(m * cells, (m + 1) * cells)
        rim = (far[m, 2].astype(F32) * slope[inside]).astype(BF16)
        for first in (low.start, high.start):
            deltas[first + m * cells : first + (m + 1) * cells, :] = rim
        planes = []
        for n in range(depth):
            up = jnp.where(last, grad[m, n].astype(F32), incoming[m, n].astype(F32))
            upstream[m, n] = up.astype(BF16)
            first = (n + 1) * block + m * cells
            delta = up * slopes[first : first + cells, :]
            deltas[first : first + cells, :] = delta.astype(BF16)
            planes.append(delta)
        first = part + m * cells
        sends[0][first : first + cells, :] = jnp.where(even, planes[-1], planes[0]).astype(BF16)
    for dz in range(3):
        total = None
        for n in range(depth):
            term = lax.dot_general(
                shifts[(dz + n) * block : (dz + n + 1) * block, :],
                deltas[(n + 1) * block : (n + 2) * block, :],
                (((0,), (0,)), ((), ())),
                preferred_element_type=F32,
            )
            total = term if total is None else total + term
        raw[dz * span : (dz + 1) * span, :] = total
    for turn in range(4):
        keep[turn] = raw[pl.ds((spot[0] ^ turn) * part, part), :]
        sends[turn][:part, :] = raw[pl.ds((spot[0] ^ turn ^ 4) * part, part), :].astype(BF16)


def add_kernel(turn, keep, got, out):
    out[...] = (keep[turn] + got[...].astype(F32)).astype(BF16)


def sum_kernel(keep, *refs):
    total = keep[0]
    for got in refs[:-1]:
        total = total + got[: total.shape[0], :].astype(F32)
    refs[-1][...] = total.astype(refs[-1].dtype)


def both_kernel(mine, other, out):
    out[...] = (mine[...].astype(F32) + other[...].astype(F32)).astype(BF16)


def column_squares(value):
    value = value.astype(F32)
    return jnp.sum(value * value, axis=0, keepdims=True)


def norm_kernel(*refs):
    sums = [column_squares(piece[...]) for piece in refs[:-1]]
    while len(sums) > 1:
        sums = [a + b for a, b in zip(sums[::2], sums[1::2], strict=True)]
    refs[-1][...] = jnp.broadcast_to(sums[0], refs[-1].shape)


def back_kernel(
    height, deltas, by_near, in_far, far_slope, upstream, mirror, out, shifts
):
    micro, depth, cells, channels = upstream.shape
    block = micro * cells
    last = lax.axis_index("segment") == lax.axis_size("segment") - 1
    even = lax.rem(lax.axis_index("slab"), 2) == 0
    start = by_near.shape[0] - block
    for m in range(micro):
        inside = slice(m * cells, (m + 1) * cells)
        near = by_near[start + m * cells : start + (m + 1) * cells, :].astype(F32)
        far = (in_far[m, 0].astype(F32) * far_slope[inside, :]).astype(BF16).astype(F32)
        far = jnp.where(last, deltas[inside, :].astype(F32), far)
        write_shifts(jnp.where(even, far, near), height, shifts, m * cells)
        first = (depth + 1) * block + m * cells
        write_shifts(jnp.where(even, near, far), height, shifts, first)
        for n in range(1, depth + 1):
            first = n * block + m * cells
            write_shifts(deltas[first : first + cells, :], height, shifts, first)
    back = back_product(shifts, mirror, block, depth)
    for m in range(micro):
        for n in range(depth):
            first = n * block + m * cells
            total = upstream[m, n].astype(F32) + back[first : first + cells]
            out[m, n] = total.astype(BF16)


def place_kernel(bound, count, spot, *refs):
    sums, pieces, (out, scaled, sems) = refs[: 2 * count], refs[2 * count : -3], refs[-3:]
    mine, other = (sum(value[:1, :] for value in sums[side::2]) for side in range(2))
    squares = mine + other
    norm = jnp.sqrt(jnp.sum(squares, axis=1, keepdims=True))
    factor = jnp.minimum(1.0, bound / (norm + 1e-06))
    copies = []
    for n, piece in enumerate(pieces):
        scaled[n] = piece[...].astype(F32) * factor
        copies.append(pltpu.make_async_copy(scaled.at[n], out.at[spot[0] ^ n], sems.at[n]))
        copies[-1].start()
    for copy in copies:
        copy.wait()


def shards(activations, weights, out_grad):
    weight = weights[0]
    channels = weight.shape[1]
    micro, depth, width, height = activations.shape[1:5]
    cells = width * height
    acts = activations[0].reshape(micro, depth, cells, channels)
    grad = out_grad.reshape(micro, depth, cells, channels)
    rows = depth * cells
    segments = lax.axis_size("segment")
    count = lax.axis_size("slab")
    index = lax.axis_index("slab")
    last = lax.axis_index("segment") == segments - 1
    large = pltpu.CompilerParams(vmem_limit_bytes=16 << 20)
    small = pltpu.CompilerParams(vmem_limit_bytes=4 << 20)

    shape = jax.ShapeDtypeStruct
    rim = shape((micro, 3, cells, channels), BF16)
    volume = shape((micro, depth, cells, channels), BF16)
    to_near, to_far, acts, grad = pl.pallas_call(
        rim_kernel,
        out_shape=(rim, rim, volume, volume),
        in_specs=[HBM, HBM],
        out_specs=(VMEM,) * 4,
        scratch_shapes=[pltpu.SemaphoreType.DMA((2, micro, 2)), pltpu.SemaphoreType.DMA((2,))],
        compiler_params=small,
    )(*(pltpu.with_memory_space_constraint(a, pltpu.HBM) for a in (acts, grad)))
    near, far = swap(to_near, to_far)

    plane, span = micro * cells, 9 * channels
    whole = shape(weight.shape, BF16)
    outer = shape(((depth + 2) * plane, channels), F32)
    weight, mirror, part = pl.pallas_call(
        functools.partial(own_kernel, height),
        out_shape=(whole, whole, outer),
        in_specs=[VMEM, HBM],
        out_specs=(VMEM,) * 3,
        scratch_shapes=[pltpu.VMEM((depth * plane, span), BF16), pltpu.SemaphoreType.DMA],
        compiler_params=large,
    )(acts, pltpu.with_memory_space_constraint(weight, pltpu.HBM))

    edge = shape((micro, 1, cells, channels), BF16)
    wide = pltpu.VMEM(((depth + 2) * plane, span), BF16)
    edges = (edge,) * (1 if segments == 2 else 2)
    result, slopes, to_far, *to_near = pl.pallas_call(
        functools.partial(first_kernel, height),
        out_shape=(volume, outer) + edges,
        in_specs=[VMEM] * 6,
        out_specs=(VMEM,) * (2 + len(edges)),
        scratch_shapes=[pltpu.VMEM((4 * plane, span), BF16), wide],
        compiler_params=large,
    )(near, far, grad, weight, mirror, part)

    def conv_back(deltas, by_near, in_far, far_slope, upstream):
        return pl.pallas_call(
            functools.partial(back_kernel, height),
            out_shape=volume,
            in_specs=[VMEM] * 6,
            out_specs=VMEM,
            scratch_shapes=[wide],
            compiler_params=large,
        )(deltas, by_near, in_far, far_slope, upstream, mirror)

    part = weight.shape[0] // 8
    even = lax.rem(index, 2) == 0
    for step in range(1, segments - 1):
        incoming, in_near, in_far = cross(result, 1, 0), cross(to_near[0], 1, 1), cross_far(to_far)
        upstream = jnp.where(last, grad, incoming)
        stacked = jnp.swapaxes(upstream, 0, 1).reshape(depth * plane, channels).astype(F32)
        deltas = (stacked * slopes[plane:-plane]).astype(BF16)
        near_slope = jnp.where(even, slopes[-plane:], slopes[:plane])
        far_slope = jnp.where(even, slopes[:plane], slopes[-plane:])
        by_near = jnp.where(last, near[:, 2:], in_near).reshape(plane, channels).astype(F32)
        rim = (far[:, 2:].reshape(plane, channels).astype(F32) * far_slope).astype(BF16)
        deltas = jnp.concatenate([rim, deltas, rim], axis=0)
        result = conv_back(
            deltas, (by_near * near_slope).astype(BF16), in_far, far_slope, upstream
        )
        low, high = result[:, :1], result[:, -1:]
        to_near, to_far = [jnp.where(even, high, low)], jnp.where(even, low, high)
    incoming = cross(result, 1, 0)
    shifts = pl.pallas_call(
        functools.partial(shift_kernel, height),
        out_shape=shape(((depth + 2) * plane, span), BF16),
        in_specs=[VMEM] * 4,
        out_specs=VMEM,
        compiler_params=large,
    )(acts, near, far, result)
    bits = [1 << n for n in range(1, count.bit_length() - 1)]
    inner = [bits[n : n + 2] for n in range(2, len(bits), 2)]
    crossing = inner[-1][0] if len(inner[-1]) == 1 else 0
    side = lax.rem(index, 2) ^ jnp.where(index & crossing, 1, 0)
    quarter = jnp.where(index & 2, 2, 0) + jnp.where(index & 4, 1, 0)
    masks = {1: 4, 2: 2, 3: 6}
    spot = (side * 4 + quarter).astype(jnp.int32).reshape(1)
    piece = shape((part, channels), BF16)

    upstream, deltas, far_slope, *rest = pl.pallas_call(
        raw_kernel,
        out_shape=(
            volume,
            shape(outer.shape, BF16),
            shape((plane, channels), F32),
            shape((part + plane, channels), BF16),
            piece,
            piece,
            piece,
            shape((4, part, channels), F32),
        ),
        in_specs=[SMEM] + [VMEM] * 5,
        out_specs=(VMEM,) * 8,
        scratch_shapes=[pltpu.VMEM((8 * part, channels), F32)],
        compiler_params=large,
    )(spot, incoming, grad, far, slopes, shifts)
    sends, keep = rest[:4], rest[4]
    order = (2, 1, 3)
    got = {turn: exchange(sends[turn], 1) for turn in order + (0,)}
    across = []
    for turn in order:
        added = pl.pallas_call(
            functools.partial(add_kernel, turn),
            out_shape=piece,
            in_specs=[VMEM] * 2,
            out_specs=VMEM,
            compiler_params=small,
        )(keep, got[turn])
        if turn == order[-1]:
            added, to_far = lax.optimization_barrier((added, to_far))
        across.append(exchange(added, masks[turn]))
    in_far = cross_far(to_far)
    across[2], in_far = lax.optimization_barrier((across[2], in_far))
    gradients = conv_back(deltas, got[0], in_far, far_slope, upstream)
    single = len(inner[-1]) == 1
    direct = single and len(inner) == 1
    chunk = pl.pallas_call(
        sum_kernel,
        out_shape=shape((part, channels), BF16 if direct else F32),
        in_specs=[VMEM] * 5,
        out_specs=VMEM,
        compiler_params=small,
    )(keep, got[0], *across)

    def places(group):
        own = sum(jnp.where(index & bit, 1 << n, 0) for n, bit in enumerate(group))
        others = []
        for turn in range(1, 1 << len(group)):
            others.append((sum(bit for n, bit in enumerate(group) if turn >> n & 1), own ^ turn))
        return own, others

    paired = inner[:-1] if single else inner
    for group in paired:
        own, others = places(group)
        size = chunk.shape[0] >> len(group)
        took = [exchange(block(chunk, there, size, BF16), mask) for mask, there in others]
        chunk = block(chunk, own, size, F32) + sum(g.astype(F32) for g in took)
    gathered = chunk.astype(BF16)
    if single:
        other = exchange(gathered, crossing | 1)
        other, gradients = lax.optimization_barrier((other, gradients))
        gathered = pl.pallas_call(
            both_kernel,
            out_shape=shape(gathered.shape, BF16),
            in_specs=[VMEM] * 2,
            out_specs=VMEM,
            compiler_params=small,
        )(gathered, other)

    for group in reversed(paired):
        own, others = places(group)
        took = [(there, exchange(gathered, mask)) for mask, there in others]
        blocks = []
        for n in range(1 << len(group)):
            value = jnp.where(own == n, gathered, took[0][1])
            for there, other in took[1:]:
                value = jnp.where(there == n, other, value)
            blocks.append(value)
        gathered = jnp.concatenate(blocks, axis=0)
    pieces = {turn: exchange(gathered, masks[turn]) for turn in (2, 1, 3)}
    ours = [gathered] + [pieces[turn] for turn in (1, 2, 3)]
    theirs = [exchange(piece, 1) for piece in ours]
    sums = [
        pl.pallas_call(
            norm_kernel,
            out_shape=shape((8, channels), F32),
            in_specs=[VMEM] * 4,
            out_specs=VMEM,
            compiler_params=small,
        )(*four)
        for four in (ours, theirs)
    ]
    sums += [cross(sums[0], back, mask) for back in range(1, segments) for mask in (0, 1)]
    bound = math.sqrt(27.0 * channels * channels * segments)
    update = pl.pallas_call(
        functools.partial(place_kernel, bound, segments),
        out_shape=jax.ShapeDtypeStruct((8, part, channels), F32),
        in_specs=[SMEM] + [VMEM] * (2 * segments + 8),
        out_specs=ANY,
        scratch_shapes=[pltpu.VMEM((8, part, channels), F32), pltpu.SemaphoreType.DMA((8,))],
        compiler_params=large,
    )((side * 4 + quarter).astype(jnp.int32).reshape(1), *sums, *ours, *theirs)
    gradients = gradients.reshape(1, micro, depth, width, height, channels)
    return (update.reshape(1, 8 * part, channels), gradients)


def solution(mesh):
    return jax.shard_map(
        shards,
        mesh=mesh,
        in_specs=(
            P("segment", None, "slab", None, None, None),
            P("segment", None, None),
            P(None, "slab", None, None, None),
        ),
        out_specs=(P("segment", None, None), P("segment", None, "slab", None, None, None)),
        check_vma=False,
    )
```

```python
import functools
import math

import jax
import jax.numpy as jnp
from jax import lax
from jax.experimental import pallas as pl
from jax.experimental.pallas import tpu as pltpu
from jax.sharding import PartitionSpec as P

BF16 = jnp.bfloat16
F32 = jnp.float32
VMEM = pl.BlockSpec(memory_space=pltpu.VMEM)
SMEM = pl.BlockSpec(memory_space=pltpu.SMEM)
ANY = pl.BlockSpec(memory_space=pl.ANY)
HBM = pl.BlockSpec(memory_space=pltpu.HBM)


def far_route(count):
    return [(i, ((i + 1) ^ 1) - 1) for i in range(1, count - 1)]


def swap(to_near, to_far):
    count = lax.axis_size("slab")
    near = [(i, i ^ 1) for i in range(count)]
    return lax.ppermute(to_near, "slab", near), lax.ppermute(to_far, "slab", far_route(count))


def exchange(value, mask):
    count = lax.axis_size("slab")
    return lax.ppermute(value, "slab", [(i, i ^ mask) for i in range(count)])


def cross(value, back, mask):
    segments, count = lax.axis_size("segment"), lax.axis_size("slab")
    if back == 0 and mask == 0:
        return value
    route = [
        (s * count + i, (s - back) % segments * count + (i ^ mask))
        for s in range(segments)
        for i in range(count)
    ]
    return lax.ppermute(value, ("segment", "slab"), route)


def block(value, place, rows, dtype):
    return lax.dynamic_slice_in_dim(value, place * rows, rows, 0).astype(dtype)


def write_shifts(plane, height, out_ref, first):
    cells, channels = plane.shape
    width = cells // height
    rows = plane.astype(F32).reshape(width, height, channels)
    at = lax.broadcasted_iota(jnp.int32, rows.shape, 1)
    zero = jnp.zeros((1, height, channels), F32)
    before = jnp.where(at == 0, 0.0, pltpu.roll(rows, 1, 1))
    after = jnp.where(at == height - 1, 0.0, pltpu.roll(rows, height - 1, 1))
    for dy, moved in enumerate((before, rows, after)):
        for dx in range(3):
            if dx == 0:
                value = jnp.concatenate([zero, moved[:-1]], axis=0)
            elif dx == 1:
                value = moved
            else:
                value = jnp.concatenate([moved[1:], zero], axis=0)
            j = dx * 3 + dy
            out_ref[first : first + cells, j * channels : (j + 1) * channels] = value.reshape(
                cells, channels
            ).astype(BF16)


def back_product(shifts, mirror, block, depth):
    span = shifts.shape[1]
    total = None
    for dz in range(3):
        term = jnp.dot(
            shifts[dz * block : (dz + depth) * block, :],
            mirror[dz * span : (dz + 1) * span, :],
            preferred_element_type=F32,
        )
        total = term if total is None else total + term
    return total


def rim_kernel(acts, grad, near, far, acts_here, grad_here, sems, loads):
    micro, depth = acts.shape[:2]
    top = 1 - lax.rem(lax.axis_index("slab"), 2)
    copies = []
    for which, (out, high) in enumerate(((near, top), (far, 1 - top))):
        for m in range(micro):
            for part, (source, size, at) in enumerate(((acts, 2, 0), (grad, 1, 2))):
                copies.append(
                    pltpu.make_async_copy(
                        source.at[m, pl.ds(high * (depth - size), size)],
                        out.at[m, at : at + size],
                        sems.at[which, m, part],
                    )
                )
    for n, (source, out) in enumerate(((acts, acts_here), (grad, grad_here))):
        copies.append(pltpu.make_async_copy(source, out, loads.at[n]))
    for copy in copies:
        copy.start()
    for copy in copies:
        copy.wait()


def own_kernel(height, acts, stored, weight, mirror, part, own, sem):
    micro, depth, cells, channels = acts.shape
    block, span = micro * cells, 9 * channels
    copy = pltpu.make_async_copy(stored, weight, sem)
    copy.start()
    for n in range(depth):
        for m in range(micro):
            write_shifts(acts[m, n], height, own, n * block + m * cells)
    copy.wait()
    part[...] = jnp.zeros(part.shape, F32)
    for dz in range(3):
        rows = slice((2 - dz) * block, (2 - dz + depth) * block)
        part[rows, :] += jnp.dot(
            own[...], weight[dz * span : (dz + 1) * span, :], preferred_element_type=F32
        )
    for k in range(27):
        mirror[(26 - k) * channels : (27 - k) * channels, :] = weight[
            k * channels : (k + 1) * channels, :
        ].T


def first_kernel(
    height, near, far, grad, weight, mirror, part, result, slopes, rim, shifts
):
    micro, depth, cells, channels = grad.shape
    even = lax.rem(lax.axis_index("slab"), 2) == 0
    block, span = micro * cells, 9 * channels

    def pick(m, n, below):
        a, b = near[m, n].astype(F32), far[m, n].astype(F32)
        return jnp.where(even, b, a) if below else jnp.where(even, a, b)

    for n in range(4):
        for m in range(micro):
            write_shifts(pick(m, n % 2, n < 2), height, rim, n * block + m * cells)
    terms = [
        jnp.dot(
            rim[dz * block : (dz + 2) * block, :],
            weight[dz * span : (dz + 1) * span, :],
            preferred_element_type=F32,
        )
        for dz in range(3)
    ]
    head, tail = [term[:block] for term in terms], [term[block:] for term in terms]
    extra = {0: [head[0], head[1]], 1: [tail[0]]}
    extra.setdefault(depth, []).append(head[2])
    extra.setdefault(depth + 1, []).extend([tail[1], tail[2]])
    for n in range(depth + 2):
        rows = slice(n * block, (n + 1) * block)
        preact = part[rows, :]
        for term in extra.get(n, []):
            preact = preact + term
        sig = 1.0 / (1.0 + jnp.exp(-preact))
        slope = sig * (1.0 + preact * (1.0 - sig))
        if 0 < n <= depth:
            slopes[(n - 1) * block : n * block, :] = slope
        for m in range(micro):
            if n == 0 or n == depth + 1:
                up = pick(m, 2, n == 0)
            else:
                up = grad[m, n - 1].astype(F32)
            delta = (up * slope[m * cells : (m + 1) * cells]).astype(BF16)
            write_shifts(delta, height, shifts, n * block + m * cells)
    back = back_product(shifts, mirror, block, depth)
    for m in range(micro):
        for n in range(depth):
            first = n * block + m * cells
            total = grad[m, n].astype(F32) + back[first : first + cells]
            result[m, n] = total.astype(BF16)


def shift_kernel(height, acts, near, far, after, shifts):
    micro, depth, cells, _ = acts.shape
    even = lax.rem(lax.axis_index("slab"), 2) == 0
    for m in range(micro):
        below = jnp.where(even, far[m, 1].astype(F32), near[m, 1].astype(F32))
        above = jnp.where(even, near[m, 0].astype(F32), far[m, 0].astype(F32))
        planes = [below] + [acts[m, n] for n in range(depth)] + [above]
        for n, plane in enumerate(planes):
            write_shifts(plane, height, shifts, (n * micro + m) * cells)


def raw_kernel(spot, incoming, grad, slopes, shifts, upstream, deltas, far_rim, *refs):
    sends, (keep, raw) = refs[:4], refs[4:]
    part = keep.shape[1]
    micro, depth, cells, channels = upstream.shape
    block, span = micro * cells, 9 * channels
    last = lax.axis_index("segment") == lax.axis_size("segment") - 1
    even = lax.rem(lax.axis_index("slab"), 2) == 0
    for m in range(micro):
        planes = []
        for n in range(depth):
            up = jnp.where(last, grad[m, n].astype(F32), incoming[m, n].astype(F32))
            upstream[m, n] = up.astype(BF16)
            first = n * block + m * cells
            delta = up * slopes[first : first + cells, :]
            deltas[first : first + cells, :] = delta.astype(BF16)
            planes.append(delta)
        low, high = planes[0], planes[-1]
        far_rim[m * cells : (m + 1) * cells, :] = jnp.where(even, low, high).astype(BF16)
        first = part + m * cells
        sends[0][first : first + cells, :] = jnp.where(even, high, low).astype(BF16)
    for dz in range(3):
        total = None
        for n in range(depth):
            term = lax.dot_general(
                shifts[(dz + n) * block : (dz + n + 1) * block, :],
                deltas[n * block : (n + 1) * block, :],
                (((0,), (0,)), ((), ())),
                preferred_element_type=F32,
            )
            total = term if total is None else total + term
        raw[dz * span : (dz + 1) * span, :] = total
    for turn in range(4):
        keep[turn] = raw[pl.ds((spot[0] ^ turn) * part, part), :]
        sends[turn][:part, :] = raw[pl.ds((spot[0] ^ turn ^ 4) * part, part), :].astype(BF16)


def add_kernel(turn, keep, got, *refs):
    rows, out = keep.shape[1], refs[-1]
    out[:rows, :] = (keep[turn] + got[...].astype(F32)).astype(BF16)
    if len(refs) > 1:
        out[rows:, :] = refs[0][...]


def sum_kernel(count, keep, *refs):
    total, out = keep[0], refs[-1]
    rows = total.shape[0]
    for got in refs[:count]:
        total = total + got[:rows, :].astype(F32)
    out[:rows, :] = total.astype(out.dtype)
    if out.shape[0] > rows:
        out[rows:, :] = refs[count][...]


def both_kernel(mine, other, out):
    rows = out.shape[0]
    out[...] = (mine[:rows, :].astype(F32) + other[:rows, :].astype(F32)).astype(BF16)


def column_squares(value):
    value = value.astype(F32)
    return jnp.sum(value * value, axis=0, keepdims=True)


def norm_kernel(*refs):
    sums = [column_squares(piece[...]) for piece in refs[:-1]]
    while len(sums) > 1:
        sums = [a + b for a, b in zip(sums[::2], sums[1::2], strict=True)]
    refs[-1][...] = jnp.broadcast_to(sums[0], refs[-1].shape)


def back_kernel(height, riders, deltas, by_near, upstream, mirror, *refs):
    by_far, (out, shifts) = refs[:-2], refs[-2:]
    micro, depth, cells, channels = upstream.shape
    block = micro * cells
    index = lax.axis_index("slab")
    even = lax.rem(index, 2) == 0
    link = index ^ jnp.where(even, index - 1, index + 1)

    def tail(ref, m):
        start = ref.shape[0] - block + m * cells
        return ref[start : start + cells, :].astype(F32)

    for m in range(micro):
        near = tail(by_near, m)
        if riders:
            far = jnp.zeros((cells, channels), F32)
            for mask, ref in zip(riders, by_far, strict=True):
                far = jnp.where(link == mask, tail(ref, m), far)
        else:
            far = tail(by_far[0], m)
        write_shifts(jnp.where(even, far, near), height, shifts, m * cells)
        first = (depth + 1) * block + m * cells
        write_shifts(jnp.where(even, near, far), height, shifts, first)
        for n in range(depth):
            first = n * block + m * cells
            write_shifts(deltas[first : first + cells, :], height, shifts, first + block)
    back = back_product(shifts, mirror, block, depth)
    for m in range(micro):
        for n in range(depth):
            first = n * block + m * cells
            total = upstream[m, n].astype(F32) + back[first : first + cells]
            out[m, n] = total.astype(BF16)


def place_kernel(bound, count, spot, *refs):
    sums, pieces, (out, scaled, sems) = refs[: 2 * count], refs[2 * count : -3], refs[-3:]
    mine, other = (sum(value[:1, :] for value in sums[side::2]) for side in range(2))
    squares = mine + other
    norm = jnp.sqrt(jnp.sum(squares, axis=1, keepdims=True))
    factor = jnp.minimum(1.0, bound / (norm + 1e-06))
    copies = []
    for n, piece in enumerate(pieces):
        scaled[n] = piece[...].astype(F32) * factor
        copies.append(pltpu.make_async_copy(scaled.at[n], out.at[spot[0] ^ n], sems.at[n]))
        copies[-1].start()
    for copy in copies:
        copy.wait()


def shards(activations, weights, out_grad):
    weight = weights[0]
    channels = weight.shape[1]
    micro, depth, width, height = activations.shape[1:5]
    cells = width * height
    acts = activations[0].reshape(micro, depth, cells, channels)
    grad = out_grad.reshape(micro, depth, cells, channels)
    rows = depth * cells
    segments = lax.axis_size("segment")
    count = lax.axis_size("slab")
    index = lax.axis_index("slab")
    last = lax.axis_index("segment") == segments - 1
    large = pltpu.CompilerParams(vmem_limit_bytes=16 << 20)
    small = pltpu.CompilerParams(vmem_limit_bytes=4 << 20)

    shape = jax.ShapeDtypeStruct
    rim = shape((micro, 3, cells, channels), BF16)
    volume = shape((micro, depth, cells, channels), BF16)
    to_near, to_far, acts, grad = pl.pallas_call(
        rim_kernel,
        out_shape=(rim, rim, volume, volume),
        in_specs=[HBM, HBM],
        out_specs=(VMEM,) * 4,
        scratch_shapes=[pltpu.SemaphoreType.DMA((2, micro, 2)), pltpu.SemaphoreType.DMA((2,))],
        compiler_params=small,
    )(*(pltpu.with_memory_space_constraint(a, pltpu.HBM) for a in (acts, grad)))
    near, far = swap(to_near, to_far)

    plane, span = micro * cells, 9 * channels
    whole = shape(weight.shape, BF16)
    outer = shape(((depth + 2) * plane, channels), F32)
    weight, mirror, part = pl.pallas_call(
        functools.partial(own_kernel, height),
        out_shape=(whole, whole, outer),
        in_specs=[VMEM, HBM],
        out_specs=(VMEM,) * 3,
        scratch_shapes=[pltpu.VMEM((depth * plane, span), BF16), pltpu.SemaphoreType.DMA],
        compiler_params=large,
    )(acts, pltpu.with_memory_space_constraint(weight, pltpu.HBM))

    wide = pltpu.VMEM(((depth + 2) * plane, span), BF16)
    inside = shape((depth * plane, channels), F32)
    result, slopes = pl.pallas_call(
        functools.partial(first_kernel, height),
        out_shape=(volume, inside),
        in_specs=[VMEM] * 6,
        out_specs=(VMEM,) * 2,
        scratch_shapes=[pltpu.VMEM((4 * plane, span), BF16), wide],
        compiler_params=large,
    )(near, far, grad, weight, mirror, part)

    def conv_back(riders, deltas, by_near, by_far, upstream):
        return pl.pallas_call(
            functools.partial(back_kernel, height, riders),
            out_shape=volume,
            in_specs=[VMEM] * (4 + len(by_far)),
            out_specs=VMEM,
            scratch_shapes=[wide],
            compiler_params=large,
        )(deltas, by_near, upstream, mirror, *by_far)

    part = whole.shape[0] // 8
    even = lax.rem(index, 2) == 0
    for step in range(1, segments - 1):
        incoming = cross(result, 1, 0)
        upstream = jnp.where(last, grad, incoming)
        stacked = jnp.swapaxes(upstream, 0, 1).reshape(inside.shape).astype(F32)
        deltas = (stacked * slopes).astype(BF16)
        low, high = deltas[:plane], deltas[-plane:]
        by_near, by_far = swap(jnp.where(even, high, low), jnp.where(even, low, high))
        result = conv_back((), deltas, by_near, [by_far], upstream)
    incoming = cross(result, 1, 0)
    shifts = pl.pallas_call(
        functools.partial(shift_kernel, height),
        out_shape=shape(((depth + 2) * plane, span), BF16),
        in_specs=[VMEM] * 4,
        out_specs=VMEM,
        compiler_params=large,
    )(acts, near, far, result)
    bits = [1 << n for n in range(1, count.bit_length() - 1)]
    inner = [bits[n : n + 2] for n in range(2, len(bits), 2)]
    crossing = inner[-1][0] if len(inner[-1]) == 1 else 0
    side = lax.rem(index, 2) ^ jnp.where(index & crossing, 1, 0)
    quarter = jnp.where(index & 2, 2, 0) + jnp.where(index & 4, 1, 0)
    masks, across_mask, riders = {1: 4, 2: 2, 3: 6}, crossing | 1, ()
    if count == 16:
        side = lax.rem(index, 2) ^ jnp.where(index & 2, 1, 0)
        quarter = quarter ^ jnp.where(index & 8, 3, 0)
        masks, across_mask, riders = {1: 4, 2: 3, 3: 7}, 15, (3, 7, 15)
    spot = (side * 4 + quarter).astype(jnp.int32).reshape(1)
    piece = shape((part, channels), BF16)
    longer = shape((part + plane, channels), BF16)

    upstream, deltas, far_rim, *rest = pl.pallas_call(
        raw_kernel,
        out_shape=(
            volume,
            shape(inside.shape, BF16),
            shape((plane, channels), BF16),
            longer,
            piece,
            piece,
            piece,
            shape((4, part, channels), F32),
        ),
        in_specs=[SMEM] + [VMEM] * 4,
        out_specs=(VMEM,) * 8,
        scratch_shapes=[pltpu.VMEM((8 * part, channels), F32)],
        compiler_params=large,
    )(spot, incoming, grad, slopes, shifts)
    sends, keep = rest[:4], rest[4]
    order = (2, 1, 3)
    got = {turn: exchange(sends[turn], 1) for turn in order + (0,)}
    across = {}
    for turn in order:
        rides = masks[turn] in riders
        added = pl.pallas_call(
            functools.partial(add_kernel, turn),
            out_shape=longer if rides else piece,
            in_specs=[VMEM] * (3 if rides else 2),
            out_specs=VMEM,
            compiler_params=small,
        )(keep, got[turn], *([far_rim] if rides else []))
        across[turn] = exchange(added, masks[turn])
    single = len(inner[-1]) == 1
    direct = single and len(inner) == 1
    rides = across_mask in riders
    rows = part + plane if rides else part
    chunk = pl.pallas_call(
        functools.partial(sum_kernel, 4),
        out_shape=shape((rows, channels), BF16 if direct else F32),
        in_specs=[VMEM] * (6 if rides else 5),
        out_specs=VMEM,
        compiler_params=small,
    )(keep, got[0], *across.values(), *([far_rim] if rides else []))

    def places(group):
        own = sum(jnp.where(index & bit, 1 << n, 0) for n, bit in enumerate(group))
        others = []
        for turn in range(1, 1 << len(group)):
            others.append((sum(bit for n, bit in enumerate(group) if turn >> n & 1), own ^ turn))
        return own, others

    paired = inner[:-1] if single else inner
    for group in paired:
        own, others = places(group)
        size = chunk.shape[0] >> len(group)
        took = [exchange(block(chunk, there, size, BF16), mask) for mask, there in others]
        chunk = block(chunk, own, size, F32) + sum(g.astype(F32) for g in took)
    gathered = chunk.astype(BF16)
    if single:
        other = exchange(gathered, across_mask)
        gathered = pl.pallas_call(
            both_kernel,
            out_shape=piece if rides else shape(gathered.shape, BF16),
            in_specs=[VMEM] * 2,
            out_specs=VMEM,
            compiler_params=small,
        )(gathered, other)

    for group in reversed(paired):
        own, others = places(group)
        took = [(there, exchange(gathered, mask)) for mask, there in others]
        blocks = []
        for n in range(1 << len(group)):
            value = jnp.where(own == n, gathered, took[0][1])
            for there, other in took[1:]:
                value = jnp.where(there == n, other, value)
            blocks.append(value)
        gathered = jnp.concatenate(blocks, axis=0)
    pieces = {turn: exchange(gathered, masks[turn]) for turn in (2, 1, 3)}
    if riders:
        by_far = [across[2], across[3], other]
    else:
        by_far = [lax.ppermute(far_rim, "slab", far_route(count))]
    gradients = conv_back(riders, deltas, got[0], by_far, upstream)
    pieces[3], gradients = lax.optimization_barrier((pieces[3], gradients))
    ours = [gathered] + [pieces[turn] for turn in (1, 2, 3)]
    theirs = [exchange(piece, 1) for piece in ours]
    sums = [
        pl.pallas_call(
            norm_kernel,
            out_shape=shape((8, channels), F32),
            in_specs=[VMEM] * 4,
            out_specs=VMEM,
            compiler_params=small,
        )(*four)
        for four in (ours, theirs)
    ]
    sums += [cross(sums[0], back, mask) for back in range(1, segments) for mask in (0, 1)]
    bound = math.sqrt(27.0 * channels * channels * segments)
    update = pl.pallas_call(
        functools.partial(place_kernel, bound, segments),
        out_shape=jax.ShapeDtypeStruct((8, part, channels), F32),
        in_specs=[SMEM] + [VMEM] * (2 * segments + 8),
        out_specs=ANY,
        scratch_shapes=[pltpu.VMEM((8, part, channels), F32), pltpu.SemaphoreType.DMA((8,))],
        compiler_params=large,
    )((side * 4 + quarter).astype(jnp.int32).reshape(1), *sums, *ours, *theirs)
    gradients = gradients.reshape(1, micro, depth, width, height, channels)
    return (update.reshape(1, 8 * part, channels), gradients)


def solution(mesh):
    return jax.shard_map(
        shards,
        mesh=mesh,
        in_specs=(
            P("segment", None, "slab", None, None, None),
            P("segment", None, None),
            P(None, "slab", None, None, None),
        ),
        out_specs=(P("segment", None, None), P("segment", None, "slab", None, None, None)),
        check_vma=False,
    )
```

```python
import functools
import math

import jax
import jax.numpy as jnp
from jax import lax
from jax.experimental import pallas as pl
from jax.experimental.pallas import tpu as pltpu
from jax.sharding import PartitionSpec as P

BF16 = jnp.bfloat16
F32 = jnp.float32
VMEM = pl.BlockSpec(memory_space=pltpu.VMEM)
SMEM = pl.BlockSpec(memory_space=pltpu.SMEM)
ANY = pl.BlockSpec(memory_space=pl.ANY)
HBM = pl.BlockSpec(memory_space=pltpu.HBM)


def far_route(count):
    return [(i, ((i + 1) ^ 1) - 1) for i in range(1, count - 1)]


def swap(to_near, to_far):
    count = lax.axis_size("slab")
    near = [(i, i ^ 1) for i in range(count)]
    return lax.ppermute(to_near, "slab", near), lax.ppermute(to_far, "slab", far_route(count))


def cross_far(value):
    segments, count = lax.axis_size("segment"), lax.axis_size("slab")
    route = [
        (s * count + i, (s - 1) % segments * count + j)
        for s in range(segments)
        for i, j in far_route(count)
    ]
    return lax.ppermute(value, ("segment", "slab"), route)


def exchange(value, mask):
    count = lax.axis_size("slab")
    return lax.ppermute(value, "slab", [(i, i ^ mask) for i in range(count)])


def cross(value, back, mask):
    segments, count = lax.axis_size("segment"), lax.axis_size("slab")
    if back == 0 and mask == 0:
        return value
    route = [
        (s * count + i, (s - back) % segments * count + (i ^ mask))
        for s in range(segments)
        for i in range(count)
    ]
    return lax.ppermute(value, ("segment", "slab"), route)


def block(value, place, rows, dtype):
    return lax.dynamic_slice_in_dim(value, place * rows, rows, 0).astype(dtype)


def write_shifts(plane, height, out_ref, first):
    cells, channels = plane.shape
    width = cells // height
    rows = plane.astype(F32).reshape(width, height, channels)
    at = lax.broadcasted_iota(jnp.int32, rows.shape, 1)
    zero = jnp.zeros((1, height, channels), F32)
    before = jnp.where(at == 0, 0.0, pltpu.roll(rows, 1, 1))
    after = jnp.where(at == height - 1, 0.0, pltpu.roll(rows, height - 1, 1))
    for dy, moved in enumerate((before, rows, after)):
        for dx in range(3):
            if dx == 0:
                value = jnp.concatenate([zero, moved[:-1]], axis=0)
            elif dx == 1:
                value = moved
            else:
                value = jnp.concatenate([moved[1:], zero], axis=0)
            j = dx * 3 + dy
            out_ref[first : first + cells, j * channels : (j + 1) * channels] = value.reshape(
                cells, channels
            ).astype(BF16)


def back_product(shifts, mirror, block, depth):
    span = shifts.shape[1]
    total = None
    for dz in range(3):
        term = jnp.dot(
            shifts[dz * block : (dz + depth) * block, :],
            mirror[dz * span : (dz + 1) * span, :],
            preferred_element_type=F32,
        )
        total = term if total is None else total + term
    return total


def rim_kernel(acts, grad, near, far, sems):
    micro, depth = acts.shape[:2]
    top = 1 - lax.rem(lax.axis_index("slab"), 2)
    copies = []
    for which, (out, high) in enumerate(((near, top), (far, 1 - top))):
        for m in range(micro):
            for part, (source, size, at) in enumerate(((acts, 2, 0), (grad, 1, 2))):
                copies.append(
                    pltpu.make_async_copy(
                        source.at[m, pl.ds(high * (depth - size), size)],
                        out.at[m, at : at + size],
                        sems.at[which, m, part],
                    )
                )
    for copy in copies:
        copy.start()
    for copy in copies:
        copy.wait()


def own_kernel(
    height, stored_acts, stored_grad, stored, acts, grad, weight, mirror, part, own, sems
):
    micro, depth, cells, channels = acts.shape
    block, span = micro * cells, 9 * channels
    pairs = ((stored_acts, acts), (stored, weight), (stored_grad, grad))
    copies = [pltpu.make_async_copy(a, b, sems.at[n]) for n, (a, b) in enumerate(pairs)]
    for copy in copies:
        copy.start()
    copies[0].wait()
    for n in range(depth):
        for m in range(micro):
            write_shifts(acts[m, n], height, own, n * block + m * cells)
    copies[1].wait()
    copies[2].wait()
    part[...] = jnp.zeros(part.shape, F32)
    for dz in range(3):
        rows = slice((2 - dz) * block, (2 - dz + depth) * block)
        part[rows, :] += jnp.dot(
            own[...], weight[dz * span : (dz + 1) * span, :], preferred_element_type=F32
        )
    for k in range(27):
        mirror[(26 - k) * channels : (27 - k) * channels, :] = weight[
            k * channels : (k + 1) * channels, :
        ].T


def first_kernel(
    height, near, far, grad, weight, mirror, part, result, slopes, to_far, *refs
):
    rim, shifts = refs[-2:]
    micro, depth, cells, channels = grad.shape
    even = lax.rem(lax.axis_index("slab"), 2) == 0
    block, span = micro * cells, 9 * channels

    def pick(m, n, below):
        a, b = near[m, n].astype(F32), far[m, n].astype(F32)
        return jnp.where(even, b, a) if below else jnp.where(even, a, b)

    for n in range(4):
        for m in range(micro):
            write_shifts(pick(m, n % 2, n < 2), height, rim, n * block + m * cells)
    terms = [
        jnp.dot(
            rim[dz * block : (dz + 2) * block, :],
            weight[dz * span : (dz + 1) * span, :],
            preferred_element_type=F32,
        )
        for dz in range(3)
    ]
    head, tail = [term[:block] for term in terms], [term[block:] for term in terms]
    extra = {0: [head[0], head[1]], 1: [tail[0]]}
    extra.setdefault(depth, []).append(head[2])
    extra.setdefault(depth + 1, []).extend([tail[1], tail[2]])
    for n in range(depth + 2):
        rows = slice(n * block, (n + 1) * block)
        preact = part[rows, :]
        for term in extra.get(n, []):
            preact = preact + term
        sig = 1.0 / (1.0 + jnp.exp(-preact))
        slope = sig * (1.0 + preact * (1.0 - sig))
        slopes[rows, :] = slope
        for m in range(micro):
            if n == 0 or n == depth + 1:
                up = pick(m, 2, n == 0)
            else:
                up = grad[m, n - 1].astype(F32)
            delta = (up * slope[m * cells : (m + 1) * cells]).astype(BF16)
            write_shifts(delta, height, shifts, n * block + m * cells)
    back = back_product(shifts, mirror, block, depth)
    for m in range(micro):
        ends = []
        for n in range(depth):
            first = n * block + m * cells
            total = grad[m, n].astype(F32) + back[first : first + cells]
            result[m, n] = total.astype(BF16)
            if n in (0, depth - 1):
                ends.append(total)
        low, high = ends[0], ends[-1]
        for to_near in refs[:-2]:
            to_near[m, 0] = jnp.where(even, high, low).astype(BF16)
        to_far[m, 0] = jnp.where(even, low, high).astype(BF16)


def shift_kernel(height, acts, near, far, after, shifts):
    micro, depth, cells, _ = acts.shape
    even = lax.rem(lax.axis_index("slab"), 2) == 0
    for m in range(micro):
        below = jnp.where(even, far[m, 1].astype(F32), near[m, 1].astype(F32))
        above = jnp.where(even, near[m, 0].astype(F32), far[m, 0].astype(F32))
        planes = [below] + [acts[m, n] for n in range(depth)] + [above]
        for n, plane in enumerate(planes):
            write_shifts(plane, height, shifts, (n * micro + m) * cells)


def raw_kernel(
    spot, incoming, grad, far, slopes, shifts, upstream, deltas, far_slope, *refs
):
    sends, (keep, raw) = refs[:4], refs[4:]
    part = keep.shape[1]
    micro, depth, cells, channels = upstream.shape
    block, span = micro * cells, 9 * channels
    last = lax.axis_index("segment") == lax.axis_size("segment") - 1
    even = lax.rem(lax.axis_index("slab"), 2) == 0
    low, high = slice(0, block), slice((depth + 1) * block, (depth + 2) * block)
    slope = jnp.where(even, slopes[low, :], slopes[high, :])
    far_slope[...] = slope
    for m in range(micro):
        inside = slice(m * cells, (m + 1) * cells)
        rim = (far[m, 2].astype(F32) * slope[inside]).astype(BF16)
        for first in (low.start, high.start):
            deltas[first + m * cells : first + (m + 1) * cells, :] = rim
        planes = []
        for n in range(depth):
            up = jnp.where(last, grad[m, n].astype(F32), incoming[m, n].astype(F32))
            upstream[m, n] = up.astype(BF16)
            first = (n + 1) * block + m * cells
            delta = up * slopes[first : first + cells, :]
            deltas[first : first + cells, :] = delta.astype(BF16)
            planes.append(delta)
        first = part + m * cells
        sends[0][first : first + cells, :] = jnp.where(even, planes[-1], planes[0]).astype(BF16)
    for dz in range(3):
        total = None
        for n in range(depth):
            term = lax.dot_general(
                shifts[(dz + n) * block : (dz + n + 1) * block, :],
                deltas[(n + 1) * block : (n + 2) * block, :],
                (((0,), (0,)), ((), ())),
                preferred_element_type=F32,
            )
            total = term if total is None else total + term
        raw[dz * span : (dz + 1) * span, :] = total
    for turn in range(4):
        keep[turn] = raw[pl.ds((spot[0] ^ turn) * part, part), :]
        sends[turn][:part, :] = raw[pl.ds((spot[0] ^ turn ^ 4) * part, part), :].astype(BF16)


def add_kernel(turn, keep, got, out):
    out[...] = (keep[turn] + got[...].astype(F32)).astype(BF16)


def sum_kernel(keep, *refs):
    total = keep[0]
    for got in refs[:-1]:
        total = total + got[: total.shape[0], :].astype(F32)
    refs[-1][...] = total.astype(refs[-1].dtype)


def both_kernel(mine, other, out):
    out[...] = (mine[...].astype(F32) + other[...].astype(F32)).astype(BF16)


def column_squares(value):
    value = value.astype(F32)
    return jnp.sum(value * value, axis=0, keepdims=True)


def norm_kernel(*refs):
    sums = [column_squares(piece[...]) for piece in refs[:-1]]
    while len(sums) > 1:
        sums = [a + b for a, b in zip(sums[::2], sums[1::2], strict=True)]
    refs[-1][...] = jnp.broadcast_to(sums[0], refs[-1].shape)


def back_kernel(
    height, deltas, by_near, in_far, far_slope, upstream, mirror, out, shifts
):
    micro, depth, cells, channels = upstream.shape
    block = micro * cells
    last = lax.axis_index("segment") == lax.axis_size("segment") - 1
    even = lax.rem(lax.axis_index("slab"), 2) == 0
    start = by_near.shape[0] - block
    for m in range(micro):
        inside = slice(m * cells, (m + 1) * cells)
        near = by_near[start + m * cells : start + (m + 1) * cells, :].astype(F32)
        far = (in_far[m, 0].astype(F32) * far_slope[inside, :]).astype(BF16).astype(F32)
        far = jnp.where(last, deltas[inside, :].astype(F32), far)
        write_shifts(jnp.where(even, far, near), height, shifts, m * cells)
        first = (depth + 1) * block + m * cells
        write_shifts(jnp.where(even, near, far), height, shifts, first)
        for n in range(1, depth + 1):
            first = n * block + m * cells
            write_shifts(deltas[first : first + cells, :], height, shifts, first)
    back = back_product(shifts, mirror, block, depth)
    for m in range(micro):
        for n in range(depth):
            first = n * block + m * cells
            total = upstream[m, n].astype(F32) + back[first : first + cells]
            out[m, n] = total.astype(BF16)


def place_kernel(bound, count, spot, *refs):
    sums, pieces, (out, scaled, sems) = refs[: 2 * count], refs[2 * count : -3], refs[-3:]
    mine, other = (sum(value[:1, :] for value in sums[side::2]) for side in range(2))
    squares = mine + other
    norm = jnp.sqrt(jnp.sum(squares, axis=1, keepdims=True))
    factor = jnp.minimum(1.0, bound / (norm + 1e-06))
    copies = []
    for n, piece in enumerate(pieces):
        scaled[n] = piece[...].astype(F32) * factor
        copies.append(pltpu.make_async_copy(scaled.at[n], out.at[spot[0] ^ n], sems.at[n]))
        copies[-1].start()
    for copy in copies:
        copy.wait()


def shards(activations, weights, out_grad):
    weight = weights[0]
    channels = weight.shape[1]
    micro, depth, width, height = activations.shape[1:5]
    cells = width * height
    acts = activations[0].reshape(micro, depth, cells, channels)
    grad = out_grad.reshape(micro, depth, cells, channels)
    rows = depth * cells
    segments = lax.axis_size("segment")
    count = lax.axis_size("slab")
    index = lax.axis_index("slab")
    last = lax.axis_index("segment") == segments - 1
    large = pltpu.CompilerParams(vmem_limit_bytes=16 << 20)
    small = pltpu.CompilerParams(vmem_limit_bytes=4 << 20)

    shape = jax.ShapeDtypeStruct
    rim = shape((micro, 3, cells, channels), BF16)
    volume = shape((micro, depth, cells, channels), BF16)
    acts, grad = (pltpu.with_memory_space_constraint(a, pltpu.HBM) for a in (acts, grad))
    to_near, to_far = pl.pallas_call(
        rim_kernel,
        out_shape=(rim, rim),
        in_specs=[HBM, HBM],
        out_specs=(VMEM,) * 2,
        scratch_shapes=[pltpu.SemaphoreType.DMA((2, micro, 2))],
        compiler_params=small,
    )(acts, grad)
    near, far = swap(to_near, to_far)

    plane, span = micro * cells, 9 * channels
    whole = shape(weight.shape, BF16)
    outer = shape(((depth + 2) * plane, channels), F32)
    stored = acts, grad, pltpu.with_memory_space_constraint(weight, pltpu.HBM)
    acts, grad, weight, mirror, part = pl.pallas_call(
        functools.partial(own_kernel, height),
        out_shape=(volume, volume, whole, whole, outer),
        in_specs=[HBM] * 3,
        out_specs=(VMEM,) * 5,
        scratch_shapes=[
            pltpu.VMEM((depth * plane, span), BF16),
            pltpu.SemaphoreType.DMA((3,)),
        ],
        compiler_params=large,
    )(*stored)

    edge = shape((micro, 1, cells, channels), BF16)
    wide = pltpu.VMEM(((depth + 2) * plane, span), BF16)
    edges = (edge,) * (1 if segments == 2 else 2)
    result, slopes, to_far, *to_near = pl.pallas_call(
        functools.partial(first_kernel, height),
        out_shape=(volume, outer) + edges,
        in_specs=[VMEM] * 6,
        out_specs=(VMEM,) * (2 + len(edges)),
        scratch_shapes=[pltpu.VMEM((4 * plane, span), BF16), wide],
        compiler_params=large,
    )(near, far, grad, weight, mirror, part)

    def conv_back(deltas, by_near, in_far, far_slope, upstream):
        return pl.pallas_call(
            functools.partial(back_kernel, height),
            out_shape=volume,
            in_specs=[VMEM] * 6,
            out_specs=VMEM,
            scratch_shapes=[wide],
            compiler_params=large,
        )(deltas, by_near, in_far, far_slope, upstream, mirror)

    part = weight.shape[0] // 8
    even = lax.rem(index, 2) == 0
    for step in range(1, segments - 1):
        incoming, in_near, in_far = cross(result, 1, 0), cross(to_near[0], 1, 1), cross_far(to_far)
        upstream = jnp.where(last, grad, incoming)
        stacked = jnp.swapaxes(upstream, 0, 1).reshape(depth * plane, channels).astype(F32)
        deltas = (stacked * slopes[plane:-plane]).astype(BF16)
        near_slope = jnp.where(even, slopes[-plane:], slopes[:plane])
        far_slope = jnp.where(even, slopes[:plane], slopes[-plane:])
        by_near = jnp.where(last, near[:, 2:], in_near).reshape(plane, channels).astype(F32)
        rim = (far[:, 2:].reshape(plane, channels).astype(F32) * far_slope).astype(BF16)
        deltas = jnp.concatenate([rim, deltas, rim], axis=0)
        result = conv_back(
            deltas, (by_near * near_slope).astype(BF16), in_far, far_slope, upstream
        )
        low, high = result[:, :1], result[:, -1:]
        to_near, to_far = [jnp.where(even, high, low)], jnp.where(even, low, high)
    incoming = cross(result, 1, 0)
    shifts = pl.pallas_call(
        functools.partial(shift_kernel, height),
        out_shape=shape(((depth + 2) * plane, span), BF16),
        in_specs=[VMEM] * 4,
        out_specs=VMEM,
        compiler_params=large,
    )(acts, near, far, result)
    bits = [1 << n for n in range(1, count.bit_length() - 1)]
    inner = [bits[n : n + 2] for n in range(2, len(bits), 2)]
    crossing = inner[-1][0] if len(inner[-1]) == 1 else 0
    side = lax.rem(index, 2)
    quarter = jnp.where(index & 2, 2, 0) + jnp.where(index & 4, 1, 0)
    masks = {1: 4, 2: 2, 3: 6}
    spot = (side * 4 + quarter).astype(jnp.int32).reshape(1)
    piece = shape((part, channels), BF16)

    upstream, deltas, far_slope, *rest = pl.pallas_call(
        raw_kernel,
        out_shape=(
            volume,
            shape(outer.shape, BF16),
            shape((plane, channels), F32),
            shape((part + plane, channels), BF16),
            piece,
            piece,
            piece,
            shape((4, part, channels), F32),
        ),
        in_specs=[SMEM] + [VMEM] * 5,
        out_specs=(VMEM,) * 8,
        scratch_shapes=[pltpu.VMEM((8 * part, channels), F32)],
        compiler_params=large,
    )(spot, incoming, grad, far, slopes, shifts)
    sends, keep = rest[:4], rest[4]
    order = (2, 1, 3)
    got = {turn: exchange(sends[turn], 1) for turn in order + (0,)}
    across = []
    for turn in order:
        added = pl.pallas_call(
            functools.partial(add_kernel, turn),
            out_shape=piece,
            in_specs=[VMEM] * 2,
            out_specs=VMEM,
            compiler_params=small,
        )(keep, got[turn])
        if turn == order[-1]:
            added, to_far = lax.optimization_barrier((added, to_far))
        across.append(exchange(added, masks[turn]))
    in_far = cross_far(to_far)
    across[2], in_far = lax.optimization_barrier((across[2], in_far))
    gradients = conv_back(deltas, got[0], in_far, far_slope, upstream)
    single = len(inner[-1]) == 1
    direct = single and len(inner) == 1
    chunk = pl.pallas_call(
        sum_kernel,
        out_shape=shape((part, channels), BF16 if direct else F32),
        in_specs=[VMEM] * 5,
        out_specs=VMEM,
        compiler_params=small,
    )(keep, got[0], *across)

    def places(group):
        own = sum(jnp.where(index & bit, 1 << n, 0) for n, bit in enumerate(group))
        others = []
        for turn in range(1, 1 << len(group)):
            others.append((sum(bit for n, bit in enumerate(group) if turn >> n & 1), own ^ turn))
        return own, others

    paired = inner[:-1] if single else inner
    for group in paired:
        own, others = places(group)
        size = chunk.shape[0] >> len(group)
        took = [exchange(block(chunk, there, size, BF16), mask) for mask, there in others]
        chunk = block(chunk, own, size, F32) + sum(g.astype(F32) for g in took)
    gathered = chunk.astype(BF16)
    if single:
        other = exchange(gathered, crossing)
        other, gradients = lax.optimization_barrier((other, gradients))
        gathered = pl.pallas_call(
            both_kernel,
            out_shape=shape(gathered.shape, BF16),
            in_specs=[VMEM] * 2,
            out_specs=VMEM,
            compiler_params=small,
        )(gathered, other)

    for group in reversed(paired):
        own, others = places(group)
        took = [(there, exchange(gathered, mask)) for mask, there in others]
        blocks = []
        for n in range(1 << len(group)):
            value = jnp.where(own == n, gathered, took[0][1])
            for there, other in took[1:]:
                value = jnp.where(there == n, other, value)
            blocks.append(value)
        gathered = jnp.concatenate(blocks, axis=0)
    pieces = {turn: exchange(gathered, masks[turn]) for turn in (2, 1, 3)}
    ours = [gathered] + [pieces[turn] for turn in (1, 2, 3)]
    theirs = [exchange(piece, 1) for piece in ours]
    sums = [
        pl.pallas_call(
            norm_kernel,
            out_shape=shape((8, channels), F32),
            in_specs=[VMEM] * 4,
            out_specs=VMEM,
            compiler_params=small,
        )(*four)
        for four in (ours, theirs)
    ]
    sums += [cross(sums[0], back, mask) for back in range(1, segments) for mask in (0, 1)]
    bound = math.sqrt(27.0 * channels * channels * segments)
    update = pl.pallas_call(
        functools.partial(place_kernel, bound, segments),
        out_shape=jax.ShapeDtypeStruct((8, part, channels), F32),
        in_specs=[SMEM] + [VMEM] * (2 * segments + 8),
        out_specs=ANY,
        scratch_shapes=[pltpu.VMEM((8, part, channels), F32), pltpu.SemaphoreType.DMA((8,))],
        compiler_params=large,
    )((side * 4 + quarter).astype(jnp.int32).reshape(1), *sums, *ours, *theirs)
    gradients = gradients.reshape(1, micro, depth, width, height, channels)
    return (update.reshape(1, 8 * part, channels), gradients)


def solution(mesh):
    return jax.shard_map(
        shards,
        mesh=mesh,
        in_specs=(
            P("segment", None, "slab", None, None, None),
            P("segment", None, None),
            P(None, "slab", None, None, None),
        ),
        out_specs=(P("segment", None, None), P("segment", None, "slab", None, None, None)),
        check_vma=False,
    )
```

```python
import functools
import math

import jax
import jax.numpy as jnp
from jax import lax
from jax.experimental import pallas as pl
from jax.experimental.pallas import tpu as pltpu
from jax.sharding import PartitionSpec as P

BF16 = jnp.bfloat16
F32 = jnp.float32
VMEM = pl.BlockSpec(memory_space=pltpu.VMEM)
SMEM = pl.BlockSpec(memory_space=pltpu.SMEM)
ANY = pl.BlockSpec(memory_space=pl.ANY)
HBM = pl.BlockSpec(memory_space=pltpu.HBM)


def far_route(count):
    return [(i, ((i + 1) ^ 1) - 1) for i in range(1, count - 1)]


def swap(to_near, to_far):
    count = lax.axis_size("slab")
    near = [(i, i ^ 1) for i in range(count)]
    return lax.ppermute(to_near, "slab", near), lax.ppermute(to_far, "slab", far_route(count))


def cross_far(value):
    segments, count = lax.axis_size("segment"), lax.axis_size("slab")
    route = [
        (s * count + i, (s - 1) % segments * count + j)
        for s in range(segments)
        for i, j in far_route(count)
    ]
    return lax.ppermute(value, ("segment", "slab"), route)


def exchange(value, mask):
    count = lax.axis_size("slab")
    return lax.ppermute(value, "slab", [(i, i ^ mask) for i in range(count)])


def cross(value, back, mask):
    segments, count = lax.axis_size("segment"), lax.axis_size("slab")
    if back == 0 and mask == 0:
        return value
    route = [
        (s * count + i, (s - back) % segments * count + (i ^ mask))
        for s in range(segments)
        for i in range(count)
    ]
    return lax.ppermute(value, ("segment", "slab"), route)


def block(value, place, rows, dtype):
    return lax.dynamic_slice_in_dim(value, place * rows, rows, 0).astype(dtype)


def write_shifts(plane, height, out_ref, first):
    cells, channels = plane.shape
    width = cells // height
    rows = plane.astype(F32).reshape(width, height, channels)
    at = lax.broadcasted_iota(jnp.int32, rows.shape, 1)
    zero = jnp.zeros((1, height, channels), F32)
    before = jnp.where(at == 0, 0.0, pltpu.roll(rows, 1, 1))
    after = jnp.where(at == height - 1, 0.0, pltpu.roll(rows, height - 1, 1))
    for dy, moved in enumerate((before, rows, after)):
        for dx in range(3):
            if dx == 0:
                value = jnp.concatenate([zero, moved[:-1]], axis=0)
            elif dx == 1:
                value = moved
            else:
                value = jnp.concatenate([moved[1:], zero], axis=0)
            j = dx * 3 + dy
            out_ref[first : first + cells, j * channels : (j + 1) * channels] = value.reshape(
                cells, channels
            ).astype(BF16)


def back_product(shifts, mirror, block, depth):
    span = shifts.shape[1]
    total = None
    for dz in range(3):
        term = jnp.dot(
            shifts[dz * block : (dz + depth) * block, :],
            mirror[dz * span : (dz + 1) * span, :],
            preferred_element_type=F32,
        )
        total = term if total is None else total + term
    return total


def rim_kernel(acts, grad, near, far, sems):
    micro, depth = acts.shape[:2]
    top = 1 - lax.rem(lax.axis_index("slab"), 2)
    copies = []
    for which, (out, high) in enumerate(((near, top), (far, 1 - top))):
        for m in range(micro):
            for part, (source, size, at) in enumerate(((acts, 2, 0), (grad, 1, 2))):
                copies.append(
                    pltpu.make_async_copy(
                        source.at[m, pl.ds(high * (depth - size), size)],
                        out.at[m, at : at + size],
                        sems.at[which, m, part],
                    )
                )
    for copy in copies:
        copy.start()
    for copy in copies:
        copy.wait()


def own_kernel(
    height, stored_acts, stored_grad, stored, acts, grad, weight, mirror, part, own, sems
):
    micro, depth, cells, channels = acts.shape
    block, span = micro * cells, 9 * channels
    pairs = ((stored_acts, acts), (stored, weight), (stored_grad, grad))
    copies = [pltpu.make_async_copy(a, b, sems.at[n]) for n, (a, b) in enumerate(pairs)]
    for copy in copies:
        copy.start()
    copies[0].wait()
    for n in range(depth):
        for m in range(micro):
            write_shifts(acts[m, n], height, own, n * block + m * cells)
    copies[1].wait()
    copies[2].wait()
    part[...] = jnp.zeros(part.shape, F32)
    for dz in range(3):
        rows = slice((2 - dz) * block, (2 - dz + depth) * block)
        part[rows, :] += jnp.dot(
            own[...], weight[dz * span : (dz + 1) * span, :], preferred_element_type=F32
        )
    for k in range(27):
        mirror[(26 - k) * channels : (27 - k) * channels, :] = weight[
            k * channels : (k + 1) * channels, :
        ].T


def first_kernel(
    height, near, far, grad, weight, mirror, part, result, slopes, to_far, *refs
):
    rim, shifts = refs[-2:]
    micro, depth, cells, channels = grad.shape
    even = lax.rem(lax.axis_index("slab"), 2) == 0
    block, span = micro * cells, 9 * channels

    def pick(m, n, below):
        a, b = near[m, n].astype(F32), far[m, n].astype(F32)
        return jnp.where(even, b, a) if below else jnp.where(even, a, b)

    for n in range(4):
        for m in range(micro):
            write_shifts(pick(m, n % 2, n < 2), height, rim, n * block + m * cells)
    terms = [
        jnp.dot(
            rim[dz * block : (dz + 2) * block, :],
            weight[dz * span : (dz + 1) * span, :],
            preferred_element_type=F32,
        )
        for dz in range(3)
    ]
    head, tail = [term[:block] for term in terms], [term[block:] for term in terms]
    extra = {0: [head[0], head[1]], 1: [tail[0]]}
    extra.setdefault(depth, []).append(head[2])
    extra.setdefault(depth + 1, []).extend([tail[1], tail[2]])
    for n in range(depth + 2):
        rows = slice(n * block, (n + 1) * block)
        preact = part[rows, :]
        for term in extra.get(n, []):
            preact = preact + term
        sig = 1.0 / (1.0 + jnp.exp(-preact))
        slope = sig * (1.0 + preact * (1.0 - sig))
        slopes[rows, :] = slope
        for m in range(micro):
            if n == 0 or n == depth + 1:
                up = pick(m, 2, n == 0)
            else:
                up = grad[m, n - 1].astype(F32)
            delta = (up * slope[m * cells : (m + 1) * cells]).astype(BF16)
            write_shifts(delta, height, shifts, n * block + m * cells)
    back = back_product(shifts, mirror, block, depth)
    for m in range(micro):
        ends = []
        for n in range(depth):
            first = n * block + m * cells
            total = grad[m, n].astype(F32) + back[first : first + cells]
            result[m, n] = total.astype(BF16)
            if n in (0, depth - 1):
                ends.append(total)
        low, high = ends[0], ends[-1]
        for to_near in refs[:-2]:
            to_near[m, 0] = jnp.where(even, high, low).astype(BF16)
        to_far[m, 0] = jnp.where(even, low, high).astype(BF16)


def shift_kernel(height, acts, near, far, after, shifts):
    micro, depth, cells, _ = acts.shape
    even = lax.rem(lax.axis_index("slab"), 2) == 0
    for m in range(micro):
        below = jnp.where(even, far[m, 1].astype(F32), near[m, 1].astype(F32))
        above = jnp.where(even, near[m, 0].astype(F32), far[m, 0].astype(F32))
        planes = [below] + [acts[m, n] for n in range(depth)] + [above]
        for n, plane in enumerate(planes):
            write_shifts(plane, height, shifts, (n * micro + m) * cells)


def raw_kernel(
    spot, incoming, grad, far, slopes, shifts, upstream, deltas, far_slope, *refs
):
    sends, (keep, raw) = refs[:4], refs[4:]
    part = keep.shape[1]
    micro, depth, cells, channels = upstream.shape
    block, span = micro * cells, 9 * channels
    last = lax.axis_index("segment") == lax.axis_size("segment") - 1
    even = lax.rem(lax.axis_index("slab"), 2) == 0
    low, high = slice(0, block), slice((depth + 1) * block, (depth + 2) * block)
    slope = jnp.where(even, slopes[low, :], slopes[high, :])
    far_slope[...] = slope
    for m in range(micro):
        inside = slice(m * cells, (m + 1) * cells)
        rim = (far[m, 2].astype(F32) * slope[inside]).astype(BF16)
        for first in (low.start, high.start):
            deltas[first + m * cells : first + (m + 1) * cells, :] = rim
        planes = []
        for n in range(depth):
            up = jnp.where(last, grad[m, n].astype(F32), incoming[m, n].astype(F32))
            upstream[m, n] = up.astype(BF16)
            first = (n + 1) * block + m * cells
            delta = up * slopes[first : first + cells, :]
            deltas[first : first + cells, :] = delta.astype(BF16)
            planes.append(delta)
        first = part + m * cells
        sends[0][first : first + cells, :] = jnp.where(even, planes[-1], planes[0]).astype(BF16)
    for dz in range(3):
        total = None
        for n in range(depth):
            term = lax.dot_general(
                shifts[(dz + n) * block : (dz + n + 1) * block, :],
                deltas[(n + 1) * block : (n + 2) * block, :],
                (((0,), (0,)), ((), ())),
                preferred_element_type=F32,
            )
            total = term if total is None else total + term
        raw[dz * span : (dz + 1) * span, :] = total
    for turn in range(4):
        keep[turn] = raw[pl.ds((spot[0] ^ turn) * part, part), :]
        sends[turn][:part, :] = raw[pl.ds((spot[0] ^ turn ^ 4) * part, part), :].astype(BF16)


def add_kernel(turn, keep, got, out):
    out[...] = (keep[turn] + got[...].astype(F32)).astype(BF16)


def sum_kernel(keep, *refs):
    total = keep[0]
    for got in refs[:-1]:
        total = total + got[: total.shape[0], :].astype(F32)
    refs[-1][...] = total.astype(refs[-1].dtype)


def both_kernel(mine, other, out):
    out[...] = (mine[...].astype(F32) + other[...].astype(F32)).astype(BF16)


def column_squares(value):
    value = value.astype(F32)
    return jnp.sum(value * value, axis=0, keepdims=True)


def norm_kernel(*refs):
    sums = [column_squares(piece[...]) for piece in refs[:-1]]
    while len(sums) > 1:
        sums = [a + b for a, b in zip(sums[::2], sums[1::2], strict=True)]
    refs[-1][...] = jnp.broadcast_to(sums[0], refs[-1].shape)


def back_kernel(
    height, deltas, by_near, in_far, far_slope, upstream, mirror, out, shifts
):
    micro, depth, cells, channels = upstream.shape
    block = micro * cells
    last = lax.axis_index("segment") == lax.axis_size("segment") - 1
    even = lax.rem(lax.axis_index("slab"), 2) == 0
    start = by_near.shape[0] - block
    for m in range(micro):
        inside = slice(m * cells, (m + 1) * cells)
        near = by_near[start + m * cells : start + (m + 1) * cells, :].astype(F32)
        far = (in_far[m, 0].astype(F32) * far_slope[inside, :]).astype(BF16).astype(F32)
        far = jnp.where(last, deltas[inside, :].astype(F32), far)
        write_shifts(jnp.where(even, far, near), height, shifts, m * cells)
        first = (depth + 1) * block + m * cells
        write_shifts(jnp.where(even, near, far), height, shifts, first)
        for n in range(1, depth + 1):
            first = n * block + m * cells
            write_shifts(deltas[first : first + cells, :], height, shifts, first)
    back = back_product(shifts, mirror, block, depth)
    for m in range(micro):
        for n in range(depth):
            first = n * block + m * cells
            total = upstream[m, n].astype(F32) + back[first : first + cells]
            out[m, n] = total.astype(BF16)


def place_kernel(bound, count, spot, *refs):
    sums, pieces, (out, scaled, sems) = refs[: 2 * count], refs[2 * count : -3], refs[-3:]
    mine, other = (sum(value[:1, :] for value in sums[side::2]) for side in range(2))
    squares = mine + other
    norm = jnp.sqrt(jnp.sum(squares, axis=1, keepdims=True))
    factor = jnp.minimum(1.0, bound / (norm + 1e-06))
    copies = []
    for n, piece in enumerate(pieces):
        scaled[n] = piece[...].astype(F32) * factor
        copies.append(pltpu.make_async_copy(scaled.at[n], out.at[spot[0] ^ n], sems.at[n]))
        copies[-1].start()
    for copy in copies:
        copy.wait()


def shards(activations, weights, out_grad):
    weight = weights[0]
    channels = weight.shape[1]
    micro, depth, width, height = activations.shape[1:5]
    cells = width * height
    acts = activations[0].reshape(micro, depth, cells, channels)
    grad = out_grad.reshape(micro, depth, cells, channels)
    rows = depth * cells
    segments = lax.axis_size("segment")
    count = lax.axis_size("slab")
    index = lax.axis_index("slab")
    last = lax.axis_index("segment") == segments - 1
    large = pltpu.CompilerParams(vmem_limit_bytes=16 << 20)
    small = pltpu.CompilerParams(vmem_limit_bytes=4 << 20)

    shape = jax.ShapeDtypeStruct
    rim = shape((micro, 3, cells, channels), BF16)
    volume = shape((micro, depth, cells, channels), BF16)
    acts, grad = (pltpu.with_memory_space_constraint(a, pltpu.HBM) for a in (acts, grad))
    to_near, to_far = pl.pallas_call(
        rim_kernel,
        out_shape=(rim, rim),
        in_specs=[HBM, HBM],
        out_specs=(VMEM,) * 2,
        scratch_shapes=[pltpu.SemaphoreType.DMA((2, micro, 2))],
        compiler_params=small,
    )(acts, grad)
    near, far = swap(to_near, to_far)

    plane, span = micro * cells, 9 * channels
    whole = shape(weight.shape, BF16)
    outer = shape(((depth + 2) * plane, channels), F32)
    stored = acts, grad, pltpu.with_memory_space_constraint(weight, pltpu.HBM)
    acts, grad, weight, mirror, part = pl.pallas_call(
        functools.partial(own_kernel, height),
        out_shape=(volume, volume, whole, whole, outer),
        in_specs=[HBM] * 3,
        out_specs=(VMEM,) * 5,
        scratch_shapes=[
            pltpu.VMEM((depth * plane, span), BF16),
            pltpu.SemaphoreType.DMA((3,)),
        ],
        compiler_params=large,
    )(*stored)

    edge = shape((micro, 1, cells, channels), BF16)
    wide = pltpu.VMEM(((depth + 2) * plane, span), BF16)
    edges = (edge,) * (1 if segments == 2 else 2)
    result, slopes, to_far, *to_near = pl.pallas_call(
        functools.partial(first_kernel, height),
        out_shape=(volume, outer) + edges,
        in_specs=[VMEM] * 6,
        out_specs=(VMEM,) * (2 + len(edges)),
        scratch_shapes=[pltpu.VMEM((4 * plane, span), BF16), wide],
        compiler_params=large,
    )(near, far, grad, weight, mirror, part)

    def conv_back(deltas, by_near, in_far, far_slope, upstream):
        return pl.pallas_call(
            functools.partial(back_kernel, height),
            out_shape=volume,
            in_specs=[VMEM] * 6,
            out_specs=VMEM,
            scratch_shapes=[wide],
            compiler_params=large,
        )(deltas, by_near, in_far, far_slope, upstream, mirror)

    part = weight.shape[0] // 8
    even = lax.rem(index, 2) == 0
    for step in range(1, segments - 1):
        incoming, in_near, in_far = cross(result, 1, 0), cross(to_near[0], 1, 1), cross_far(to_far)
        upstream = jnp.where(last, grad, incoming)
        stacked = jnp.swapaxes(upstream, 0, 1).reshape(depth * plane, channels).astype(F32)
        deltas = (stacked * slopes[plane:-plane]).astype(BF16)
        near_slope = jnp.where(even, slopes[-plane:], slopes[:plane])
        far_slope = jnp.where(even, slopes[:plane], slopes[-plane:])
        by_near = jnp.where(last, near[:, 2:], in_near).reshape(plane, channels).astype(F32)
        rim = (far[:, 2:].reshape(plane, channels).astype(F32) * far_slope).astype(BF16)
        deltas = jnp.concatenate([rim, deltas, rim], axis=0)
        result = conv_back(
            deltas, (by_near * near_slope).astype(BF16), in_far, far_slope, upstream
        )
        low, high = result[:, :1], result[:, -1:]
        to_near, to_far = [jnp.where(even, high, low)], jnp.where(even, low, high)
    incoming = cross(result, 1, 0)
    shifts = pl.pallas_call(
        functools.partial(shift_kernel, height),
        out_shape=shape(((depth + 2) * plane, span), BF16),
        in_specs=[VMEM] * 4,
        out_specs=VMEM,
        compiler_params=large,
    )(acts, near, far, result)
    bits = [1 << n for n in range(1, count.bit_length() - 1)]
    inner = [bits[n : n + 2] for n in range(2, len(bits), 2)]
    crossing = inner[-1][0] if len(inner[-1]) == 1 else 0
    side = lax.rem(index, 2)
    quarter = jnp.where(index & 2, 2, 0) + jnp.where(index & 4, 1, 0)
    masks = {1: 4, 2: 2, 3: 6}
    spot = (side * 4 + quarter).astype(jnp.int32).reshape(1)
    piece = shape((part, channels), BF16)

    upstream, deltas, far_slope, *rest = pl.pallas_call(
        raw_kernel,
        out_shape=(
            volume,
            shape(outer.shape, BF16),
            shape((plane, channels), F32),
            shape((part + plane, channels), BF16),
            piece,
            piece,
            piece,
            shape((4, part, channels), F32),
        ),
        in_specs=[SMEM] + [VMEM] * 5,
        out_specs=(VMEM,) * 8,
        scratch_shapes=[pltpu.VMEM((8 * part, channels), F32)],
        compiler_params=large,
    )(spot, incoming, grad, far, slopes, shifts)
    sends, keep = rest[:4], rest[4]
    order = (1, 2, 3)
    got = {turn: exchange(sends[turn], 1) for turn in order + (0,)}
    across = []
    for turn in order:
        added = pl.pallas_call(
            functools.partial(add_kernel, turn),
            out_shape=piece,
            in_specs=[VMEM] * 2,
            out_specs=VMEM,
            compiler_params=small,
        )(keep, got[turn])
        across.append(exchange(added, masks[turn]))
    in_far = cross_far(to_far)
    across[2], in_far = lax.optimization_barrier((across[2], in_far))
    gradients = conv_back(deltas, got[0], in_far, far_slope, upstream)
    single = len(inner[-1]) == 1
    direct = single and len(inner) == 1
    chunk = pl.pallas_call(
        sum_kernel,
        out_shape=shape((part, channels), BF16 if direct else F32),
        in_specs=[VMEM] * 5,
        out_specs=VMEM,
        compiler_params=small,
    )(keep, got[0], *across)

    def places(group):
        own = sum(jnp.where(index & bit, 1 << n, 0) for n, bit in enumerate(group))
        others = []
        for turn in range(1, 1 << len(group)):
            others.append((sum(bit for n, bit in enumerate(group) if turn >> n & 1), own ^ turn))
        return own, others

    paired = inner[:-1] if single else inner
    for group in paired:
        own, others = places(group)
        size = chunk.shape[0] >> len(group)
        took = [exchange(block(chunk, there, size, BF16), mask) for mask, there in others]
        chunk = block(chunk, own, size, F32) + sum(g.astype(F32) for g in took)
    gathered = chunk.astype(BF16)
    if single:
        other = exchange(gathered, crossing)
        other, gradients = lax.optimization_barrier((other, gradients))
        gathered = pl.pallas_call(
            both_kernel,
            out_shape=shape(gathered.shape, BF16),
            in_specs=[VMEM] * 2,
            out_specs=VMEM,
            compiler_params=small,
        )(gathered, other)

    for group in reversed(paired):
        own, others = places(group)
        took = [(there, exchange(gathered, mask)) for mask, there in others]
        blocks = []
        for n in range(1 << len(group)):
            value = jnp.where(own == n, gathered, took[0][1])
            for there, other in took[1:]:
                value = jnp.where(there == n, other, value)
            blocks.append(value)
        gathered = jnp.concatenate(blocks, axis=0)
    pieces = {turn: exchange(gathered, masks[turn]) for turn in (1, 2, 3)}
    ours = [gathered] + [pieces[turn] for turn in (1, 2, 3)]
    theirs = [exchange(piece, 1) for piece in ours]
    sums = [
        pl.pallas_call(
            norm_kernel,
            out_shape=shape((8, channels), F32),
            in_specs=[VMEM] * 4,
            out_specs=VMEM,
            compiler_params=small,
        )(*four)
        for four in (ours, theirs)
    ]
    sums += [cross(sums[0], back, mask) for back in range(1, segments) for mask in (0, 1)]
    bound = math.sqrt(27.0 * channels * channels * segments)
    update = pl.pallas_call(
        functools.partial(place_kernel, bound, segments),
        out_shape=jax.ShapeDtypeStruct((8, part, channels), F32),
        in_specs=[SMEM] + [VMEM] * (2 * segments + 8),
        out_specs=ANY,
        scratch_shapes=[pltpu.VMEM((8, part, channels), F32), pltpu.SemaphoreType.DMA((8,))],
        compiler_params=large,
    )((side * 4 + quarter).astype(jnp.int32).reshape(1), *sums, *ours, *theirs)
    gradients = gradients.reshape(1, micro, depth, width, height, channels)
    return (update.reshape(1, 8 * part, channels), gradients)


def solution(mesh):
    return jax.shard_map(
        shards,
        mesh=mesh,
        in_specs=(
            P("segment", None, "slab", None, None, None),
            P("segment", None, None),
            P(None, "slab", None, None, None),
        ),
        out_specs=(P("segment", None, None), P("segment", None, "slab", None, None, None)),
        check_vma=False,
    )
```

```python
import functools
import math

import jax
import jax.numpy as jnp
from jax import lax
from jax.experimental import pallas as pl
from jax.experimental.pallas import tpu as pltpu
from jax.sharding import PartitionSpec as P

BF16 = jnp.bfloat16
F32 = jnp.float32
VMEM = pl.BlockSpec(memory_space=pltpu.VMEM)
SMEM = pl.BlockSpec(memory_space=pltpu.SMEM)
ANY = pl.BlockSpec(memory_space=pl.ANY)
HBM = pl.BlockSpec(memory_space=pltpu.HBM)


def far_route(count):
    return [(i, ((i + 1) ^ 1) - 1) for i in range(1, count - 1)]


def swap(to_near, to_far):
    count = lax.axis_size("slab")
    near = [(i, i ^ 1) for i in range(count)]
    return lax.ppermute(to_near, "slab", near), lax.ppermute(to_far, "slab", far_route(count))


def cross_far(value):
    segments, count = lax.axis_size("segment"), lax.axis_size("slab")
    route = [
        (s * count + i, (s - 1) % segments * count + j)
        for s in range(segments)
        for i, j in far_route(count)
    ]
    return lax.ppermute(value, ("segment", "slab"), route)


def exchange(value, mask):
    count = lax.axis_size("slab")
    return lax.ppermute(value, "slab", [(i, i ^ mask) for i in range(count)])


def cross(value, back, mask):
    segments, count = lax.axis_size("segment"), lax.axis_size("slab")
    if back == 0 and mask == 0:
        return value
    route = [
        (s * count + i, (s - back) % segments * count + (i ^ mask))
        for s in range(segments)
        for i in range(count)
    ]
    return lax.ppermute(value, ("segment", "slab"), route)


def block(value, place, rows, dtype):
    return lax.dynamic_slice_in_dim(value, place * rows, rows, 0).astype(dtype)


def write_shifts(plane, height, out_ref, first):
    cells, channels = plane.shape
    width = cells // height
    rows = plane.astype(F32).reshape(width, height, channels)
    at = lax.broadcasted_iota(jnp.int32, rows.shape, 1)
    zero = jnp.zeros((1, height, channels), F32)
    before = jnp.where(at == 0, 0.0, pltpu.roll(rows, 1, 1))
    after = jnp.where(at == height - 1, 0.0, pltpu.roll(rows, height - 1, 1))
    for dy, moved in enumerate((before, rows, after)):
        for dx in range(3):
            if dx == 0:
                value = jnp.concatenate([zero, moved[:-1]], axis=0)
            elif dx == 1:
                value = moved
            else:
                value = jnp.concatenate([moved[1:], zero], axis=0)
            j = dx * 3 + dy
            out_ref[first : first + cells, j * channels : (j + 1) * channels] = value.reshape(
                cells, channels
            ).astype(BF16)


def back_product(shifts, mirror, block, depth):
    span = shifts.shape[1]
    total = None
    for dz in range(3):
        term = jnp.dot(
            shifts[dz * block : (dz + depth) * block, :],
            mirror[dz * span : (dz + 1) * span, :],
            preferred_element_type=F32,
        )
        total = term if total is None else total + term
    return total


def rim_kernel(acts, grad, near, far, sems):
    micro, depth = acts.shape[:2]
    top = 1 - lax.rem(lax.axis_index("slab"), 2)
    copies = []
    for which, (out, high) in enumerate(((near, top), (far, 1 - top))):
        for m in range(micro):
            for part, (source, size, at) in enumerate(((acts, 2, 0), (grad, 1, 2))):
                copies.append(
                    pltpu.make_async_copy(
                        source.at[m, pl.ds(high * (depth - size), size)],
                        out.at[m, at : at + size],
                        sems.at[which, m, part],
                    )
                )
    for copy in copies:
        copy.start()
    for copy in copies:
        copy.wait()


def own_kernel(
    height, stored_acts, stored_grad, stored, acts, grad, weight, mirror, part, own, sems
):
    micro, depth, cells, channels = acts.shape
    block, span = micro * cells, 9 * channels
    pairs = ((stored, weight), (stored_acts, acts), (stored_grad, grad))
    copies = [pltpu.make_async_copy(a, b, sems.at[n]) for n, (a, b) in enumerate(pairs)]
    for copy in copies:
        copy.start()
    copies[1].wait()
    for n in range(depth):
        for m in range(micro):
            write_shifts(acts[m, n], height, own, n * block + m * cells)
    copies[0].wait()
    copies[2].wait()
    part[...] = jnp.zeros(part.shape, F32)
    for dz in range(3):
        rows = slice((2 - dz) * block, (2 - dz + depth) * block)
        part[rows, :] += jnp.dot(
            own[...], weight[dz * span : (dz + 1) * span, :], preferred_element_type=F32
        )
    for k in range(27):
        mirror[(26 - k) * channels : (27 - k) * channels, :] = weight[
            k * channels : (k + 1) * channels, :
        ].T


def first_kernel(
    height, near, far, grad, weight, mirror, part, result, slopes, to_far, *refs
):
    rim, shifts = refs[-2:]
    micro, depth, cells, channels = grad.shape
    even = lax.rem(lax.axis_index("slab"), 2) == 0
    block, span = micro * cells, 9 * channels

    def pick(m, n, below):
        a, b = near[m, n].astype(F32), far[m, n].astype(F32)
        return jnp.where(even, b, a) if below else jnp.where(even, a, b)

    for n in range(4):
        for m in range(micro):
            write_shifts(pick(m, n % 2, n < 2), height, rim, n * block + m * cells)
    terms = [
        jnp.dot(
            rim[dz * block : (dz + 2) * block, :],
            weight[dz * span : (dz + 1) * span, :],
            preferred_element_type=F32,
        )
        for dz in range(3)
    ]
    head, tail = [term[:block] for term in terms], [term[block:] for term in terms]
    extra = {0: [head[0], head[1]], 1: [tail[0]]}
    extra.setdefault(depth, []).append(head[2])
    extra.setdefault(depth + 1, []).extend([tail[1], tail[2]])
    for n in range(depth + 2):
        rows = slice(n * block, (n + 1) * block)
        preact = part[rows, :]
        for term in extra.get(n, []):
            preact = preact + term
        sig = 1.0 / (1.0 + jnp.exp(-preact))
        slope = sig * (1.0 + preact * (1.0 - sig))
        slopes[rows, :] = slope
        for m in range(micro):
            if n == 0 or n == depth + 1:
                up = pick(m, 2, n == 0)
            else:
                up = grad[m, n - 1].astype(F32)
            delta = (up * slope[m * cells : (m + 1) * cells]).astype(BF16)
            write_shifts(delta, height, shifts, n * block + m * cells)
    back = back_product(shifts, mirror, block, depth)
    for m in range(micro):
        ends = []
        for n in range(depth):
            first = n * block + m * cells
            total = grad[m, n].astype(F32) + back[first : first + cells]
            result[m, n] = total.astype(BF16)
            if n in (0, depth - 1):
                ends.append(total)
        low, high = ends[0], ends[-1]
        for to_near in refs[:-2]:
            to_near[m, 0] = jnp.where(even, high, low).astype(BF16)
        to_far[m, 0] = jnp.where(even, low, high).astype(BF16)


def shift_kernel(height, acts, near, far, after, shifts):
    micro, depth, cells, _ = acts.shape
    even = lax.rem(lax.axis_index("slab"), 2) == 0
    for m in range(micro):
        below = jnp.where(even, far[m, 1].astype(F32), near[m, 1].astype(F32))
        above = jnp.where(even, near[m, 0].astype(F32), far[m, 0].astype(F32))
        planes = [below] + [acts[m, n] for n in range(depth)] + [above]
        for n, plane in enumerate(planes):
            write_shifts(plane, height, shifts, (n * micro + m) * cells)


def raw_kernel(
    spot, incoming, grad, far, slopes, shifts, upstream, deltas, far_slope, *refs
):
    sends, (keep, raw) = refs[:4], refs[4:]
    part = keep.shape[1]
    micro, depth, cells, channels = upstream.shape
    block, span = micro * cells, 9 * channels
    last = lax.axis_index("segment") == lax.axis_size("segment") - 1
    even = lax.rem(lax.axis_index("slab"), 2) == 0
    low, high = slice(0, block), slice((depth + 1) * block, (depth + 2) * block)
    slope = jnp.where(even, slopes[low, :], slopes[high, :])
    far_slope[...] = slope
    for m in range(micro):
        inside = slice(m * cells, (m + 1) * cells)
        rim = (far[m, 2].astype(F32) * slope[inside]).astype(BF16)
        for first in (low.start, high.start):
            deltas[first + m * cells : first + (m + 1) * cells, :] = rim
        planes = []
        for n in range(depth):
            up = jnp.where(last, grad[m, n].astype(F32), incoming[m, n].astype(F32))
            upstream[m, n] = up.astype(BF16)
            first = (n + 1) * block + m * cells
            delta = up * slopes[first : first + cells, :]
            deltas[first : first + cells, :] = delta.astype(BF16)
            planes.append(delta)
        first = part + m * cells
        sends[0][first : first + cells, :] = jnp.where(even, planes[-1], planes[0]).astype(BF16)
    for dz in range(3):
        total = None
        for n in range(depth):
            term = lax.dot_general(
                shifts[(dz + n) * block : (dz + n + 1) * block, :],
                deltas[(n + 1) * block : (n + 2) * block, :],
                (((0,), (0,)), ((), ())),
                preferred_element_type=F32,
            )
            total = term if total is None else total + term
        raw[dz * span : (dz + 1) * span, :] = total
    for turn in range(4):
        keep[turn] = raw[pl.ds((spot[0] ^ turn) * part, part), :]
        sends[turn][:part, :] = raw[pl.ds((spot[0] ^ turn ^ 4) * part, part), :].astype(BF16)


def add_kernel(turn, keep, got, out):
    out[...] = (keep[turn] + got[...].astype(F32)).astype(BF16)


def sum_kernel(keep, *refs):
    total = keep[0]
    for got in refs[:-1]:
        total = total + got[: total.shape[0], :].astype(F32)
    refs[-1][...] = total.astype(refs[-1].dtype)


def both_kernel(mine, other, out):
    out[...] = (mine[...].astype(F32) + other[...].astype(F32)).astype(BF16)


def column_squares(value):
    value = value.astype(F32)
    return jnp.sum(value * value, axis=0, keepdims=True)


def norm_kernel(*refs):
    sums = [column_squares(piece[...]) for piece in refs[:-1]]
    while len(sums) > 1:
        sums = [a + b for a, b in zip(sums[::2], sums[1::2], strict=True)]
    refs[-1][...] = jnp.broadcast_to(sums[0], refs[-1].shape)


def back_kernel(
    height, deltas, by_near, in_far, far_slope, upstream, mirror, out, shifts
):
    micro, depth, cells, channels = upstream.shape
    block = micro * cells
    last = lax.axis_index("segment") == lax.axis_size("segment") - 1
    even = lax.rem(lax.axis_index("slab"), 2) == 0
    start = by_near.shape[0] - block
    for m in range(micro):
        inside = slice(m * cells, (m + 1) * cells)
        near = by_near[start + m * cells : start + (m + 1) * cells, :].astype(F32)
        far = (in_far[m, 0].astype(F32) * far_slope[inside, :]).astype(BF16).astype(F32)
        far = jnp.where(last, deltas[inside, :].astype(F32), far)
        write_shifts(jnp.where(even, far, near), height, shifts, m * cells)
        first = (depth + 1) * block + m * cells
        write_shifts(jnp.where(even, near, far), height, shifts, first)
        for n in range(1, depth + 1):
            first = n * block + m * cells
            write_shifts(deltas[first : first + cells, :], height, shifts, first)
    back = back_product(shifts, mirror, block, depth)
    for m in range(micro):
        for n in range(depth):
            first = n * block + m * cells
            total = upstream[m, n].astype(F32) + back[first : first + cells]
            out[m, n] = total.astype(BF16)


def place_kernel(bound, count, spot, *refs):
    sums, pieces, (out, scaled, sems) = refs[: 2 * count], refs[2 * count : -3], refs[-3:]
    mine, other = (sum(value[:1, :] for value in sums[side::2]) for side in range(2))
    squares = mine + other
    norm = jnp.sqrt(jnp.sum(squares, axis=1, keepdims=True))
    factor = jnp.minimum(1.0, bound / (norm + 1e-06))
    copies = []
    for n, piece in enumerate(pieces):
        scaled[n] = piece[...].astype(F32) * factor
        copies.append(pltpu.make_async_copy(scaled.at[n], out.at[spot[0] ^ n], sems.at[n]))
        copies[-1].start()
    for copy in copies:
        copy.wait()


def shards(activations, weights, out_grad):
    weight = weights[0]
    channels = weight.shape[1]
    micro, depth, width, height = activations.shape[1:5]
    cells = width * height
    acts = activations[0].reshape(micro, depth, cells, channels)
    grad = out_grad.reshape(micro, depth, cells, channels)
    rows = depth * cells
    segments = lax.axis_size("segment")
    count = lax.axis_size("slab")
    index = lax.axis_index("slab")
    last = lax.axis_index("segment") == segments - 1
    large = pltpu.CompilerParams(vmem_limit_bytes=16 << 20)
    small = pltpu.CompilerParams(vmem_limit_bytes=4 << 20)

    shape = jax.ShapeDtypeStruct
    rim = shape((micro, 3, cells, channels), BF16)
    volume = shape((micro, depth, cells, channels), BF16)
    acts, grad = (pltpu.with_memory_space_constraint(a, pltpu.HBM) for a in (acts, grad))
    to_near, to_far = pl.pallas_call(
        rim_kernel,
        out_shape=(rim, rim),
        in_specs=[HBM, HBM],
        out_specs=(VMEM,) * 2,
        scratch_shapes=[pltpu.SemaphoreType.DMA((2, micro, 2))],
        compiler_params=small,
    )(acts, grad)
    near, far = swap(to_near, to_far)

    plane, span = micro * cells, 9 * channels
    whole = shape(weight.shape, BF16)
    outer = shape(((depth + 2) * plane, channels), F32)
    stored = acts, grad, pltpu.with_memory_space_constraint(weight, pltpu.HBM)
    acts, grad, weight, mirror, part = pl.pallas_call(
        functools.partial(own_kernel, height),
        out_shape=(volume, volume, whole, whole, outer),
        in_specs=[HBM] * 3,
        out_specs=(VMEM,) * 5,
        scratch_shapes=[
            pltpu.VMEM((depth * plane, span), BF16),
            pltpu.SemaphoreType.DMA((3,)),
        ],
        compiler_params=large,
    )(*stored)

    edge = shape((micro, 1, cells, channels), BF16)
    wide = pltpu.VMEM(((depth + 2) * plane, span), BF16)
    edges = (edge,) * (1 if segments == 2 else 2)
    result, slopes, to_far, *to_near = pl.pallas_call(
        functools.partial(first_kernel, height),
        out_shape=(volume, outer) + edges,
        in_specs=[VMEM] * 6,
        out_specs=(VMEM,) * (2 + len(edges)),
        scratch_shapes=[pltpu.VMEM((4 * plane, span), BF16), wide],
        compiler_params=large,
    )(near, far, grad, weight, mirror, part)

    def conv_back(deltas, by_near, in_far, far_slope, upstream):
        return pl.pallas_call(
            functools.partial(back_kernel, height),
            out_shape=volume,
            in_specs=[VMEM] * 6,
            out_specs=VMEM,
            scratch_shapes=[wide],
            compiler_params=large,
        )(deltas, by_near, in_far, far_slope, upstream, mirror)

    part = weight.shape[0] // 8
    even = lax.rem(index, 2) == 0
    for step in range(1, segments - 1):
        incoming, in_near, in_far = cross(result, 1, 0), cross(to_near[0], 1, 1), cross_far(to_far)
        upstream = jnp.where(last, grad, incoming)
        stacked = jnp.swapaxes(upstream, 0, 1).reshape(depth * plane, channels).astype(F32)
        deltas = (stacked * slopes[plane:-plane]).astype(BF16)
        near_slope = jnp.where(even, slopes[-plane:], slopes[:plane])
        far_slope = jnp.where(even, slopes[:plane], slopes[-plane:])
        by_near = jnp.where(last, near[:, 2:], in_near).reshape(plane, channels).astype(F32)
        rim = (far[:, 2:].reshape(plane, channels).astype(F32) * far_slope).astype(BF16)
        deltas = jnp.concatenate([rim, deltas, rim], axis=0)
        result = conv_back(
            deltas, (by_near * near_slope).astype(BF16), in_far, far_slope, upstream
        )
        low, high = result[:, :1], result[:, -1:]
        to_near, to_far = [jnp.where(even, high, low)], jnp.where(even, low, high)
    incoming = cross(result, 1, 0)
    shifts = pl.pallas_call(
        functools.partial(shift_kernel, height),
        out_shape=shape(((depth + 2) * plane, span), BF16),
        in_specs=[VMEM] * 4,
        out_specs=VMEM,
        compiler_params=large,
    )(acts, near, far, result)
    bits = [1 << n for n in range(1, count.bit_length() - 1)]
    inner = [bits[n : n + 2] for n in range(2, len(bits), 2)]
    crossing = inner[-1][0] if len(inner[-1]) == 1 else 0
    side = lax.rem(index, 2)
    quarter = jnp.where(index & 2, 2, 0) + jnp.where(index & 4, 1, 0)
    masks = {1: 4, 2: 2, 3: 6}
    spot = (side * 4 + quarter).astype(jnp.int32).reshape(1)
    piece = shape((part, channels), BF16)

    upstream, deltas, far_slope, *rest = pl.pallas_call(
        raw_kernel,
        out_shape=(
            volume,
            shape(outer.shape, BF16),
            shape((plane, channels), F32),
            shape((part + plane, channels), BF16),
            piece,
            piece,
            piece,
            shape((4, part, channels), F32),
        ),
        in_specs=[SMEM] + [VMEM] * 5,
        out_specs=(VMEM,) * 8,
        scratch_shapes=[pltpu.VMEM((8 * part, channels), F32)],
        compiler_params=large,
    )(spot, incoming, grad, far, slopes, shifts)
    sends, keep = rest[:4], rest[4]
    order = (1, 2, 3)
    got = {turn: exchange(sends[turn], 1) for turn in order + (0,)}
    across = []
    for turn in order:
        added = pl.pallas_call(
            functools.partial(add_kernel, turn),
            out_shape=piece,
            in_specs=[VMEM] * 2,
            out_specs=VMEM,
            compiler_params=small,
        )(keep, got[turn])
        across.append(exchange(added, masks[turn]))
    in_far = cross_far(to_far)
    across[2], in_far = lax.optimization_barrier((across[2], in_far))
    gradients = conv_back(deltas, got[0], in_far, far_slope, upstream)
    single = len(inner[-1]) == 1
    direct = single and len(inner) == 1
    chunk = pl.pallas_call(
        sum_kernel,
        out_shape=shape((part, channels), BF16 if direct else F32),
        in_specs=[VMEM] * 5,
        out_specs=VMEM,
        compiler_params=small,
    )(keep, got[0], *across)

    def places(group):
        own = sum(jnp.where(index & bit, 1 << n, 0) for n, bit in enumerate(group))
        others = []
        for turn in range(1, 1 << len(group)):
            others.append((sum(bit for n, bit in enumerate(group) if turn >> n & 1), own ^ turn))
        return own, others

    paired = inner[:-1] if single else inner
    for group in paired:
        own, others = places(group)
        size = chunk.shape[0] >> len(group)
        took = [exchange(block(chunk, there, size, BF16), mask) for mask, there in others]
        chunk = block(chunk, own, size, F32) + sum(g.astype(F32) for g in took)
    gathered = chunk.astype(BF16)
    if single:
        other = exchange(gathered, crossing)
        other, gradients = lax.optimization_barrier((other, gradients))
        gathered = pl.pallas_call(
            both_kernel,
            out_shape=shape(gathered.shape, BF16),
            in_specs=[VMEM] * 2,
            out_specs=VMEM,
            compiler_params=small,
        )(gathered, other)

    for group in reversed(paired):
        own, others = places(group)
        took = [(there, exchange(gathered, mask)) for mask, there in others]
        blocks = []
        for n in range(1 << len(group)):
            value = jnp.where(own == n, gathered, took[0][1])
            for there, other in took[1:]:
                value = jnp.where(there == n, other, value)
            blocks.append(value)
        gathered = jnp.concatenate(blocks, axis=0)
    pieces = {turn: exchange(gathered, masks[turn]) for turn in (1, 2, 3)}
    ours = [gathered] + [pieces[turn] for turn in (1, 2, 3)]
    theirs = [exchange(piece, 1) for piece in ours]
    sums = [
        pl.pallas_call(
            norm_kernel,
            out_shape=shape((8, channels), F32),
            in_specs=[VMEM] * 4,
            out_specs=VMEM,
            compiler_params=small,
        )(*four)
        for four in (ours, theirs)
    ]
    sums += [cross(sums[0], back, mask) for back in range(1, segments) for mask in (0, 1)]
    bound = math.sqrt(27.0 * channels * channels * segments)
    update = pl.pallas_call(
        functools.partial(place_kernel, bound, segments),
        out_shape=jax.ShapeDtypeStruct((8, part, channels), F32),
        in_specs=[SMEM] + [VMEM] * (2 * segments + 8),
        out_specs=ANY,
        scratch_shapes=[pltpu.VMEM((8, part, channels), F32), pltpu.SemaphoreType.DMA((8,))],
        compiler_params=large,
    )((side * 4 + quarter).astype(jnp.int32).reshape(1), *sums, *ours, *theirs)
    gradients = gradients.reshape(1, micro, depth, width, height, channels)
    return (update.reshape(1, 8 * part, channels), gradients)


def solution(mesh):
    return jax.shard_map(
        shards,
        mesh=mesh,
        in_specs=(
            P("segment", None, "slab", None, None, None),
            P("segment", None, None),
            P(None, "slab", None, None, None),
        ),
        out_specs=(P("segment", None, None), P("segment", None, "slab", None, None, None)),
        check_vma=False,
    )
```
